128 devices in a mesh: layer: 4 (over x), node: 32 (over y, z, core).
Axes of the slice: x: 4, y: 4, z: 4, core: 2. Of those that a mesh axis runs over, the one named last changes fastest.
Arguments:
- features: bfloat16 [4, 8192, 512], P(None, 'node'), may hold values from -6 to 6
- w_self: bfloat16 [4, 512, 512], P('layer'), may hold values from -0.1875 to 0.1875
- w_neigh: bfloat16 [4, 512, 512], P('layer'), may hold values from -0.1875 to 0.1875
- w_out: bfloat16 [512, 172], replicated, may hold values from -0.25 to 0.25
- labels: int32 [4, 8192], P(None, 'node'), may hold values from 0 to 171
- train_mask: int32 [4, 8192], P(None, 'node'), may hold values 0 or 1
- tile_cols: int32 [4, 32, 2, 4], P(None, 'node'), may hold values from 0 to 3
- tile_vals: bfloat16 [4, 32, 2, 4, 128, 128], P(None, 'node'), may hold values from -0.25 to 0.25
- send_rows: int32 [4, 32, 32, 8], P(None, 'node'), may hold values from 0 to 255
- send_counts: int32 [4, 32, 32], P(None, 'node'), may hold values from 0 to 8, as said below
Outputs:
- layer_acts: bfloat16 [4, 4, 8192, 512], P('layer', None, 'node')
- act_grads: bfloat16 [4, 4, 8192, 512], P('layer', None, 'node')
- grad_self: float32 [4, 512, 512], P('layer')
- grad_neigh: float32 [4, 512, 512], P('layer')
The draws below stay inside these ranges and needn't reach their ends.
Inputs may be any that keep to these rules, and one draw needn't show every extreme that they name: `send_counts`: in every span one partition, drawn per span, gets 8 rows from every partition, itself included; the other counts are at most 4. `send_rows`: entries of slots at or past the count are ignored; rows may repeat. `tile_cols`: A value below 2 is a tile of the partition's own rows; larger values are tiles of the received rows in source order, 8 slots per source, then zero rows; tiles of a row tile may repeat.
All inputs are finite; a program needn't handle non-finite values. No bound on the sum of `train_mask` on one device may be relied on, other than what follows from the above.
Results may differ from the reference program's by a relative error of at most 0.03.
Values may be sent and summed in bfloat16 or wider, within the bound.
No kernel may reach another device: no remote copies, remote signals or barrier semaphores. Data moves between devices by JAX's collectives and lax.ppermute only.
A program may use at most 128 MiB of HBM per device.

```python
import jax
import jax.numpy as jnp

D = 512
C = 172
NR = 256
M = 4
TILE = 128
DEG = 4
CAP = 8
NODES = 8192
WIN_NODES = 32768
N_LAYER = 4
N_NODE = 32


def draw_send_counts(key, part):
    key_counts, key_target = jax.random.split(jax.random.fold_in(key, 17))
    base_counts = jax.random.randint(key_counts, (M, N_NODE, N_NODE), CAP // 8, CAP // 2 + 1)
    busy_target = jax.random.randint(key_target, (M,), 0, N_NODE)
    is_busy = jnp.arange(N_NODE)[None, None, :] == busy_target[:, None, None]
    return jnp.where(is_busy, CAP, base_counts).astype(jnp.int32)


def set_ends(entries, own_key, low, high):
    index_at = [jax.random.randint(jax.random.fold_in(own_key, axis), (), 0, length) for axis, length in enumerate(entries.shape)]
    longest = entries.shape.index(max(entries.shape))
    neighbour = index_at[:longest] + [(index_at[longest] + 1) % entries.shape[longest]] + index_at[longest + 1:]
    return entries.at[tuple(index_at)].set(low).at[tuple(neighbour)].set(high)


def block_levels(key, shape, cuts, low, top_value):
    def one(axis_at, blocks):
        draws = jax.random.uniform(jax.random.fold_in(jax.random.fold_in(key, 6), axis_at), (blocks,), jnp.float32, low / len(cuts), top_value / len(cuts))
        return jnp.repeat(jnp.exp(draws), shape[axis_at] // blocks).reshape((-1,) + (1,) * (len(shape) - axis_at - 1))

    loudness = one(*cuts[0])
    for cut in cuts[1:]:
        loudness = loudness * one(*cut)
    return loudness


def noise(stream_key, dims, scale, most, cuts=(), kind=jnp.bfloat16):
    array = scale * jax.random.normal(stream_key, dims, jnp.float32)
    if cuts:
        array = array * block_levels(stream_key, dims, cuts, -0.22, 0.18)
    return jnp.clip(array, -most, most).astype(kind)


def setup_inputs(seed: int = 0) -> dict:
    keys = jax.random.split(jax.random.key(seed), 11)
    return {
        "features": noise(keys[0], (M, NODES, D), 1.0, 6.0, ((1, 32),)),
        "w_self": noise(keys[1], (N_LAYER, D, D), (2 * D) ** -0.5, 0.1875, ((0, 4),)),
        "w_neigh": noise(keys[2], (N_LAYER, D, D), (2 * D) ** -0.5, 0.1875, ((0, 4),)),
        "w_out": noise(keys[3], (D, C), D ** -0.5, 0.25),
        "labels": set_ends(jax.random.randint(keys[4], (M, NODES), 0, C), jax.random.fold_in(keys[4], 1), 0, C - 1).astype(jnp.int32),
        "train_mask": set_ends((jax.random.randint(keys[5], (M, NODES), 0, 2) < 1).astype(jnp.int32), jax.random.fold_in(keys[5], 1), 0, 1),
        "tile_cols": set_ends(jax.random.randint(keys[6], (M, N_NODE, NR // TILE, DEG), 0, (NR + N_NODE * CAP + TILE - 1) // TILE), jax.random.fold_in(keys[6], 1), 0, ((NR + N_NODE * CAP + TILE - 1) // TILE) - 1).astype(jnp.int32),
        "tile_vals": noise(keys[7], (M, N_NODE, NR // TILE, DEG, TILE, TILE), (TILE * DEG) ** -0.5, 0.25, ((1, 32),)),
        "send_rows": set_ends(jax.random.randint(keys[8], (M, N_NODE, N_NODE, CAP), 0, NR), jax.random.fold_in(keys[8], 1), 0, NR - 1).astype(jnp.int32),
        "send_counts": draw_send_counts(jax.random.fold_in(keys[10], 71), 0),
    }


def silu_slope(preact):
    sigma = jax.nn.sigmoid(preact)
    return sigma * (1.0 + preact * (1.0 - sigma))


def extend_rows(hidden_in, arrived):
    extended = jnp.concatenate([hidden_in, arrived], axis=0)
    ext_len = extended.shape[0]
    padded_len = (ext_len + TILE - 1) // TILE * TILE
    return jnp.pad(extended, ((0, padded_len - ext_len), (0, 0)))


def aggregate_part(extended, col_tiles, values):
    blocks = jnp.take(extended.reshape(-1, TILE, D), col_tiles, axis=0)
    summed = jnp.einsum("rkij,rkjd->rid", values.astype(jnp.float32), blocks.astype(jnp.float32))
    return summed.reshape(NR, D).astype(jnp.bfloat16)


def spread_part(d_agg, col_tiles, values):
    ext_rows = (NR + N_NODE * CAP + TILE - 1) // TILE * TILE
    pieces = jnp.einsum("rkij,rid->rkjd", values.astype(jnp.float32), d_agg.reshape(-1, TILE, D).astype(jnp.float32))
    d_ext = jax.ops.segment_sum(pieces.reshape(-1, TILE, D), col_tiles.reshape(-1), num_segments=ext_rows // TILE)
    return d_ext.reshape(ext_rows, D)


def take_rows(hidden, rows):
    return jnp.take(hidden, rows, axis=0)


def scatter_rows(masked, rows):
    return jax.ops.segment_sum(masked.reshape(-1, D), rows.reshape(-1), num_segments=NR)


def reference(features, w_self, w_neigh, w_out, labels, train_mask, tile_cols, tile_vals, send_rows, send_counts):
    acts_all = [[None] * M for layer_idx in range(N_LAYER)]
    grads_all = [[None] * M for layer_idx in range(N_LAYER)]
    g_self = [jnp.zeros((D, D), jnp.float32) for layer_idx in range(N_LAYER)]
    g_neigh = [jnp.zeros((D, D), jnp.float32) for layer_idx in range(N_LAYER)]
    for span_idx in range(M):
        col_tiles = tile_cols[span_idx]
        values = tile_vals[span_idx]
        rows = send_rows[span_idx]
        is_live = jnp.arange(CAP)[None, None, :] < send_counts[span_idx][:, :, None]
        hidden = features[span_idx].reshape(N_NODE, NR, D)
        saved = []
        for layer_idx in range(N_LAYER):
            sent = jax.vmap(take_rows)(hidden, rows)
            sent = jnp.where(is_live[..., None], sent, jnp.zeros((), jnp.bfloat16))
            arrived = jnp.swapaxes(sent, 0, 1).reshape(N_NODE, N_NODE * CAP, D)
            extended = jax.vmap(extend_rows)(hidden, arrived)
            aggregate = jax.vmap(aggregate_part)(extended, col_tiles, values)
            preact = jnp.einsum("pnd,de->pne", hidden.astype(jnp.float32), w_self[layer_idx].astype(jnp.float32))
            preact = preact + jnp.einsum("pnd,de->pne", aggregate.astype(jnp.float32), w_neigh[layer_idx].astype(jnp.float32))
            output = jax.nn.silu(preact).astype(jnp.bfloat16)
            saved.append((hidden, aggregate, preact))
            acts_all[layer_idx][span_idx] = output.reshape(NODES, D)
            hidden = output
        logits = jnp.einsum("pnd,dc->pnc", hidden.astype(jnp.float32), w_out.astype(jnp.float32))
        expo = jnp.exp(logits)
        probs = expo / jnp.sum(expo, axis=-1, keepdims=True)
        label_rows = labels[span_idx].reshape(N_NODE, NR)
        onehot = (label_rows[..., None] == jnp.arange(C)[None, None, :]).astype(jnp.float32)
        mask_rows = train_mask[span_idx].reshape(N_NODE, NR, 1).astype(jnp.float32)
        g_logits = (mask_rows * (probs - onehot)).astype(jnp.bfloat16)
        d_out = jnp.einsum("pnc,dc->pnd", g_logits.astype(jnp.float32), w_out.astype(jnp.float32)).astype(jnp.bfloat16)
        for layer_idx in range(N_LAYER - 1, -1, -1):
            hidden_in, aggregate, preact = saved[layer_idx]
            d_pre = (d_out.astype(jnp.float32) * silu_slope(preact)).astype(jnp.bfloat16)
            g_self[layer_idx] = g_self[layer_idx] + jnp.einsum("pnd,pne->de", hidden_in.astype(jnp.float32), d_pre.astype(jnp.float32))
            g_neigh[layer_idx] = g_neigh[layer_idx] + jnp.einsum("pnd,pne->de", aggregate.astype(jnp.float32), d_pre.astype(jnp.float32))
            back_self = jnp.einsum("pne,de->pnd", d_pre.astype(jnp.float32), w_self[layer_idx].astype(jnp.float32))
            d_agg = jnp.einsum("pne,de->pnd", d_pre.astype(jnp.float32), w_neigh[layer_idx].astype(jnp.float32)).astype(jnp.bfloat16)
            d_ext = jax.vmap(spread_part)(d_agg, col_tiles, values)
            local_part = d_ext[:, :NR]
            d_sent = d_ext[:, NR:NR + N_NODE * CAP].reshape(N_NODE, N_NODE, CAP, D).astype(jnp.bfloat16)
            returned = jnp.swapaxes(d_sent, 0, 1)
            masked = jnp.where(is_live[..., None], returned.astype(jnp.float32), jnp.zeros((), jnp.float32))
            scattered = jax.vmap(scatter_rows)(masked, rows)
            d_in = (back_self + local_part + scattered).astype(jnp.bfloat16)
            grads_all[layer_idx][span_idx] = d_in.reshape(NODES, D)
            d_out = d_in
    layer_acts = jnp.stack([jnp.stack(acts_all[layer_idx]) for layer_idx in range(N_LAYER)])
    act_grads = jnp.stack([jnp.stack(grads_all[layer_idx]) for layer_idx in range(N_LAYER)])
    grad_self = jnp.stack(g_self) / WIN_NODES
    grad_neigh = jnp.stack(g_neigh) / WIN_NODES
    return (layer_acts, act_grads, grad_self, grad_neigh)
```

```python
import functools

import jax
import jax.numpy as jnp
from jax import lax
from jax.experimental import pallas as pl
from jax.experimental.pallas import tpu as pltpu
from jax.sharding import PartitionSpec as P

BF = jnp.bfloat16
F32 = jnp.float32
NN = (((1,), (0,)), ((), ()))
NT = (((1,), (1,)), ((), ()))
TN = (((0,), (0,)), ((), ()))
ANY = pl.BlockSpec(memory_space=pl.ANY)
VMEM_BYTES = 40 * 1024 * 1024


def dot(a, b, dims=NN):
    return lax.dot_general(a, b, dims, preferred_element_type=F32)


def shift(value, axis, steps):
    count = lax.axis_size(axis)
    return lax.ppermute(value, axis, [(i, (i + steps) % count) for i in range(count)])


def sibling(value):
    count = lax.axis_size("node")
    return lax.ppermute(value, "node", [(i, i ^ 1) for i in range(count)])


def exchange(value):
    return lax.all_to_all(value, "node", split_axis=0, concat_axis=0, tiled=True)


def whole(shape):
    return pl.BlockSpec(shape, lambda i, ids, cols: (0,) * len(shape))


def of_span(shape):
    return pl.BlockSpec((None, *shape), lambda i, ids, cols: (ids[0], *((0,) * len(shape))))


def at_offset(shape, layer):
    return pl.BlockSpec(
        (None, *shape),
        lambda i, ids, cols: (lax.rem(layer - ids[0] + 4, 4), *((0,) * len(shape))),
    )


def sds(shape, dtype):
    return jax.ShapeDtypeStruct(shape, dtype)


def run(kernel, name, scalars, ins, outs, scratch=(), aliases=None, flops=0, moved=0):
    arrays = [a for a, _ in ins]
    return pl.pallas_call(
        kernel,
        name=name,
        grid_spec=pltpu.PrefetchScalarGridSpec(
            num_scalar_prefetch=2,
            grid=(1,),
            in_specs=[s for _, s in ins],
            out_specs=[s for _, s in outs],
            scratch_shapes=list(scratch),
        ),
        out_shape=[o for o, _ in outs],
        input_output_aliases={} if aliases is None else {k + 2: v for k, v in aliases.items()},
        compiler_params=pltpu.CompilerParams(vmem_limit_bytes=VMEM_BYTES),
        cost_estimate=pl.CostEstimate(flops=flops, bytes_accessed=moved, transcendentals=0),
    )(*scalars, *arrays)


def weight_copies(which, core, w_refs, w_scr, sems):
    own_s, own_n, left, left_x, right, right_x, far_a, far_b, far_ax, far_bx = w_refs
    half = w_scr.shape[1] // 2
    top, low = pl.ds(0, half), pl.ds(half, half)
    plans = {
        0: [(own_s, w_scr.at[0]), (own_n, w_scr.at[1])],
        1: [(right, w_scr.at[core]), (right_x, w_scr.at[1 - core])],
        2: [
            (far_a, w_scr.at[core, top]),
            (far_b, w_scr.at[core, low]),
            (far_ax, w_scr.at[1 - core, top]),
            (far_bx, w_scr.at[1 - core, low]),
        ],
        3: [(left, w_scr.at[core]), (left_x, w_scr.at[1 - core])],
    }
    return [pltpu.make_async_copy(s, d, sems.at[n]) for n, (s, d) in enumerate(plans[which])]


def each_weight(layer, ids, w_refs, w_scr, sems, act):
    which = lax.rem(layer - ids[0] + 4, 4)
    for option in range(4):

        @pl.when(which == option)
        def _():
            for copy in weight_copies(option, ids[1], w_refs, w_scr, sems):
                act(copy)


def start_weights(layer, ids, w_refs, w_scr, sems):
    each_weight(layer, ids, w_refs, w_scr, sems, lambda copy: copy.start())


def wait_weights(layer, ids, w_refs, w_scr, sems):
    each_weight(layer, ids, w_refs, w_scr, sems, lambda copy: copy.wait())


def side_by_side(vals_ref, r, degree):
    return jnp.concatenate([vals_ref[r, j] for j in range(degree)], axis=1)


def aggregate_rows(ids, cols, vals_ref, ext):
    tiles, degree, size = vals_ref.shape[0], vals_ref.shape[1], vals_ref.shape[2]
    parts = []
    for r in range(tiles):
        base = ids[0] * (tiles * degree) + r * degree
        picked = jnp.concatenate(
            [ext[pl.ds(pl.multiple_of(cols[base + j] * size, size), size), :] for j in range(degree)],
            axis=0,
        )
        parts.append(dot(side_by_side(vals_ref, r, degree), picked))
    return jnp.concatenate(parts, axis=0).astype(BF)


def spread_rows(ids, cols, vals_ref, d_agg, d_ext):
    tiles, degree, size = vals_ref.shape[0], vals_ref.shape[1], vals_ref.shape[2]
    d_ext[...] = jnp.zeros_like(d_ext)
    for r in range(tiles):
        base = ids[0] * (tiles * degree) + r * degree
        pieces = dot(side_by_side(vals_ref, r, degree), d_agg[r * size : (r + 1) * size], TN)
        for j in range(degree):
            rows = pl.ds(pl.multiple_of(cols[base + j] * size, size), size)
            d_ext[rows, :] += pieces[j * size : (j + 1) * size]


def sigmoid(v):
    return 1.0 / (1.0 + jnp.exp(-v))


def pre_kernel(ids, cols, h_ref, rows_ref, counts_ref, pick_ref, out_ref):
    peers, slots = rows_ref.shape
    total, node_rows = pick_ref.shape
    bits = slots.bit_length() - 1
    slot = lax.broadcasted_iota(jnp.int32, (total, peers), 0)
    owner = lax.broadcasted_iota(jnp.int32, (total, peers), 1)
    mine = lax.shift_right_logical(slot, bits) == owner
    wide = dot(mine.astype(F32).astype(BF), rows_ref[...].astype(F32).astype(BF))
    slot_k = lax.broadcasted_iota(jnp.int32, (total, slots), 0) & (slots - 1)
    in_slot = slot_k == lax.broadcasted_iota(jnp.int32, (total, slots), 1)
    row = jnp.sum(jnp.where(in_slot, wide, 0.0), axis=1, keepdims=True)
    counts = jnp.broadcast_to(counts_ref[...].astype(F32), (total, peers))
    count = jnp.sum(jnp.where(mine, counts, 0.0), axis=1, keepdims=True)
    k = (lax.broadcasted_iota(jnp.int32, (total, 1), 0) & (slots - 1)).astype(F32)
    row = jnp.where(k < count, row, -1.0)
    place = lax.broadcasted_iota(jnp.int32, (total, node_rows), 1).astype(F32)
    pick = (place == row).astype(F32).astype(BF)
    pick_ref[...] = pick
    out_ref[...] = dot(pick, h_ref[...]).astype(BF)


def forward_math(layer, ids, cols, h_ref, arr_ref, vals_ref, w_refs, ext, w_scr, sems):
    start_weights(layer, ids, w_refs, w_scr, sems)
    rows = h_ref.shape[0]
    ext[0:rows, :] = h_ref[...]
    ext[rows : 2 * rows, :] = arr_ref[...]
    agg = aggregate_rows(ids, cols, vals_ref, ext)
    wait_weights(layer, ids, w_refs, w_scr, sems)
    pre = dot(h_ref[...], w_scr[0]) + dot(agg, w_scr[1])
    sig = sigmoid(pre)
    return agg, pre, sig, (pre * sig).astype(BF)


def forward_kernel(layer, first, ids, cols, h_ref, arr_ref, vals_ref, pick_ref, *rest):
    w_refs, rest = rest[:10], rest[10:]
    if not first:
        rest = rest[1:]
    agg_ref, pre_ref, hid_ref, out_ref, buf_ref, ext, w_scr, sems = rest
    agg, pre, _, hid = forward_math(
        layer, ids, cols, h_ref, arr_ref, vals_ref, w_refs, ext, w_scr, sems
    )
    agg_ref[...] = agg
    pre_ref[...] = pre
    hid_ref[...] = hid
    buf_ref[...] = hid
    out_ref[...] = dot(pick_ref[...], hid).astype(BF)


def backward_math(ids, cols, d_pre, vals_ref, w_scr, d_ext):
    d_agg = dot(d_pre, w_scr[1], NT).astype(BF)
    spread_rows(ids, cols, vals_ref, d_agg, d_ext)
    return dot(d_pre, w_scr[0], NT)


def top_kernel(layer, ids, cols, h_ref, arr_ref, vals_ref, wout_ref, lab_ref, mask_ref, *rest):
    w_refs, rest = rest[:10], rest[11:]
    agg_ref, dpre_ref, remote_ref, part_ref, buf_ref, ext, w_scr, sems, d_ext = rest
    rows = h_ref.shape[0]
    agg, pre, sig, hid = forward_math(
        layer, ids, cols, h_ref, arr_ref, vals_ref, w_refs, ext, w_scr, sems
    )
    agg_ref[...] = agg
    buf_ref[...] = hid
    logits = dot(hid, wout_ref[...])
    expo = jnp.exp(logits)
    probs = expo / jnp.sum(expo, axis=1, keepdims=True)
    onehot = (lab_ref[...] == lax.broadcasted_iota(jnp.int32, logits.shape, 1)).astype(F32)
    g_logits = (mask_ref[...].astype(F32) * (probs - onehot)).astype(BF)
    d_out = dot(g_logits, wout_ref[...], NT).astype(BF)
    d_pre = (d_out.astype(F32) * (sig * (1.0 + pre * (1.0 - sig)))).astype(BF)
    dpre_ref[...] = d_pre
    back = backward_math(ids, cols, d_pre, vals_ref, w_scr, d_ext)
    part_ref[...] = back + d_ext[0:rows, :]
    remote_ref[...] = d_ext[rows : 2 * rows, :].astype(BF).reshape(remote_ref.shape)


def chunk_sum(block):
    total = block[0:2].astype(F32)
    for n in range(2, block.shape[0], 2):
        total = total + block[n : n + 2].astype(F32)
    return total


def backward_kernel(layer, carry, has_buf, ids, cols, ret_ref, part_in, pre_ref, vals_ref, pick_ref, *rest):
    w_refs, rest = rest[:10], rest[10:]
    if carry:
        keep_ref, recv_ref, rest = rest[0], rest[1], rest[2:]
    if has_buf:
        rest = rest[1:]
    got_chunk = ret_ref.shape[1] > 8
    dpre_ref, remote_ref, part_ref, buf_ref, rest = *rest[:4], rest[4:]
    if got_chunk:
        chunk_ref, rest = rest[0], rest[1:]
    w_scr, sems, d_ext = rest
    start_weights(layer, ids, w_refs, w_scr, sems)
    rows, feat = part_in.shape
    returned = ret_ref[:, 0:8, :].reshape(rows, feat)
    d_out = (part_in[...] + dot(pick_ref[...], returned, TN)).astype(BF)
    buf_ref[...] = d_out
    pre = pre_ref[...]
    sig = sigmoid(pre)
    d_pre = (d_out.astype(F32) * (sig * (1.0 + pre * (1.0 - sig)))).astype(BF)
    dpre_ref[...] = d_pre
    wait_weights(layer, ids, w_refs, w_scr, sems)
    back = backward_math(ids, cols, d_pre, vals_ref, w_scr, d_ext)
    part_ref[...] = back + d_ext[0:rows, :]
    remote = d_ext[rows : 2 * rows, :].astype(BF).reshape(ret_ref.shape[0], 8, feat)
    remote_ref[:, 0:8, :] = remote
    if carry:
        both = (keep_ref[...].astype(F32) + recv_ref[...].astype(F32)).astype(BF)
        remote_ref[:, 8:24, :] = both.reshape(ret_ref.shape[0], 16, feat)
    if got_chunk:
        chunk_ref[...] = chunk_sum(ret_ref[:, 8:24, :]).astype(BF)


def grad_kernel(ids, cols, h_ref, agg_ref, dpre_ref, keep_ref, send_ref):
    d_pre = dpre_ref[...]
    on_rows = dot(h_ref[...], d_pre, TN).astype(BF)
    on_agg = dot(agg_ref[...], d_pre, TN).astype(BF)

    @pl.when(ids[1] == 0)
    def _():
        keep_ref[...] = on_rows
        send_ref[...] = on_agg

    @pl.when(ids[1] != 0)
    def _():
        keep_ref[...] = on_agg
        send_ref[...] = on_rows


def join_kernel(ids, cols, remote_ref, keep_a, recv_a, keep_b, recv_b, out_ref):
    peers, feat = out_ref.shape[0], out_ref.shape[2]
    out_ref[:, 0:8, :] = remote_ref[:, 0:8, :]
    first = (keep_a[...].astype(F32) + recv_a[...].astype(F32)).astype(BF)
    out_ref[:, 8:24, :] = first.reshape(peers, 16, feat)
    second = (keep_b[...].astype(F32) + recv_b[...].astype(F32)).astype(BF)
    out_ref[:, 24:40, :] = second.reshape(peers, 16, feat)


def end_kernel(ids, cols, ret_ref, part_in, pick_ref, buf_in, c_3, c_2, buf_ref, chunks_ref):
    rows, feat = part_in.shape
    returned = ret_ref[:, 0:8, :].reshape(rows, feat)
    buf_ref[...] = (part_in[...] + dot(pick_ref[...], returned, TN)).astype(BF)
    home = ids[0]
    chunks_ref[lax.rem(7 - home, 4)] = c_3[...]
    chunks_ref[lax.rem(6 - home, 4)] = c_2[...]
    chunks_ref[lax.rem(5 - home, 4)] = chunk_sum(ret_ref[:, 8:24, :]).astype(BF)
    chunks_ref[lax.rem(4 - home, 4)] = chunk_sum(ret_ref[:, 24:40, :]).astype(BF)


def layer_sum_kernel(ids, cols, own_ref, a_ref, b_ref, c_ref, out_ref):
    total = own_ref[0].astype(F32) + a_ref[...].astype(F32)
    total = (total + b_ref[...].astype(F32) + c_ref[...].astype(F32)).astype(BF)
    for n in range(0, out_ref.shape[0], 2):
        out_ref[n : n + 2] = total


def scale_kernel(scale, ids, cols, mine_ref, other_ref, self_ref, neigh_ref):
    mine = mine_ref[...].astype(F32) * scale
    other = other_ref[...].astype(F32) * scale

    @pl.when(ids[1] == 0)
    def _():
        self_ref[0] = mine
        neigh_ref[0] = other

    @pl.when(ids[1] != 0)
    def _():
        self_ref[0] = other
        neigh_ref[0] = mine


def home_kernel(ids, cols, own_ref, a_ref, b_ref, c_ref, out_ref, sems):
    home = ids[0]
    copies = [
        pltpu.make_async_copy(own_ref.at[0], out_ref.at[0, home], sems.at[0]),
        pltpu.make_async_copy(a_ref, out_ref.at[0, lax.rem(home + 3, 4)], sems.at[1]),
        pltpu.make_async_copy(b_ref, out_ref.at[0, lax.rem(home + 2, 4)], sems.at[2]),
        pltpu.make_async_copy(c_ref, out_ref.at[0, lax.rem(home + 1, 4)], sems.at[3]),
    ]
    for copy in copies:
        copy.start()
    for copy in copies:
        copy.wait()


def body(
    features,
    w_self,
    w_neigh,
    w_out,
    labels,
    train_mask,
    tile_cols,
    tile_vals,
    send_rows,
    send_counts,
):
    home = lax.axis_index("layer")
    node = lax.axis_index("node")
    core = lax.rem(node, 2)
    spans, rows, feat = features.shape
    peers, slots = send_rows.shape[2], send_rows.shape[3]
    tiles, degree, size = tile_vals.shape[2], tile_vals.shape[3], tile_vals.shape[4]
    classes = w_out.shape[1]
    scale = 1.0 / (spans * rows * peers)
    scalars = (jnp.stack([home, core]).astype(jnp.int32), tile_cols.reshape(-1))
    act = sds((rows, feat), BF)
    square = sds((feat, feat), BF)
    stack = sds((spans, rows, feat), BF)
    wide = sds((rows, feat), F32)
    act_spec, square_spec = whole((rows, feat)), whole((feat, feat))

    mine = jnp.where(core == 0, w_self[0], w_neigh[0])
    left = shift(mine, "layer", 1)
    right = shift(mine, "layer", -1)
    half = feat // 2
    far_a = shift(left[:half], "layer", 1)
    far_b = shift(right[half:], "layer", -1)
    weights = [
        (w, ANY)
        for w in (
            w_self[0],
            w_neigh[0],
            left,
            sibling(left),
            right,
            sibling(right),
            far_a,
            far_b,
            sibling(far_a),
            sibling(far_b),
        )
    ]
    features_in = (features, of_span((rows, feat)))
    vals_in = (
        tile_vals.reshape(spans, tiles, degree, size, size),
        of_span((tiles, degree, size, size)),
    )
    w_scratch = [pltpu.VMEM((2, feat, feat), BF), pltpu.SemaphoreType.DMA((4,))]
    ext_scratch = pltpu.VMEM((2 * rows, feat), BF)
    d_ext_scratch = pltpu.VMEM((2 * rows, feat), F32)

    pick, outgoing = run(
        pre_kernel,
        "gather_rows",
        scalars,
        [
            features_in,
            (send_rows.reshape(spans, peers, slots), of_span((peers, slots))),
            (send_counts.reshape(spans, 1, peers), of_span((1, peers))),
        ],
        [
            (sds((peers * slots, rows), BF), whole((peers * slots, rows))),
            (sds((peers * slots, feat), BF), whole((peers * slots, feat))),
        ],
        flops=10**8,
        moved=10**6,
    )
    pick_in = (pick, whole(pick.shape))
    back_rows = lambda value: exchange(value.reshape(peers, slots, feat))

    hidden, aggs, pres = [features_in], [], []
    acts_buf = None
    for layer in range(spans - 1):
        arrived = back_rows(outgoing).reshape(rows, feat)
        ins = [hidden[layer], (arrived, act_spec), vals_in, pick_in, *weights]
        aliases = None
        if layer:
            ins.append((acts_buf, ANY))
            aliases = {len(ins) - 1: 4}
        agg, pre, hid, outgoing, acts_buf = run(
            functools.partial(forward_kernel, layer, layer == 0),
            f"layer_forward_{layer}",
            scalars,
            ins,
            [
                (act, act_spec),
                (wide, act_spec),
                (act, act_spec),
                (act, act_spec),
                (stack, at_offset((rows, feat), layer)),
            ],
            [ext_scratch, *w_scratch],
            aliases,
            flops=6 * 10**8,
            moved=4 * 10**6,
        )
        hidden.append((hid, act_spec))
        aggs.append(agg)
        pres.append(pre)

    top = spans - 1
    arrived = back_rows(outgoing).reshape(rows, feat)
    column = (rows, 1)
    ins = [
        hidden[top],
        (arrived, act_spec),
        vals_in,
        (w_out, whole((feat, classes))),
        (labels.reshape(spans, *column), of_span(column)),
        (train_mask.reshape(spans, *column), of_span(column)),
        *weights,
        (acts_buf, ANY),
    ]
    agg, d_pre, remote, part, acts_buf = run(
        functools.partial(top_kernel, top),
        "top_layer",
        scalars,
        ins,
        [
            (act, act_spec),
            (act, act_spec),
            (sds((peers, slots, feat), BF), whole((peers, slots, feat))),
            (wide, act_spec),
            (stack, at_offset((rows, feat), top)),
        ],
        [ext_scratch, *w_scratch, d_ext_scratch],
        {len(ins) - 1: 4},
        flops=10**9,
        moved=5 * 10**6,
    )
    aggs.append(agg)

    def send_home(buf):
        return run(
            home_kernel,
            "put_home",
            scalars,
            [(buf, ANY), *[(shift(buf[s], "layer", s), ANY) for s in range(1, spans)]],
            [(sds((1, spans, rows, feat), BF), ANY)],
            [pltpu.SemaphoreType.DMA((4,))],
            moved=2 * 10**6,
        )[0]

    def weight_partials(layer, d_pre):
        keep, send = run(
            grad_kernel,
            f"weight_partials_{layer}",
            scalars,
            [hidden[layer], (aggs[layer], act_spec), (d_pre, act_spec)],
            [(square, square_spec), (square, square_spec)],
            flops=3 * 10**8,
            moved=2 * 10**6,
        )
        return keep, sibling(send)

    layer_acts = send_home(acts_buf)
    chunk_rows = feat // peers
    chunk_shape = (2, chunk_rows, feat)
    grads_buf = None
    chunks = {}
    for layer in range(top - 1, -1, -1):
        returned = exchange(remote)
        got_chunk = returned.shape[1] > slots
        partials = weight_partials(layer + 1, d_pre)
        carry = layer > 0
        out_rows = slots + chunk_rows if carry else slots
        ins = [
            (returned, whole(returned.shape)),
            (part, act_spec),
            (pres[layer], act_spec),
            vals_in,
            pick_in,
            *weights,
        ]
        if carry:
            ins += [(partials[0], square_spec), (partials[1], square_spec)]
        aliases = None
        if grads_buf is not None:
            ins.append((grads_buf, ANY))
            aliases = {len(ins) - 1: 3}
        outs = [
            (act, act_spec),
            (sds((peers, out_rows, feat), BF), whole((peers, out_rows, feat))),
            (wide, act_spec),
            (stack, at_offset((rows, feat), layer + 1)),
        ]
        if got_chunk:
            outs.append((sds(chunk_shape, BF), whole(chunk_shape)))
        result = run(
            functools.partial(backward_kernel, layer, carry, grads_buf is not None),
            f"layer_backward_{layer}",
            scalars,
            ins,
            outs,
            [*w_scratch, d_ext_scratch],
            aliases,
            flops=7 * 10**8,
            moved=5 * 10**6,
        )
        d_pre, remote, part, grads_buf = result[:4]
        if got_chunk:
            chunks[layer + 2] = result[4]

    last = weight_partials(0, d_pre)
    joined = run(
        join_kernel,
        "join_rows",
        scalars,
        [
            (remote, whole(remote.shape)),
            (partials[0], square_spec),
            (partials[1], square_spec),
            (last[0], square_spec),
            (last[1], square_spec),
        ],
        [
            (
                sds((peers, slots + 2 * chunk_rows, feat), BF),
                whole((peers, slots + 2 * chunk_rows, feat)),
            )
        ],
        moved=3 * 10**6,
    )[0]
    returned = exchange(joined)
    c_2 = chunks[2]
    grads_buf, sums = run(
        end_kernel,
        "input_grads",
        scalars,
        [
            (returned, whole(returned.shape)),
            (part, act_spec),
            pick_in,
            (grads_buf, ANY),
            (chunks[3], whole(chunk_shape)),
            (c_2, whole(chunk_shape)),
        ],
        [
            (stack, at_offset((rows, feat), 0)),
            (sds((spans, *chunk_shape), BF), whole((spans, *chunk_shape))),
        ],
        aliases={3: 0},
        flops=10**8,
        moved=3 * 10**6,
    )
    spread = run(
        layer_sum_kernel,
        "sum_over_layer",
        scalars,
        [
            (sums, whole((spans, *chunk_shape))),
            *[(shift(sums[s], "layer", s), whole(chunk_shape)) for s in range(1, spans)],
        ],
        [(sds((peers, chunk_rows, feat), BF), whole((peers, chunk_rows, feat)))],
        moved=10**6,
    )[0]
    act_grads = send_home(grads_buf)
    gathered = exchange(spread).reshape(feat, feat)
    grad_self, grad_neigh = run(
        functools.partial(scale_kernel, scale),
        "scale_grads",
        scalars,
        [(gathered, square_spec), (sibling(gathered), square_spec)],
        [(sds((1, feat, feat), F32), whole((1, feat, feat)))] * 2,
        moved=3 * 10**6,
    )
    return (layer_acts, act_grads, grad_self, grad_neigh)


def solution(mesh):
    in_specs = (
        P(None, "node", None),
        P("layer", None, None),
        P("layer", None, None),
        P(),
        P(None, "node"),
        P(None, "node"),
        P(None, "node", None, None),
        P(None, "node", None, None, None, None),
        P(None, "node", None, None),
        P(None, "node", None),
    )
    out_specs = (
        P("layer", None, "node", None),
        P("layer", None, "node", None),
        P("layer", None, None),
        P("layer", None, None),
    )
    return jax.shard_map(body, mesh=mesh, in_specs=in_specs, out_specs=out_specs, check_vma=False)
```

```python
import functools

import jax
import jax.numpy as jnp
from jax import lax
from jax.experimental import pallas as pl
from jax.experimental.pallas import tpu as pltpu
from jax.sharding import PartitionSpec as P

BF = jnp.bfloat16
F32 = jnp.float32
NN = (((1,), (0,)), ((), ()))
NT = (((1,), (1,)), ((), ()))
TN = (((0,), (0,)), ((), ()))
ANY = pl.BlockSpec(memory_space=pltpu.HBM)
LOCAL = pl.BlockSpec(memory_space=pltpu.VMEM)
VMEM_BYTES = 40 * 1024 * 1024


def dot(a, b, dims=NN):
    return lax.dot_general(a, b, dims, preferred_element_type=F32)


def shift(value, axis, steps):
    count = lax.axis_size(axis)
    return lax.ppermute(value, axis, [(i, (i + steps) % count) for i in range(count)])


def sibling(value):
    count = lax.axis_size("node")
    return lax.ppermute(value, "node", [(i, i ^ 1) for i in range(count)])


def exchange(value):
    return lax.all_to_all(value, "node", split_axis=0, concat_axis=0, tiled=True)


def whole(shape):
    return pl.BlockSpec(shape, lambda i, ids, cols: (0,) * len(shape))


def of_span(shape):
    return pl.BlockSpec((None, *shape), lambda i, ids, cols: (ids[0], *((0,) * len(shape))))


def at_offset(shape, layer):
    return pl.BlockSpec(
        (None, *shape),
        lambda i, ids, cols: (lax.rem(layer - ids[0] + 4, 4), *((0,) * len(shape))),
    )


def sds(shape, dtype):
    return jax.ShapeDtypeStruct(shape, dtype)


def run(kernel, name, scalars, ins, outs, scratch=(), aliases=None, flops=0, moved=0):
    arrays = [
        a if s is LOCAL else pltpu.with_memory_space_constraint(a, pltpu.HBM) for a, s in ins
    ]
    return pl.pallas_call(
        kernel,
        name=name,
        grid_spec=pltpu.PrefetchScalarGridSpec(
            num_scalar_prefetch=2,
            grid=(1,),
            in_specs=[s for _, s in ins],
            out_specs=[s for _, s in outs],
            scratch_shapes=list(scratch),
        ),
        out_shape=[pltpu.HBM(o.shape, o.dtype) for o, _ in outs],
        input_output_aliases={} if aliases is None else {k + 2: v for k, v in aliases.items()},
        compiler_params=pltpu.CompilerParams(vmem_limit_bytes=VMEM_BYTES),
        cost_estimate=pl.CostEstimate(flops=flops, bytes_accessed=moved, transcendentals=0),
    )(*scalars, *arrays)


def weight_copies(which, core, w_refs, w_scr, sems):
    own_s, own_n, left, left_x, right, right_x, far, far_x = w_refs
    plans = {
        0: [(own_s, w_scr.at[0]), (own_n, w_scr.at[1])],
        1: [(right, w_scr.at[core]), (right_x, w_scr.at[1 - core])],
        2: [(far, w_scr.at[core]), (far_x, w_scr.at[1 - core])],
        3: [(left, w_scr.at[core]), (left_x, w_scr.at[1 - core])],
    }
    return [pltpu.make_async_copy(s, d, sems.at[n]) for n, (s, d) in enumerate(plans[which])]


def each_weight(layer, ids, w_refs, w_scr, sems, act):
    which = lax.rem(layer - ids[0] + 4, 4)
    for option in range(4):

        @pl.when(which == option)
        def _():
            for copy in weight_copies(option, ids[1], w_refs, w_scr, sems):
                act(copy)


def start_weights(layer, ids, w_refs, w_scr, sems):
    each_weight(layer, ids, w_refs, w_scr, sems, lambda copy: copy.start())


def wait_weights(layer, ids, w_refs, w_scr, sems):
    each_weight(layer, ids, w_refs, w_scr, sems, lambda copy: copy.wait())


def side_by_side(vals_ref, r, degree):
    return jnp.concatenate([vals_ref[r, j] for j in range(degree)], axis=1)


def aggregate_rows(ids, cols, vals_ref, ext):
    tiles, degree, size = vals_ref.shape[0], vals_ref.shape[1], vals_ref.shape[2]
    parts = []
    for r in range(tiles):
        base = ids[0] * (tiles * degree) + r * degree
        picked = jnp.concatenate(
            [ext[pl.ds(pl.multiple_of(cols[base + j] * size, size), size), :] for j in range(degree)],
            axis=0,
        )
        parts.append(dot(side_by_side(vals_ref, r, degree), picked))
    return jnp.concatenate(parts, axis=0).astype(BF)


def spread_rows(ids, cols, vals_ref, d_agg, d_ext):
    tiles, degree, size = vals_ref.shape[0], vals_ref.shape[1], vals_ref.shape[2]
    d_ext[...] = jnp.zeros_like(d_ext)
    for r in range(tiles):
        base = ids[0] * (tiles * degree) + r * degree
        pieces = dot(side_by_side(vals_ref, r, degree), d_agg[r * size : (r + 1) * size], TN)
        for j in range(degree):
            rows = pl.ds(pl.multiple_of(cols[base + j] * size, size), size)
            d_ext[rows, :] += pieces[j * size : (j + 1) * size]


def sigmoid(v):
    return 1.0 / (1.0 + jnp.exp(-v))


def pre_kernel(ids, cols, h_ref, rows_ref, counts_ref, pick_ref, out_ref):
    peers, slots = rows_ref.shape
    total, node_rows = pick_ref.shape
    bits = slots.bit_length() - 1
    slot = lax.broadcasted_iota(jnp.int32, (total, peers), 0)
    owner = lax.broadcasted_iota(jnp.int32, (total, peers), 1)
    mine = lax.shift_right_logical(slot, bits) == owner
    wide = dot(mine.astype(F32).astype(BF), rows_ref[...].astype(F32).astype(BF))
    slot_k = lax.broadcasted_iota(jnp.int32, (total, slots), 0) & (slots - 1)
    in_slot = slot_k == lax.broadcasted_iota(jnp.int32, (total, slots), 1)
    row = jnp.sum(jnp.where(in_slot, wide, 0.0), axis=1, keepdims=True)
    counts = jnp.broadcast_to(counts_ref[...].astype(F32), (total, peers))
    count = jnp.sum(jnp.where(mine, counts, 0.0), axis=1, keepdims=True)
    k = (lax.broadcasted_iota(jnp.int32, (total, 1), 0) & (slots - 1)).astype(F32)
    row = jnp.where(k < count, row, -1.0)
    place = lax.broadcasted_iota(jnp.int32, (total, node_rows), 1).astype(F32)
    pick = (place == row).astype(F32).astype(BF)
    pick_ref[...] = pick
    out_ref[...] = dot(pick, h_ref[...]).astype(BF)


def forward_math(layer, ids, cols, h_ref, arr_ref, vals_ref, w_refs, ext, w_scr, sems):
    start_weights(layer, ids, w_refs, w_scr, sems)
    rows = h_ref.shape[0]
    ext[0:rows, :] = h_ref[...]
    ext[rows : 2 * rows, :] = arr_ref[...]
    agg = aggregate_rows(ids, cols, vals_ref, ext)
    wait_weights(layer, ids, w_refs, w_scr, sems)
    pre = dot(h_ref[...], w_scr[0]) + dot(agg, w_scr[1])
    sig = sigmoid(pre)
    return agg, pre, sig, (pre * sig).astype(BF)


def forward_kernel(layer, first, ids, cols, h_ref, arr_ref, vals_ref, pick_ref, *rest):
    w_refs, rest = rest[:8], rest[8:]
    if not first:
        rest = rest[1:]
    agg_ref, pre_ref, hid_ref, out_ref, buf_ref, ext, w_scr, sems = rest
    agg, pre, _, hid = forward_math(
        layer, ids, cols, h_ref, arr_ref, vals_ref, w_refs, ext, w_scr, sems
    )
    agg_ref[...] = agg
    pre_ref[...] = pre
    hid_ref[...] = hid
    buf_ref[...] = hid
    out_ref[...] = dot(pick_ref[...], hid).astype(BF)


def backward_math(ids, cols, d_pre, vals_ref, w_scr, d_ext):
    d_agg = dot(d_pre, w_scr[1], NT).astype(BF)
    spread_rows(ids, cols, vals_ref, d_agg, d_ext)
    return dot(d_pre, w_scr[0], NT)


def top_kernel(layer, ids, cols, h_ref, arr_ref, vals_ref, wout_ref, lab_ref, mask_ref, *rest):
    w_refs, rest = rest[:8], rest[9:]
    agg_ref, dpre_ref, remote_ref, part_ref, buf_ref, ext, w_scr, sems, d_ext = rest
    rows = h_ref.shape[0]
    agg, pre, sig, hid = forward_math(
        layer, ids, cols, h_ref, arr_ref, vals_ref, w_refs, ext, w_scr, sems
    )
    agg_ref[...] = agg
    buf_ref[...] = hid
    logits = dot(hid, wout_ref[...])
    expo = jnp.exp(logits)
    probs = expo / jnp.sum(expo, axis=1, keepdims=True)
    onehot = (lab_ref[...] == lax.broadcasted_iota(jnp.int32, logits.shape, 1)).astype(F32)
    g_logits = (mask_ref[...].astype(F32) * (probs - onehot)).astype(BF)
    d_out = dot(g_logits, wout_ref[...], NT).astype(BF)
    d_pre = (d_out.astype(F32) * (sig * (1.0 + pre * (1.0 - sig)))).astype(BF)
    dpre_ref[...] = d_pre
    back = backward_math(ids, cols, d_pre, vals_ref, w_scr, d_ext)
    part_ref[...] = back + d_ext[0:rows, :]
    remote_ref[...] = d_ext[rows : 2 * rows, :].astype(BF).reshape(remote_ref.shape)


def chunk_sum(block):
    total = block[0:2].astype(F32)
    for n in range(2, block.shape[0], 2):
        total = total + block[n : n + 2].astype(F32)
    return total


def backward_kernel(layer, has_buf, ids, cols, ret_ref, part_in, pre_ref, vals_ref, pick_ref, *rest):
    w_refs, rest = rest[:8], rest[9 + has_buf :]
    dpre_ref, out_ref, part_ref, buf_ref, w_scr, sems, d_ext, remote, out_sem = rest
    start_weights(layer, ids, w_refs, w_scr, sems)
    rows, feat = part_in.shape
    peers, slots = remote.shape[0], remote.shape[1]
    returned = ret_ref[:, 0:slots, :].reshape(rows, feat)
    d_out = (part_in[...] + dot(pick_ref[...], returned, TN)).astype(BF)
    buf_ref[...] = d_out
    pre = pre_ref[...]
    sig = sigmoid(pre)
    d_pre = (d_out.astype(F32) * (sig * (1.0 + pre * (1.0 - sig)))).astype(BF)
    dpre_ref[...] = d_pre
    wait_weights(layer, ids, w_refs, w_scr, sems)
    back = backward_math(ids, cols, d_pre, vals_ref, w_scr, d_ext)
    remote[...] = d_ext[rows : 2 * rows, :].astype(BF).reshape(peers, slots, feat)
    copy = pltpu.make_async_copy(remote, out_ref.at[:, pl.ds(0, slots), :], out_sem)
    copy.start()
    part_ref[...] = back + d_ext[0:rows, :]
    copy.wait()


def grad_kernel(ids, cols, h_ref, agg_ref, dpre_ref, keep_ref, send_ref):
    d_pre = dpre_ref[...]
    on_rows = dot(h_ref[...], d_pre, TN).astype(BF)
    on_agg = dot(agg_ref[...], d_pre, TN).astype(BF)

    @pl.when(ids[1] == 0)
    def _():
        keep_ref[...] = on_rows
        send_ref[...] = on_agg

    @pl.when(ids[1] != 0)
    def _():
        keep_ref[...] = on_agg
        send_ref[...] = on_rows


def carry_kernel(first, ids, cols, keep_ref, recv_ref, *rest):
    out_ref, both, sem = rest[-3:]
    total = (keep_ref[...].astype(F32) + recv_ref[...].astype(F32)).astype(BF)
    both[...] = total.reshape(both.shape)
    copy = pltpu.make_async_copy(both, out_ref.at[:, pl.ds(first, both.shape[1]), :], sem)
    copy.start()
    copy.wait()


def chunk_kernel(ids, cols, ret_ref, out_ref):
    out_ref[...] = chunk_sum(ret_ref[:, 8:24, :]).astype(BF)


def end_kernel(ids, cols, ret_ref, part_in, pick_ref, buf_in, c_3, c_2, buf_ref, chunks_ref):
    rows, feat = part_in.shape
    returned = ret_ref[:, 0:8, :].reshape(rows, feat)
    buf_ref[...] = (part_in[...] + dot(pick_ref[...], returned, TN)).astype(BF)
    home = ids[0]
    chunks_ref[lax.rem(7 - home, 4)] = c_3[...]
    chunks_ref[lax.rem(6 - home, 4)] = c_2[...]
    chunks_ref[lax.rem(5 - home, 4)] = chunk_sum(ret_ref[:, 8:24, :]).astype(BF)
    chunks_ref[lax.rem(4 - home, 4)] = chunk_sum(ret_ref[:, 24:40, :]).astype(BF)


def layer_sum_kernel(ids, cols, own_ref, a_ref, b_ref, c_ref, out_ref):
    total = own_ref[0].astype(F32) + a_ref[...].astype(F32)
    total = (total + b_ref[...].astype(F32) + c_ref[...].astype(F32)).astype(BF)
    for n in range(0, out_ref.shape[0], 2):
        out_ref[n : n + 2] = total


def scale_kernel(scale, ids, cols, mine_ref, other_ref, self_ref, neigh_ref):
    mine = mine_ref[...].astype(F32) * scale
    other = other_ref[...].astype(F32) * scale

    @pl.when(ids[1] == 0)
    def _():
        self_ref[0] = mine
        neigh_ref[0] = other

    @pl.when(ids[1] != 0)
    def _():
        self_ref[0] = other
        neigh_ref[0] = mine


def home_kernel(ids, cols, own_ref, a_ref, b_ref, c_ref, out_ref):
    home = ids[0]
    out_ref[0, home] = own_ref[...]
    out_ref[0, lax.rem(home + 3, 4)] = a_ref[...]
    out_ref[0, lax.rem(home + 2, 4)] = b_ref[...]
    out_ref[0, lax.rem(home + 1, 4)] = c_ref[...]


def body(
    features,
    w_self,
    w_neigh,
    w_out,
    labels,
    train_mask,
    tile_cols,
    tile_vals,
    send_rows,
    send_counts,
):
    home = lax.axis_index("layer")
    node = lax.axis_index("node")
    core = lax.rem(node, 2)
    spans, rows, feat = features.shape
    peers, slots = send_rows.shape[2], send_rows.shape[3]
    tiles, degree, size = tile_vals.shape[2], tile_vals.shape[3], tile_vals.shape[4]
    classes = w_out.shape[1]
    scale = 1.0 / (spans * rows * peers)
    scalars = (jnp.stack([home, core]).astype(jnp.int32), tile_cols.reshape(-1))
    act = sds((rows, feat), BF)
    square = sds((feat, feat), BF)
    stack = sds((spans, rows, feat), BF)
    wide = sds((rows, feat), F32)
    act_spec, square_spec = whole((rows, feat)), whole((feat, feat))

    features_in = (features, of_span((rows, feat)))
    vals_in = (
        tile_vals.reshape(spans, tiles, degree, size, size),
        of_span((tiles, degree, size, size)),
    )
    w_scratch = [pltpu.VMEM((2, feat, feat), BF), pltpu.SemaphoreType.DMA((2,))]
    ext_scratch = pltpu.VMEM((2 * rows, feat), BF)
    d_ext_scratch = pltpu.VMEM((2 * rows, feat), F32)

    mine = jnp.where(core == 0, w_self[0], w_neigh[0])
    left = shift(mine, "layer", 1)
    right = shift(mine, "layer", -1)
    far = shift(mine, "layer", 2)
    pick, outgoing = run(
        pre_kernel,
        "gather_rows",
        scalars,
        [
            features_in,
            (send_rows.reshape(spans, peers, slots), of_span((peers, slots))),
            (send_counts.reshape(spans, 1, peers), of_span((1, peers))),
        ],
        [
            (sds((peers * slots, rows), BF), whole((peers * slots, rows))),
            (sds((peers * slots, feat), BF), whole((peers * slots, feat))),
        ],
        flops=10**8,
        moved=10**6,
    )
    pick_in = (pick, whole(pick.shape))
    arrived = exchange(outgoing.reshape(peers, slots, feat))
    arrived, left, right, far = lax.optimization_barrier((arrived, left, right, far))
    sources = (w_self[0], w_neigh[0], left, sibling(left), right, sibling(right), far, sibling(far))
    weights = [(w, ANY) for w in sources]

    hidden, aggs, pres = [features_in], [], []
    acts_buf = None
    for layer in range(spans - 1):
        if layer:
            arrived = exchange(outgoing.reshape(peers, slots, feat))
        ins = [hidden[layer], (arrived.reshape(rows, feat), LOCAL), vals_in, pick_in, *weights]
        aliases = None
        if layer:
            ins.append((acts_buf, ANY))
            aliases = {len(ins) - 1: 4}
        agg, pre, hid, outgoing, acts_buf = run(
            functools.partial(forward_kernel, layer, layer == 0),
            f"layer_forward_{layer}",
            scalars,
            ins,
            [
                (act, act_spec),
                (wide, act_spec),
                (act, act_spec),
                (act, act_spec),
                (stack, at_offset((rows, feat), layer)),
            ],
            [ext_scratch, *w_scratch],
            aliases,
            flops=6 * 10**8,
            moved=4 * 10**6,
        )
        hidden.append((hid, act_spec))
        aggs.append(agg)
        pres.append(pre)

    top = spans - 1
    arrived = exchange(outgoing.reshape(peers, slots, feat)).reshape(rows, feat)
    column = (rows, 1)
    ins = [
        hidden[top],
        (arrived, LOCAL),
        vals_in,
        (w_out, whole((feat, classes))),
        (labels.reshape(spans, *column), of_span(column)),
        (train_mask.reshape(spans, *column), of_span(column)),
        *weights,
        (acts_buf, ANY),
    ]
    agg, d_pre, remote, part, acts_buf = run(
        functools.partial(top_kernel, top),
        "top_layer",
        scalars,
        ins,
        [
            (act, act_spec),
            (act, act_spec),
            (sds((peers, slots, feat), BF), whole((peers, slots, feat))),
            (wide, act_spec),
            (stack, at_offset((rows, feat), top)),
        ],
        [ext_scratch, *w_scratch, d_ext_scratch],
        {len(ins) - 1: 4},
        flops=10**9,
        moved=5 * 10**6,
    )
    aggs.append(agg)

    def travel(buf):
        return [shift(buf[s], "layer", s) for s in range(1, spans)]

    def send_home(buf, pieces):
        block = pl.BlockSpec((None, rows, feat), lambda i, ids, cols: (0, 0, 0))
        shape = (1, spans, rows, feat)
        return run(
            home_kernel,
            "put_home",
            scalars,
            [(buf, block), *[(piece, LOCAL) for piece in pieces]],
            [(sds(shape, BF), whole(shape))],
            moved=2 * 10**6,
        )[0]

    def weight_partials(layer, d_pre):
        keep, send = run(
            grad_kernel,
            f"weight_partials_{layer}",
            scalars,
            [hidden[layer], (aggs[layer], act_spec), (d_pre, act_spec)],
            [(square, square_spec), (square, square_spec)],
            flops=3 * 10**8,
            moved=2 * 10**6,
        )
        return keep, sibling(send)

    layer_acts = send_home(acts_buf, travel(acts_buf))
    chunk_rows = feat // peers
    chunk_shape = (2, chunk_rows, feat)
    chunk_scratch = [pltpu.VMEM((peers, chunk_rows, feat), BF), pltpu.SemaphoreType.DMA]

    def carry(partials, first, width, buf=None):
        ins = [(partials[0], square_spec), (partials[1], LOCAL)]
        if buf is not None:
            ins.append((buf, ANY))
        return run(
            functools.partial(carry_kernel, first),
            "carry_partials",
            scalars,
            ins,
            [(sds((peers, width, feat), BF), ANY)],
            chunk_scratch,
            None if buf is None else {2: 0},
            moved=2 * 10**6,
        )[0]

    grads_buf = None
    chunks = {}
    for layer in range(top - 1, -1, -1):
        returned = exchange(remote)
        if layer < top - 1:
            chunks[layer + 2] = run(
                chunk_kernel,
                "sum_chunks",
                scalars,
                [(returned, LOCAL)],
                [(sds(chunk_shape, BF), whole(chunk_shape))],
                moved=10**6,
            )[0]
        width = slots + chunk_rows * (1 if layer else 2)
        carried = carry(weight_partials(layer + 1, d_pre), slots, width)
        ins = [
            (returned, LOCAL),
            (part, act_spec),
            (pres[layer], act_spec),
            vals_in,
            pick_in,
            *weights,
            (carried, ANY),
        ]
        aliases = {len(ins) - 1: 1}
        if grads_buf is not None:
            ins.append((grads_buf, ANY))
            aliases[len(ins) - 1] = 3
        d_pre, remote, part, grads_buf = run(
            functools.partial(backward_kernel, layer, grads_buf is not None),
            f"layer_backward_{layer}",
            scalars,
            ins,
            [
                (act, act_spec),
                (sds((peers, width, feat), BF), ANY),
                (wide, act_spec),
                (stack, at_offset((rows, feat), layer + 1)),
            ],
            [
                *w_scratch,
                d_ext_scratch,
                pltpu.VMEM((peers, slots, feat), BF),
                pltpu.SemaphoreType.DMA,
            ],
            aliases,
            flops=7 * 10**8,
            moved=5 * 10**6,
        )
        if layer == 1:
            remote, layer_acts = lax.optimization_barrier((remote, layer_acts))

    joined = carry(weight_partials(0, d_pre), slots + chunk_rows, remote.shape[1], remote)
    returned = exchange(joined)
    grads_buf, sums = run(
        end_kernel,
        "input_grads",
        scalars,
        [
            (returned, LOCAL),
            (part, act_spec),
            pick_in,
            (grads_buf, ANY),
            (chunks[3], whole(chunk_shape)),
            (chunks[2], whole(chunk_shape)),
        ],
        [
            (stack, at_offset((rows, feat), 0)),
            (sds((spans, *chunk_shape), BF), whole((spans, *chunk_shape))),
        ],
        aliases={3: 0},
        flops=10**8,
        moved=3 * 10**6,
    )
    spread = run(
        layer_sum_kernel,
        "sum_over_layer",
        scalars,
        [
            (sums, whole((spans, *chunk_shape))),
            *[(shift(sums[s], "layer", s), LOCAL) for s in range(1, spans)],
        ],
        [(sds((peers, chunk_rows, feat), BF), whole((peers, chunk_rows, feat)))],
        moved=10**6,
    )[0]
    spread, grads_buf = lax.optimization_barrier((spread, grads_buf))
    pieces = travel(grads_buf)
    gathered, *pieces = lax.optimization_barrier((exchange(spread), *pieces))
    act_grads = send_home(grads_buf, pieces)
    gathered = gathered.reshape(feat, feat)
    grad_self, grad_neigh = run(
        functools.partial(scale_kernel, scale),
        "scale_grads",
        scalars,
        [(gathered, LOCAL), (sibling(gathered), LOCAL)],
        [(sds((1, feat, feat), F32), whole((1, feat, feat)))] * 2,
        moved=3 * 10**6,
    )
    return (layer_acts, act_grads, grad_self, grad_neigh)


def solution(mesh):
    in_specs = (
        P(None, "node", None),
        P("layer", None, None),
        P("layer", None, None),
        P(),
        P(None, "node"),
        P(None, "node"),
        P(None, "node", None, None),
        P(None, "node", None, None, None, None),
        P(None, "node", None, None),
        P(None, "node", None),
    )
    out_specs = (
        P("layer", None, "node", None),
        P("layer", None, "node", None),
        P("layer", None, None),
        P("layer", None, None),
    )
    return jax.shard_map(body, mesh=mesh, in_specs=in_specs, out_specs=out_specs, check_vma=False)
```

```python
import functools

import jax
import jax.numpy as jnp
from jax import lax
from jax.experimental import pallas as pl
from jax.experimental.pallas import tpu as pltpu
from jax.sharding import PartitionSpec as P

BF = jnp.bfloat16
F32 = jnp.float32
NN = (((1,), (0,)), ((), ()))
NT = (((1,), (1,)), ((), ()))
TN = (((0,), (0,)), ((), ()))
FAR = pl.BlockSpec(memory_space=pltpu.HBM)
LOCAL = pl.BlockSpec(memory_space=pltpu.VMEM)
VMEM_BYTES = 16 * 1024 * 1024


def dot(a, b, dims=NN):
    return lax.dot_general(a, b, dims, preferred_element_type=F32)


def shift(value, axis, steps):
    count = lax.axis_size(axis)
    return lax.ppermute(value, axis, [(i, (i + steps) % count) for i in range(count)])


def sibling(value):
    count = lax.axis_size("node")
    return lax.ppermute(value, "node", [(i, i ^ 1) for i in range(count)])


def exchange(value):
    return lax.all_to_all(value, "node", split_axis=0, concat_axis=0, tiled=True)


def of_span(shape):
    return pl.BlockSpec((None, *shape), lambda i, ids, cols: (ids[0], *((0,) * len(shape))))


def whole(shape):
    return pl.BlockSpec(shape, lambda i, ids, cols: (0,) * len(shape))


def near(shape, dtype=BF):
    return pltpu.VMEM(shape, dtype), LOCAL


def far_block(shape, dtype=BF):
    return pltpu.HBM(shape, dtype), whole(shape)


def run(kernel, name, scalars, ins, outs, scratch=(), aliases=None, flops=0, moved=0):
    ins = [v if isinstance(v, tuple) else (v, LOCAL) for v in ins]
    arrays = [
        pltpu.with_memory_space_constraint(a, pltpu.VMEM if s is LOCAL else pltpu.HBM)
        for a, s in ins
    ]
    return pl.pallas_call(
        kernel,
        name=name,
        grid_spec=pltpu.PrefetchScalarGridSpec(
            num_scalar_prefetch=2,
            grid=(1,),
            in_specs=[s for _, s in ins],
            out_specs=[s for _, s in outs],
            scratch_shapes=list(scratch),
        ),
        out_shape=[o for o, _ in outs],
        input_output_aliases={} if aliases is None else {k + 2: v for k, v in aliases.items()},
        compiler_params=pltpu.CompilerParams(vmem_limit_bytes=VMEM_BYTES),
        cost_estimate=pl.CostEstimate(flops=flops, bytes_accessed=moved, transcendentals=0),
    )(*scalars, *arrays)


def tie(*values):
    return lax.optimization_barrier(values)


def weight_copies(layer, ids, w_refs, w_scr, sems, act):
    own_s, own_n, left, left_x, right, right_x, far, far_x = w_refs
    core = ids[1]
    pairs = [
        [(own_s, 0), (own_n, 1)],
        [(right, core), (right_x, 1 - core)],
        [(far, core), (far_x, 1 - core)],
        [(left, core), (left_x, 1 - core)],
    ]
    which = lax.rem(layer - ids[0] + 4, 4)
    for option, pair in enumerate(pairs):

        @pl.when(which == option)
        def _():
            for n, (ref, place) in enumerate(pair):
                act(pltpu.make_async_copy(ref, w_scr.at[place], sems.at[n]))


def start_weights(*args):
    weight_copies(*args, lambda copy: copy.start())


def wait_weights(*args):
    weight_copies(*args, lambda copy: copy.wait())


def side_by_side(vals_ref, r, degree):
    return jnp.concatenate([vals_ref[r, j] for j in range(degree)], axis=1)


def aggregate_rows(ids, cols, vals_ref, ext):
    tiles, degree, size = vals_ref.shape[0], vals_ref.shape[1], vals_ref.shape[2]
    parts = []
    for r in range(tiles):
        picked = jnp.concatenate(
            [ext[pl.ds(pl.multiple_of(cols[ids[0], r, j] * size, size), size), :] for j in range(degree)],
            axis=0,
        )
        parts.append(dot(side_by_side(vals_ref, r, degree), picked))
    return jnp.concatenate(parts, axis=0).astype(BF)


def spread_rows(ids, cols, vals_ref, d_agg, d_ext):
    tiles, degree, size = vals_ref.shape[0], vals_ref.shape[1], vals_ref.shape[2]
    d_ext[...] = jnp.zeros_like(d_ext)
    for r in range(tiles):
        pieces = dot(side_by_side(vals_ref, r, degree), d_agg[r * size : (r + 1) * size], TN)
        for j in range(degree):
            rows = pl.ds(pl.multiple_of(cols[ids[0], r, j] * size, size), size)
            d_ext[rows, :] += pieces[j * size : (j + 1) * size]


def to_slot(value_ref, layer, ids, buf_ref, sem):
    return pltpu.make_async_copy(value_ref, buf_ref.at[lax.rem(layer - ids[0] + 4, 4)], sem)


def sigmoid(v):
    return 1.0 / (1.0 + jnp.exp(-v))


def pre_kernel(ids, cols, h_ref, rows_ref, counts_ref, vals_ref, pick_ref, out_ref, h_out, vals_out, pick_far):
    slots, peers = rows_ref.shape
    total, node_rows = pick_ref.shape
    bits = slots.bit_length() - 1
    slot = lax.broadcasted_iota(jnp.int32, (total, peers), 0)
    owner = lax.broadcasted_iota(jnp.int32, (total, peers), 1)
    mine = lax.shift_right_logical(slot, bits) == owner
    wide = dot(mine.astype(F32).astype(BF), rows_ref[...].astype(F32).astype(BF), NT)
    slot_k = lax.broadcasted_iota(jnp.int32, (total, slots), 0) & (slots - 1)
    in_slot = slot_k == lax.broadcasted_iota(jnp.int32, (total, slots), 1)
    row = jnp.sum(jnp.where(in_slot, wide, 0.0), axis=1, keepdims=True)
    counts = jnp.broadcast_to(counts_ref[...].astype(F32), (total, peers))
    count = jnp.sum(jnp.where(mine, counts, 0.0), axis=1, keepdims=True)
    k = (lax.broadcasted_iota(jnp.int32, (total, 1), 0) & (slots - 1)).astype(F32)
    row = jnp.where(k < count, row, -1.0)
    place = lax.broadcasted_iota(jnp.int32, (total, node_rows), 1).astype(F32)
    pick = (place == row).astype(F32).astype(BF)
    pick_ref[...] = pick
    pick_far[...] = pick
    out_ref[...] = dot(pick, h_ref[...]).astype(BF)
    h_out[...] = h_ref[...]
    vals_out[...] = vals_ref[...]


def forward_math(layer, ids, cols, h_ref, arr_ref, vals_ref, w_refs, w_ref, sems, ext):
    start_weights(layer, ids, w_refs, w_ref, sems)
    rows = h_ref.shape[0]
    ext[0:rows, :] = h_ref[...]
    ext[rows : 2 * rows, :] = arr_ref[...]
    agg = aggregate_rows(ids, cols, vals_ref, ext)
    wait_weights(layer, ids, w_refs, w_ref, sems)
    pre = dot(h_ref[...], w_ref[0]) + dot(agg, w_ref[1])
    sig = sigmoid(pre)
    return agg, pre, sig, (pre * sig).astype(BF)


def forward_kernel(layer, ids, cols, h_ref, arr_ref, vals_ref, pick_ref, *rest):
    w_refs, rest = rest[:8], rest[-9:]
    agg_ref, pre_ref, hid_ref, out_ref, w_ref, buf_ref, ext, sems, buf_sem = rest
    agg, pre, _, hid = forward_math(
        layer, ids, cols, h_ref, arr_ref, vals_ref, w_refs, w_ref, sems, ext
    )
    hid_ref[...] = hid
    copy = to_slot(hid_ref, layer, ids, buf_ref, buf_sem)
    copy.start()
    out_ref[...] = dot(pick_ref[...], hid).astype(BF)
    agg_ref[...] = agg
    pre_ref[...] = pre
    copy.wait()


def backward_math(ids, cols, d_pre, vals_ref, w_ref, d_ext):
    d_agg = dot(d_pre, w_ref[1], NT).astype(BF)
    spread_rows(ids, cols, vals_ref, d_agg, d_ext)
    return dot(d_pre, w_ref[0], NT)


def weight_partials(ids, h_ref, agg, d_pre, keep_ref, send_ref):
    on_rows = dot(h_ref[...], d_pre, TN).astype(BF)
    on_agg = dot(agg, d_pre, TN).astype(BF)

    @pl.when(ids[1] == 0)
    def _():
        keep_ref[...] = on_rows
        send_ref[...] = on_agg

    @pl.when(ids[1] != 0)
    def _():
        keep_ref[...] = on_agg
        send_ref[...] = on_rows


def top_kernel(layer, ids, cols, h_ref, arr_ref, vals_ref, wout_ref, lab_ref, mask_ref, *rest):
    w_refs, rest = rest[:8], rest[9:]
    remote_ref, part_ref, keep_ref, send_ref, buf_ref, hid_ref, w_ref, ext, d_ext, sems, buf_sem = rest
    rows = h_ref.shape[0]
    agg, pre, sig, hid = forward_math(
        layer, ids, cols, h_ref, arr_ref, vals_ref, w_refs, w_ref, sems, ext
    )
    hid_ref[...] = hid
    copy = to_slot(hid_ref, layer, ids, buf_ref, buf_sem)
    copy.start()
    logits = dot(wout_ref[...], hid, NT)
    expo = jnp.exp(logits)
    probs = expo / jnp.sum(expo, axis=0, keepdims=True)
    label = lab_ref[pl.ds(ids[0], 1), :]
    onehot = (label == lax.broadcasted_iota(jnp.int32, logits.shape, 0)).astype(F32)
    live = mask_ref[pl.ds(ids[0], 1), :].astype(F32)
    g_logits = (live * (probs - onehot)).astype(BF)
    d_out = dot(g_logits, wout_ref[...], TN).astype(BF)
    d_pre = (d_out.astype(F32) * (sig * (1.0 + pre * (1.0 - sig)))).astype(BF)
    back = backward_math(ids, cols, d_pre, vals_ref, w_ref, d_ext)
    remote_ref[...] = d_ext[rows : 2 * rows, :].astype(BF).reshape(remote_ref.shape)
    part_ref[...] = back + d_ext[0:rows, :]
    weight_partials(ids, h_ref, agg, d_pre, keep_ref, send_ref)
    copy.wait()


def chunk_sum(block):
    total = block[0:2].astype(F32)
    for n in range(2, block.shape[0], 2):
        total = total + block[n : n + 2].astype(F32)
    return total


def backward_kernel(layer, carry, ids, cols, ret_ref, part_in, pre_ref, h_ref, agg_ref, *rest):
    (vals_ref, pick_ref, w_ref), rest = rest[:3], rest[3:]
    if carry:
        keep_in, recv_in, rest = rest[0], rest[1], rest[2:]
    if layer < 2:
        rest = rest[1:]
    out_ref, part_ref, buf_ref, keep_ref, send_ref, *rest = rest
    *chunk, dout_ref, d_ext, buf_sem = rest
    rows, feat = part_in.shape
    peers = out_ref.shape[0]
    slots = rows // peers
    returned = ret_ref[:, 0:slots, :].reshape(rows, feat)
    d_out = (part_in[...] + dot(pick_ref[...], returned, TN)).astype(BF)
    dout_ref[...] = d_out
    copy = to_slot(dout_ref, layer + 1, ids, buf_ref, buf_sem)
    copy.start()
    pre = pre_ref[...]
    sig = sigmoid(pre)
    d_pre = (d_out.astype(F32) * (sig * (1.0 + pre * (1.0 - sig)))).astype(BF)
    back = backward_math(ids, cols, d_pre, vals_ref, w_ref, d_ext)
    out_ref[:, 0:slots, :] = d_ext[rows : 2 * rows, :].astype(BF).reshape(peers, slots, feat)
    part_ref[...] = back + d_ext[0:rows, :]
    weight_partials(ids, h_ref, agg_ref[...], d_pre, keep_ref, send_ref)
    if carry:
        put_carry(keep_in, recv_in, out_ref, slots)
    if chunk:
        chunk[0][...] = chunk_sum(ret_ref[:, slots:, :]).astype(BF)
    copy.wait()


def put_carry(keep_ref, recv_ref, out_ref, first):
    peers, feat = out_ref.shape[0], out_ref.shape[2]
    size = keep_ref.shape[0] // peers
    total = (keep_ref[...].astype(F32) + recv_ref[...].astype(F32)).astype(BF)
    out_ref[:, first : first + size, :] = total.reshape(peers, size, feat)


def join_kernel(ids, cols, keep_a, recv_a, keep_b, recv_b, buf_in, out_ref):
    size = keep_a.shape[0] // out_ref.shape[0]
    first = out_ref.shape[1] - 2 * size
    put_carry(keep_a, recv_a, out_ref, first)
    put_carry(keep_b, recv_b, out_ref, first + size)


def end_kernel(ids, cols, ret_ref, part_in, pick_ref, c_3, dout_ref, o_0, o_1, o_2, o_3, all_sums):
    rows, feat = part_in.shape
    slots = rows // ret_ref.shape[0]
    size = c_3.shape[1]
    all_sums[3] = c_3[...]
    for n, layer in enumerate((2, 1, 0)):
        first = slots + n * size
        all_sums[layer] = chunk_sum(ret_ref[:, first : first + size, :]).astype(BF)
    for s, out_ref in enumerate((o_0, o_1, o_2, o_3)):
        out_ref[...] = all_sums[lax.rem(ids[0] + s, 4)]
    returned = ret_ref[:, 0:slots, :].reshape(rows, feat)
    dout_ref[...] = (part_in[...] + dot(pick_ref[...], returned, TN)).astype(BF)


def layer_sum_kernel(ids, cols, own_ref, a_ref, b_ref, c_ref, out_ref):
    total = own_ref[...].astype(F32) + a_ref[...].astype(F32)
    total = (total + b_ref[...].astype(F32) + c_ref[...].astype(F32)).astype(BF)
    for n in range(0, out_ref.shape[0], 2):
        out_ref[n : n + 2] = total


def scale_kernel(scale, ids, cols, mine_ref, other_ref, self_ref, neigh_ref):
    mine = mine_ref[...].astype(F32) * scale
    other = other_ref[...].astype(F32) * scale

    @pl.when(ids[1] == 0)
    def _():
        self_ref[0] = mine
        neigh_ref[0] = other

    @pl.when(ids[1] != 0)
    def _():
        self_ref[0] = other
        neigh_ref[0] = mine


def home_kernel(ids, cols, *refs):
    pieces, out_ref = refs[:-1], refs[-1]
    home = ids[0]
    for s, piece in enumerate(pieces[:4]):
        out_ref[0, lax.rem(home + 4 - s, 4)] = piece[...]
    if len(pieces) > 4:

        @pl.when(home == 0)
        def _():
            for s, piece in enumerate(pieces[4:]):
                out_ref[0, lax.rem(4 - s, 4)] = piece[...]


def body(
    features,
    w_self,
    w_neigh,
    w_out,
    labels,
    train_mask,
    tile_cols,
    tile_vals,
    send_rows,
    send_counts,
):
    home = lax.axis_index("layer")
    node = lax.axis_index("node")
    core = lax.rem(node, 2)
    spans, rows, feat = features.shape
    peers, slots = send_rows.shape[2], send_rows.shape[3]
    tiles, degree, size = tile_vals.shape[2], tile_vals.shape[3], tile_vals.shape[4]
    scale = 1.0 / (spans * rows * peers)
    scalars = (jnp.stack([home, core]).astype(jnp.int32), tile_cols.reshape(spans, tiles, degree))
    act, wide, square = near((rows, feat)), near((rows, feat), F32), near((feat, feat))
    ext_scratch = pltpu.VMEM((2 * rows, feat), BF)
    d_ext_scratch = pltpu.VMEM((2 * rows, feat), F32)
    all_shifts = range(1, spans)

    mine = jnp.where(core == 0, w_self[0], w_neigh[0])
    left, right, far = (shift(mine, "layer", s) for s in (1, -1, 2))
    pick, outgoing, features_0, vals, pick_far = run(
        pre_kernel,
        "gather_rows",
        scalars,
        [
            (features, of_span((rows, feat))),
            (send_rows.reshape(spans, peers, slots).swapaxes(1, 2), of_span((slots, peers))),
            (send_counts.reshape(spans, 1, peers), of_span((1, peers))),
            (
                tile_vals.reshape(spans, tiles, degree, size, size),
                of_span((tiles, degree, size, size)),
            ),
        ],
        [
            near((peers * slots, rows)),
            act,
            act,
            near((tiles, degree, size, size)),
            far_block((peers * slots, rows)),
        ],
        flops=10**8,
        moved=10**6,
    )
    arrived = exchange(outgoing.reshape(peers, slots, feat))
    arrived, left, right, far = tie(arrived, left, right, far)
    sources = [(w_self[0], FAR), (w_neigh[0], FAR), left, sibling(left), right, sibling(right)]
    sources += [far, sibling(far)]
    w_scratch = [pltpu.SemaphoreType.DMA((2,))]
    weight = near((2, feat, feat))

    hidden, aggs, pres, weights = [features_0], [], [], []
    top = spans - 1
    stack = (pltpu.HBM((spans, rows, feat), BF), FAR)
    buf_sem = pltpu.SemaphoreType.DMA
    acts_buf = None
    for layer in range(top):
        ins = [hidden[layer], arrived.reshape(rows, feat), vals, pick, *sources]
        if layer:
            ins.append((acts_buf, FAR))
        agg, pre, hid, outgoing, arranged, acts_buf = run(
            functools.partial(forward_kernel, layer),
            f"layer_forward_{layer}",
            scalars,
            ins,
            [act, wide, act, act, weight, stack],
            [ext_scratch, *w_scratch, buf_sem],
            {len(ins) - 1: 5} if layer else None,
            flops=6 * 10**8,
            moved=4 * 10**6,
        )
        hidden.append(hid)
        aggs.append(agg)
        pres.append(pre)
        weights.append(arranged)
        arrived = exchange(outgoing.reshape(peers, slots, feat))

    ins = [
        hidden[top],
        arrived.reshape(rows, feat),
        vals,
        w_out.T,
        labels,
        train_mask,
        *sources,
        (acts_buf, FAR),
    ]
    remote, part, keep, send, acts_buf = run(
        functools.partial(top_kernel, top),
        "top_layer",
        scalars,
        ins,
        [near((peers, slots, feat)), wide, square, square, stack],
        [
            pltpu.VMEM((rows, feat), BF),
            pltpu.VMEM((2, feat, feat), BF),
            ext_scratch,
            d_ext_scratch,
            *w_scratch,
            buf_sem,
        ],
        {len(ins) - 1: 4},
        flops=10**9,
        moved=5 * 10**6,
    )

    def travel(buf, home_too=True):
        pieces = []
        for s in all_shifts:
            pairs = [(i, (i + s) % spans) for i in range(spans) if home_too or (i + s) % spans]
            pieces.append(lax.ppermute(buf[s], "layer", pairs))
        return pieces

    def put_home(buf, *pieces):
        block = pl.BlockSpec((None, rows, feat), lambda i, ids, cols: (0, 0, 0))
        shape = (1, spans, rows, feat)
        return run(
            home_kernel,
            "put_home",
            scalars,
            [(buf, block), *pieces],
            [far_block(shape)],
            moved=2 * 10**6,
        )[0]

    chunk_rows = feat // peers
    chunk = near((2, chunk_rows, feat))
    pairs, grads_buf = [], None
    for layer in range(top - 1, -1, -1):
        returned, send = tie(exchange(remote), send)
        pairs.append((keep, sibling(send)))
        carry = layer < top - 1
        width = slots + chunk_rows * (carry + 2 * (layer == 0))
        ins = [
            returned,
            part,
            pres[layer],
            hidden[layer],
            aggs[layer],
            vals,
            pick,
            weights[layer],
        ]
        if carry:
            ins += pairs[-2]
        aliases = None
        if grads_buf is not None:
            ins.append((grads_buf, FAR))
            aliases = {len(ins) - 1: 2}
        last = far_block if layer == 0 else near
        outs = [near((peers, width, feat)), last((rows, feat), F32), stack, square, square]
        if layer == 0:
            outs.append(far_block((2, chunk_rows, feat)))
        remote, part, grads_buf, keep, send, *c_3 = run(
            functools.partial(backward_kernel, layer, carry),
            f"layer_backward_{layer}",
            scalars,
            ins,
            outs,
            [pltpu.VMEM((rows, feat), BF), d_ext_scratch, buf_sem],
            aliases,
            flops=10**9,
            moved=5 * 10**6,
        )
        if layer:
            remote, recv = tie(remote, pairs[-1][1])
            pairs[-1] = (pairs[-1][0], recv)

    joined = run(
        join_kernel,
        "join_rows",
        scalars,
        [*pairs[-1], keep, sibling(send), remote],
        [near((peers, slots + 3 * chunk_rows, feat))],
        aliases={4: 0},
        moved=3 * 10**6,
    )[0]
    joined, acts_buf, grads_buf = tie(joined, acts_buf, grads_buf)
    acts = travel(acts_buf)
    early = travel(grads_buf, False)
    returned, *pieces = tie(exchange(joined), *acts, *early)
    acts, early = pieces[:3], pieces[3:]
    layer_acts = put_home(acts_buf, *acts)
    d_out, own_sum, *sums = run(
        end_kernel,
        "input_grads",
        scalars,
        [
            returned,
            (part, whole((rows, feat))),
            (pick_far, whole(pick_far.shape)),
            (c_3[0], whole(c_3[0].shape)),
        ],
        [far_block((rows, feat)), chunk, chunk, chunk, chunk],
        [pltpu.VMEM((spans, 2, chunk_rows, feat), BF)],
        flops=10**8,
        moved=3 * 10**6,
    )
    spread = run(
        layer_sum_kernel,
        "sum_over_layer",
        scalars,
        [own_sum, *[shift(v, "layer", s) for s, v in zip(all_shifts, sums)]],
        [near((peers, chunk_rows, feat))],
        moved=10**6,
    )[0]
    late = [lax.ppermute(d_out, "layer", [(spans - s, 0)]) for s in all_shifts]
    gathered, layer_acts, *late = tie(exchange(spread), layer_acts, *late)
    gathered = gathered.reshape(feat, feat)
    other = sibling(gathered)
    act_grads = put_home(grads_buf, *early, (d_out, whole((rows, feat))), *late)
    out_square = (1, feat, feat)
    grad_self, grad_neigh = run(
        functools.partial(scale_kernel, scale),
        "scale_grads",
        scalars,
        [gathered, other],
        [(pltpu.HBM(out_square, F32), whole(out_square))] * 2,
        moved=3 * 10**6,
    )
    return (layer_acts, act_grads, grad_self, grad_neigh)


def solution(mesh):
    in_specs = (
        P(None, "node", None),
        P("layer", None, None),
        P("layer", None, None),
        P(),
        P(None, "node"),
        P(None, "node"),
        P(None, "node", None, None),
        P(None, "node", None, None, None, None),
        P(None, "node", None, None),
        P(None, "node", None),
    )
    out_specs = (
        P("layer", None, "node", None),
        P("layer", None, "node", None),
        P("layer", None, None),
        P("layer", None, None),
    )
    return jax.shard_map(body, mesh=mesh, in_specs=in_specs, out_specs=out_specs, check_vma=False)
```

```python
import functools

import jax
import jax.numpy as jnp
from jax import lax
from jax.experimental import pallas as pl
from jax.experimental.pallas import tpu as pltpu
from jax.sharding import PartitionSpec as P

BF = jnp.bfloat16
F32 = jnp.float32
NN = (((1,), (0,)), ((), ()))
NT = (((1,), (1,)), ((), ()))
TN = (((0,), (0,)), ((), ()))
FAR = pl.BlockSpec(memory_space=pltpu.HBM)
LOCAL = pl.BlockSpec(memory_space=pltpu.VMEM)
VMEM_BYTES = 16 * 1024 * 1024


def dot(a, b, dims=NN):
    return lax.dot_general(a, b, dims, preferred_element_type=F32)


def shift(value, axis, steps):
    count = lax.axis_size(axis)
    return lax.ppermute(value, axis, [(i, (i + steps) % count) for i in range(count)])


def sibling(value):
    count = lax.axis_size("node")
    return lax.ppermute(value, "node", [(i, i ^ 1) for i in range(count)])


def exchange(value):
    return lax.all_to_all(value, "node", split_axis=0, concat_axis=0, tiled=True)


def of_span(shape):
    return pl.BlockSpec((None, *shape), lambda i, ids, cols: (ids[0], *((0,) * len(shape))))


def whole(shape):
    return pl.BlockSpec(shape, lambda i, ids, cols: (0,) * len(shape))


def near(shape, dtype=BF):
    return pltpu.VMEM(shape, dtype), LOCAL


def far_block(shape, dtype=BF):
    return pltpu.HBM(shape, dtype), whole(shape)


def run(kernel, name, scalars, ins, outs, scratch=(), aliases=None, flops=0, moved=0):
    ins = [v if isinstance(v, tuple) else (v, LOCAL) for v in ins]
    arrays = [
        pltpu.with_memory_space_constraint(a, pltpu.VMEM if s is LOCAL else pltpu.HBM)
        for a, s in ins
    ]
    return pl.pallas_call(
        kernel,
        name=name,
        grid_spec=pltpu.PrefetchScalarGridSpec(
            num_scalar_prefetch=2,
            grid=(1,),
            in_specs=[s for _, s in ins],
            out_specs=[s for _, s in outs],
            scratch_shapes=list(scratch),
        ),
        out_shape=[o for o, _ in outs],
        input_output_aliases={} if aliases is None else {k + 2: v for k, v in aliases.items()},
        compiler_params=pltpu.CompilerParams(vmem_limit_bytes=VMEM_BYTES),
        cost_estimate=pl.CostEstimate(flops=flops, bytes_accessed=moved, transcendentals=0),
    )(*scalars, *arrays)


def tie(*values):
    return lax.optimization_barrier(values)


def weight_copies(layer, ids, w_refs, w_scr, sems, act):
    own_s, own_n, left, left_x, right, right_x, far, far_x = w_refs
    core = ids[1]
    pairs = [
        [(own_s, 0), (own_n, 1)],
        [(right, core), (right_x, 1 - core)],
        [(far, core), (far_x, 1 - core)],
        [(left, core), (left_x, 1 - core)],
    ]
    which = lax.rem(layer - ids[0] + 4, 4)
    for option, pair in enumerate(pairs):

        @pl.when(which == option)
        def _():
            for n, (ref, place) in enumerate(pair):
                act(pltpu.make_async_copy(ref, w_scr.at[place], sems.at[n]))


def start_weights(*args):
    weight_copies(*args, lambda copy: copy.start())


def wait_weights(*args):
    weight_copies(*args, lambda copy: copy.wait())


def side_by_side(vals_ref, r, degree):
    return jnp.concatenate([vals_ref[r, j] for j in range(degree)], axis=1)


def aggregate_rows(ids, cols, vals_ref, ext):
    tiles, degree, size = vals_ref.shape[0], vals_ref.shape[1], vals_ref.shape[2]
    parts = []
    for r in range(tiles):
        picked = jnp.concatenate(
            [ext[pl.ds(pl.multiple_of(cols[ids[0], r, j] * size, size), size), :] for j in range(degree)],
            axis=0,
        )
        parts.append(dot(side_by_side(vals_ref, r, degree), picked))
    return jnp.concatenate(parts, axis=0).astype(BF)


def spread_rows(ids, cols, vals_ref, d_agg, d_ext):
    tiles, degree, size = vals_ref.shape[0], vals_ref.shape[1], vals_ref.shape[2]
    d_ext[...] = jnp.zeros_like(d_ext)
    for r in range(tiles):
        pieces = dot(side_by_side(vals_ref, r, degree), d_agg[r * size : (r + 1) * size], TN)
        for j in range(degree):
            rows = pl.ds(pl.multiple_of(cols[ids[0], r, j] * size, size), size)
            d_ext[rows, :] += pieces[j * size : (j + 1) * size]


def to_slot(value_ref, layer, ids, buf_ref, sem):
    return pltpu.make_async_copy(value_ref, buf_ref.at[lax.rem(layer - ids[0] + 4, 4)], sem)


def sigmoid(v):
    return 1.0 / (1.0 + jnp.exp(-v))


def pre_kernel(ids, cols, h_ref, rows_ref, counts_ref, vals_ref, pick_ref, out_ref, h_out, vals_out, pick_far):
    slots, peers = rows_ref.shape
    total, node_rows = pick_ref.shape
    bits = slots.bit_length() - 1
    slot = lax.broadcasted_iota(jnp.int32, (total, peers), 0)
    owner = lax.broadcasted_iota(jnp.int32, (total, peers), 1)
    mine = lax.shift_right_logical(slot, bits) == owner
    wide = dot(mine.astype(F32).astype(BF), rows_ref[...].astype(F32).astype(BF), NT)
    slot_k = lax.broadcasted_iota(jnp.int32, (total, slots), 0) & (slots - 1)
    in_slot = slot_k == lax.broadcasted_iota(jnp.int32, (total, slots), 1)
    row = jnp.sum(jnp.where(in_slot, wide, 0.0), axis=1, keepdims=True)
    counts = jnp.broadcast_to(counts_ref[...].astype(F32), (total, peers))
    count = jnp.sum(jnp.where(mine, counts, 0.0), axis=1, keepdims=True)
    k = (lax.broadcasted_iota(jnp.int32, (total, 1), 0) & (slots - 1)).astype(F32)
    row = jnp.where(k < count, row, -1.0)
    place = lax.broadcasted_iota(jnp.int32, (total, node_rows), 1).astype(F32)
    pick = (place == row).astype(F32).astype(BF)
    pick_ref[...] = pick
    pick_far[...] = pick
    out_ref[...] = dot(pick, h_ref[...]).astype(BF)
    h_out[...] = h_ref[...]
    vals_out[...] = vals_ref[...]


def forward_math(ids, cols, h_ref, arr_ref, vals_ref, w_ref, ext, ready=None):
    rows = h_ref.shape[0]
    ext[0:rows, :] = h_ref[...]
    ext[rows : 2 * rows, :] = arr_ref[...]
    agg = aggregate_rows(ids, cols, vals_ref, ext)
    if ready is not None:
        ready()
    pre = dot(h_ref[...], w_ref[0]) + dot(agg, w_ref[1])
    sig = sigmoid(pre)
    return agg, pre, sig, (pre * sig).astype(BF)


def forward_kernel(layer, ids, cols, h_ref, arr_ref, vals_ref, pick_ref, *rest):
    w_refs, rest = rest[:8], rest[8:]
    first = layer == 0
    w_ref, rest = (rest[6], rest) if first else (rest[0], rest[2:])
    agg_ref, pre_ref, hid_ref, out_ref, buf_ref, next_ref = rest[:6]
    ext, buf_sem, sems = rest[-3:]
    ready = None
    if first:
        here = (layer, ids, w_refs, w_ref, sems.at[0])
        start_weights(*here)
        ready = lambda: wait_weights(*here)
    ahead = (layer + 1, ids, w_refs, next_ref, sems.at[1])
    start_weights(*ahead)
    agg, pre, _, hid = forward_math(ids, cols, h_ref, arr_ref, vals_ref, w_ref, ext, ready)
    hid_ref[...] = hid
    copy = to_slot(hid_ref, layer, ids, buf_ref, buf_sem)
    copy.start()
    out_ref[...] = dot(pick_ref[...], hid).astype(BF)
    agg_ref[...] = agg
    pre_ref[...] = pre
    copy.wait()
    wait_weights(*ahead)


def backward_math(ids, cols, d_pre, vals_ref, w_ref, d_ext):
    d_agg = dot(d_pre, w_ref[1], NT).astype(BF)
    spread_rows(ids, cols, vals_ref, d_agg, d_ext)
    return dot(d_pre, w_ref[0], NT)


def weight_partials(ids, h_ref, agg, d_pre, keep_ref, send_ref):
    on_rows = dot(h_ref[...], d_pre, TN).astype(BF)
    on_agg = dot(agg, d_pre, TN).astype(BF)

    @pl.when(ids[1] == 0)
    def _():
        keep_ref[...] = on_rows
        send_ref[...] = on_agg

    @pl.when(ids[1] != 0)
    def _():
        keep_ref[...] = on_agg
        send_ref[...] = on_rows


def top_kernel(layer, ids, cols, h_ref, arr_ref, vals_ref, wout_ref, lab_ref, mask_ref, w_ref, *rest):
    remote_ref, part_ref, keep_ref, send_ref, buf_ref, hid_ref, ext, d_ext, buf_sem = rest[1:]
    rows = h_ref.shape[0]
    agg, pre, sig, hid = forward_math(ids, cols, h_ref, arr_ref, vals_ref, w_ref, ext)
    hid_ref[...] = hid
    copy = to_slot(hid_ref, layer, ids, buf_ref, buf_sem)
    copy.start()
    logits = dot(wout_ref[...], hid, NT)
    expo = jnp.exp(logits)
    probs = expo / jnp.sum(expo, axis=0, keepdims=True)
    label = lab_ref[pl.ds(ids[0], 1), :]
    onehot = (label == lax.broadcasted_iota(jnp.int32, logits.shape, 0)).astype(F32)
    live = mask_ref[pl.ds(ids[0], 1), :].astype(F32)
    g_logits = (live * (probs - onehot)).astype(BF)
    d_out = dot(g_logits, wout_ref[...], TN).astype(BF)
    d_pre = (d_out.astype(F32) * (sig * (1.0 + pre * (1.0 - sig)))).astype(BF)
    back = backward_math(ids, cols, d_pre, vals_ref, w_ref, d_ext)
    remote_ref[...] = d_ext[rows : 2 * rows, :].astype(BF).reshape(remote_ref.shape)
    part_ref[...] = back + d_ext[0:rows, :]
    weight_partials(ids, h_ref, agg, d_pre, keep_ref, send_ref)
    copy.wait()


def chunk_sum(block):
    total = block[0:2].astype(F32)
    for n in range(2, block.shape[0], 2):
        total = total + block[n : n + 2].astype(F32)
    return total


def backward_kernel(layer, carry, ids, cols, ret_ref, part_in, pre_ref, h_ref, agg_ref, *rest):
    (vals_ref, pick_ref, w_ref), rest = rest[:3], rest[3:]
    if carry:
        keep_in, recv_in, rest = rest[0], rest[1], rest[2:]
    if layer < 2:
        rest = rest[1:]
    out_ref, part_ref, buf_ref, keep_ref, send_ref, *rest = rest
    if not layer:
        *rest, local, local_sem = rest
    *chunk, dout_ref, d_ext, buf_sem = rest
    rows, feat = part_in.shape
    peers = out_ref.shape[0]
    slots = rows // peers
    returned = ret_ref[:, 0:slots, :].reshape(rows, feat)
    d_out = (part_in[...] + dot(pick_ref[...], returned, TN)).astype(BF)
    dout_ref[...] = d_out
    copy = to_slot(dout_ref, layer + 1, ids, buf_ref, buf_sem)
    copy.start()
    pre = pre_ref[...]
    sig = sigmoid(pre)
    d_pre = (d_out.astype(F32) * (sig * (1.0 + pre * (1.0 - sig)))).astype(BF)
    back = backward_math(ids, cols, d_pre, vals_ref, w_ref, d_ext)
    target = out_ref if layer else local
    target[:, 0:slots, :] = d_ext[rows : 2 * rows, :].astype(BF).reshape(peers, slots, feat)
    if carry:
        put_carry(keep_in, recv_in, target, slots)
    if not layer:
        away = pltpu.make_async_copy(local, out_ref.at[:, pl.ds(0, local.shape[1]), :], local_sem)
        away.start()
    part_ref[...] = back + d_ext[0:rows, :]
    weight_partials(ids, h_ref, agg_ref[...], d_pre, keep_ref, send_ref)
    if chunk:
        chunk[0][...] = chunk_sum(ret_ref[:, slots:, :]).astype(BF)
    copy.wait()
    if not layer:
        away.wait()


def put_carry(keep_ref, recv_ref, out_ref, first):
    peers, feat = out_ref.shape[0], out_ref.shape[2]
    size = keep_ref.shape[0] // peers
    total = (keep_ref[...].astype(F32) + recv_ref[...].astype(F32)).astype(BF)
    out_ref[:, first : first + size, :] = total.reshape(peers, size, feat)


def join_kernel(ids, cols, keep_a, recv_a, keep_b, recv_b, buf_in, out_ref, local, sem):
    size = local.shape[1] // 2
    first = out_ref.shape[1] - 2 * size
    put_carry(keep_a, recv_a, local, 0)
    put_carry(keep_b, recv_b, local, size)
    copy = pltpu.make_async_copy(local, out_ref.at[:, pl.ds(first, 2 * size), :], sem)
    copy.start()
    copy.wait()


def chunk_kernel(ids, cols, ret_ref, c_3, out_ref):
    size = c_3.shape[1]
    slots = ret_ref.shape[1] - 3 * size
    out_ref[3] = c_3[...]
    for n, layer in enumerate((2, 1, 0)):
        first = slots + n * size
        out_ref[layer] = chunk_sum(ret_ref[:, first : first + size, :]).astype(BF)


def end_kernel(ids, cols, ret_ref, part_in, pick_ref, buf_in, buf_ref, dout_ref, buf_sem):
    rows, feat = part_in.shape
    returned = ret_ref[:, 0 : rows // ret_ref.shape[0], :].reshape(rows, feat)
    dout_ref[...] = (part_in[...] + dot(pick_ref[...], returned, TN)).astype(BF)
    copy = to_slot(dout_ref, 0, ids, buf_ref, buf_sem)
    copy.start()
    copy.wait()


def layer_sum_kernel(ids, cols, sums_ref, out_ref):
    total = sums_ref[0].astype(F32)
    for span in range(1, sums_ref.shape[0]):
        total = total + sums_ref[span].astype(F32)
    total = total.astype(BF)
    for n in range(0, out_ref.shape[0], 2):
        out_ref[n : n + 2] = total


def scale_kernel(scale, ids, cols, mine_ref, other_ref, self_ref, neigh_ref):
    mine = mine_ref[...].astype(F32) * scale
    other = other_ref[...].astype(F32) * scale

    @pl.when(ids[1] == 0)
    def _():
        self_ref[0] = mine
        neigh_ref[0] = other

    @pl.when(ids[1] != 0)
    def _():
        self_ref[0] = other
        neigh_ref[0] = mine


def home_kernel(ids, cols, *refs):
    pieces, out_ref = refs[:-1], refs[-1]
    for s, piece in enumerate(pieces):
        out_ref[0, lax.rem(ids[0] + 4 - s, 4)] = piece[...]


def body(
    features,
    w_self,
    w_neigh,
    w_out,
    labels,
    train_mask,
    tile_cols,
    tile_vals,
    send_rows,
    send_counts,
):
    home = lax.axis_index("layer")
    node = lax.axis_index("node")
    core = lax.rem(node, 2)
    spans, rows, feat = features.shape
    peers, slots = send_rows.shape[2], send_rows.shape[3]
    tiles, degree, size = tile_vals.shape[2], tile_vals.shape[3], tile_vals.shape[4]
    scale = 1.0 / (spans * rows * peers)
    scalars = (jnp.stack([home, core]).astype(jnp.int32), tile_cols.reshape(spans, tiles, degree))
    act, wide, square = near((rows, feat)), near((rows, feat), F32), near((feat, feat))
    ext_scratch = pltpu.VMEM((2 * rows, feat), BF)
    d_ext_scratch = pltpu.VMEM((2 * rows, feat), F32)
    all_shifts = range(1, spans)

    mine = jnp.where(core == 0, w_self[0], w_neigh[0])
    left, right, far = (shift(mine, "layer", s) for s in (1, -1, 2))
    pick, outgoing, features_0, vals, pick_far = run(
        pre_kernel,
        "gather_rows",
        scalars,
        [
            (features, of_span((rows, feat))),
            (send_rows.reshape(spans, peers, slots).swapaxes(1, 2), of_span((slots, peers))),
            (send_counts.reshape(spans, 1, peers), of_span((1, peers))),
            (
                tile_vals.reshape(spans, tiles, degree, size, size),
                of_span((tiles, degree, size, size)),
            ),
        ],
        [
            near((peers * slots, rows)),
            act,
            act,
            near((tiles, degree, size, size)),
            far_block((peers * slots, rows)),
        ],
        flops=10**8,
        moved=10**6,
    )
    arrived = exchange(outgoing.reshape(peers, slots, feat))
    arrived, left, right, far = tie(arrived, left, right, far)
    sources = [(w_self[0], FAR), (w_neigh[0], FAR), left, sibling(left), right, sibling(right)]
    sources += [far, sibling(far)]
    weight = near((2, feat, feat))

    hidden, aggs, pres, weights = [features_0], [], [], []
    top = spans - 1
    stack = (pltpu.HBM((spans, rows, feat), BF), FAR)
    buf_sem = pltpu.SemaphoreType.DMA
    acts_buf = None
    for layer in range(top):
        ins = [hidden[layer], arrived.reshape(rows, feat), vals, pick, *sources]
        if layer:
            ins += [weights[layer], (acts_buf, FAR)]
        agg, pre, hid, outgoing, acts_buf, *arranged = run(
            functools.partial(forward_kernel, layer),
            f"layer_forward_{layer}",
            scalars,
            ins,
            [act, wide, act, act, stack] + [weight] * (2 if layer == 0 else 1),
            [ext_scratch, buf_sem, pltpu.SemaphoreType.DMA((2, 2))],
            {len(ins) - 1: 4} if layer else None,
            flops=6 * 10**8,
            moved=4 * 10**6,
        )
        hidden.append(hid)
        aggs.append(agg)
        pres.append(pre)
        weights += arranged[::-1]
        arrived = exchange(outgoing.reshape(peers, slots, feat))

    ins = [
        hidden[top],
        arrived.reshape(rows, feat),
        vals,
        w_out.T,
        labels,
        train_mask,
        weights[top],
        (acts_buf, FAR),
    ]
    remote, part, keep, send, acts_buf = run(
        functools.partial(top_kernel, top),
        "top_layer",
        scalars,
        ins,
        [near((peers, slots, feat)), wide, square, square, stack],
        [
            pltpu.VMEM((rows, feat), BF),
            ext_scratch,
            d_ext_scratch,
            buf_sem,
        ],
        {len(ins) - 1: 4},
        flops=10**9,
        moved=5 * 10**6,
    )

    def travel(buf):
        return [shift(buf[s], "layer", s) for s in all_shifts]

    def put_home(buf, *pieces):
        block = pl.BlockSpec((None, rows, feat), lambda i, ids, cols: (0, 0, 0))
        shape = (1, spans, rows, feat)
        return run(
            home_kernel,
            "put_home",
            scalars,
            [(buf, block), *pieces],
            [far_block(shape)],
            moved=2 * 10**6,
        )[0]

    chunk_rows = feat // peers
    pairs, grads_buf = [], None
    for layer in range(top - 1, -1, -1):
        returned, send = tie(exchange(remote), send)
        pairs.append((keep, sibling(send)))
        carry = layer < top - 1
        width = slots + chunk_rows * (carry + 2 * (layer == 0))
        ins = [
            returned,
            part,
            pres[layer],
            hidden[layer],
            aggs[layer],
            vals,
            pick,
            weights[layer],
        ]
        if carry:
            ins += pairs[-2]
        aliases = None
        if grads_buf is not None:
            ins.append((grads_buf, FAR))
            aliases = {len(ins) - 1: 2}
        last = far_block if layer == 0 else near
        operand = near((peers, width, feat))
        scratch = [pltpu.VMEM((rows, feat), BF), d_ext_scratch, buf_sem]
        if layer == 0:
            operand = (pltpu.HBM((peers, width, feat), BF), FAR)
            scratch += [pltpu.VMEM((peers, slots + chunk_rows, feat), BF), buf_sem]
        outs = [operand, last((rows, feat), F32), stack, square, square]
        if layer == 0:
            outs.append(far_block((2, chunk_rows, feat)))
        remote, part, grads_buf, keep, send, *c_3 = run(
            functools.partial(backward_kernel, layer, carry),
            f"layer_backward_{layer}",
            scalars,
            ins,
            outs,
            scratch,
            aliases,
            flops=10**9,
            moved=5 * 10**6,
        )
        if layer:
            remote, recv = tie(remote, pairs[-1][1])
            pairs[-1] = (pairs[-1][0], recv)

    joined = run(
        join_kernel,
        "join_rows",
        scalars,
        [*pairs[-1], keep, sibling(send), (remote, FAR)],
        [(pltpu.HBM((peers, slots + 3 * chunk_rows, feat), BF), FAR)],
        [pltpu.VMEM((peers, 2 * chunk_rows, feat), BF), buf_sem],
        aliases={4: 0},
        moved=3 * 10**6,
    )[0]
    joined, acts_buf = tie(joined, acts_buf)
    acts = travel(acts_buf)
    returned, *acts = tie(exchange(joined), *acts)
    sums = run(
        chunk_kernel,
        "sum_chunks",
        scalars,
        [returned, (c_3[0], whole(c_3[0].shape))],
        [far_block((spans, 2, chunk_rows, feat))],
        moved=10**6,
    )[0]
    sums = lax.all_to_all(sums, "layer", split_axis=0, concat_axis=0, tiled=True)
    grads_buf = run(
        end_kernel,
        "input_grads",
        scalars,
        [
            returned,
            (part, whole((rows, feat))),
            (pick_far, whole(pick_far.shape)),
            (grads_buf, FAR),
        ],
        [stack],
        [pltpu.VMEM((rows, feat), BF), buf_sem],
        {3: 0},
        flops=10**8,
        moved=10**6,
    )[0]
    spread = run(
        layer_sum_kernel,
        "sum_over_layer",
        scalars,
        [sums],
        [far_block((peers, chunk_rows, feat))],
        moved=10**6,
    )[0]
    layer_acts = put_home(acts_buf, *acts)
    grads = travel(grads_buf)
    gathered, layer_acts, *grads = tie(exchange(spread), layer_acts, *grads)
    gathered = gathered.reshape(feat, feat)
    other = sibling(gathered)
    act_grads = put_home(grads_buf, *grads)
    out_square = (1, feat, feat)
    grad_self, grad_neigh = run(
        functools.partial(scale_kernel, scale),
        "scale_grads",
        scalars,
        [gathered, other],
        [(pltpu.HBM(out_square, F32), whole(out_square))] * 2,
        moved=3 * 10**6,
    )
    return (layer_acts, act_grads, grad_self, grad_neigh)


def solution(mesh):
    in_specs = (
        P(None, "node", None),
        P("layer", None, None),
        P("layer", None, None),
        P(),
        P(None, "node"),
        P(None, "node"),
        P(None, "node", None, None),
        P(None, "node", None, None, None, None),
        P(None, "node", None, None),
        P(None, "node", None),
    )
    out_specs = (
        P("layer", None, "node", None),
        P("layer", None, "node", None),
        P("layer", None, None),
        P("layer", None, None),
    )
    return jax.shard_map(body, mesh=mesh, in_specs=in_specs, out_specs=out_specs, check_vma=False)
```

```python
import functools

import jax
import jax.numpy as jnp
from jax import lax
from jax.experimental import pallas as pl
from jax.experimental.pallas import tpu as pltpu
from jax.sharding import PartitionSpec as P

BF = jnp.bfloat16
F32 = jnp.float32
NN = (((1,), (0,)), ((), ()))
NT = (((1,), (1,)), ((), ()))
TN = (((0,), (0,)), ((), ()))
FAR = pl.BlockSpec(memory_space=pltpu.HBM)
LOCAL = pl.BlockSpec(memory_space=pltpu.VMEM)
VMEM_BYTES = 16 * 1024 * 1024


def dot(a, b, dims=NN):
    return lax.dot_general(a, b, dims, preferred_element_type=F32)


def shift(value, axis, steps):
    count = lax.axis_size(axis)
    return lax.ppermute(value, axis, [(i, (i + steps) % count) for i in range(count)])


def sibling(value):
    count = lax.axis_size("node")
    return lax.ppermute(value, "node", [(i, i ^ 1) for i in range(count)])


def exchange(value):
    return lax.all_to_all(value, "node", split_axis=0, concat_axis=0, tiled=True)


def of_span(shape):
    return pl.BlockSpec((None, *shape), lambda i, ids, cols: (ids[0], *((0,) * len(shape))))


def whole(shape):
    return pl.BlockSpec(shape, lambda i, ids, cols: (0,) * len(shape))


def near(shape, dtype=BF):
    return pltpu.VMEM(shape, dtype), LOCAL


def far_block(shape, dtype=BF):
    return pltpu.HBM(shape, dtype), whole(shape)


def run(kernel, name, scalars, ins, outs, scratch=(), aliases=None, flops=0, moved=0):
    ins = [v if isinstance(v, tuple) else (v, LOCAL) for v in ins]
    arrays = [
        pltpu.with_memory_space_constraint(a, pltpu.VMEM if s is LOCAL else pltpu.HBM)
        for a, s in ins
    ]
    return pl.pallas_call(
        kernel,
        name=name,
        grid_spec=pltpu.PrefetchScalarGridSpec(
            num_scalar_prefetch=2,
            grid=(1,),
            in_specs=[s for _, s in ins],
            out_specs=[s for _, s in outs],
            scratch_shapes=list(scratch),
        ),
        out_shape=[o for o, _ in outs],
        input_output_aliases={} if aliases is None else {k + 2: v for k, v in aliases.items()},
        compiler_params=pltpu.CompilerParams(vmem_limit_bytes=VMEM_BYTES),
        cost_estimate=pl.CostEstimate(flops=flops, bytes_accessed=moved, transcendentals=0),
    )(*scalars, *arrays)


def tie(*values):
    return lax.optimization_barrier(values)


def weight_copies(layer, ids, w_refs, w_scr, sems, act):
    own_s, own_n, left, left_x, right, right_x, far, far_x = w_refs
    core = ids[1]
    pairs = [
        [(own_s, 0), (own_n, 1)],
        [(right, core), (right_x, 1 - core)],
        [(far, core), (far_x, 1 - core)],
        [(left, core), (left_x, 1 - core)],
    ]
    which = lax.rem(layer - ids[0] + 4, 4)
    for option, pair in enumerate(pairs):

        @pl.when(which == option)
        def _():
            for n, (ref, place) in enumerate(pair):
                act(pltpu.make_async_copy(ref, w_scr.at[place], sems.at[n]))


def start_weights(*args):
    weight_copies(*args, lambda copy: copy.start())


def wait_weights(*args):
    weight_copies(*args, lambda copy: copy.wait())


def side_by_side(vals_ref, r, degree):
    return jnp.concatenate([vals_ref[r, j] for j in range(degree)], axis=1)


def aggregate_rows(ids, cols, vals_ref, ext):
    tiles, degree, size = vals_ref.shape[0], vals_ref.shape[1], vals_ref.shape[2]
    parts = []
    for r in range(tiles):
        picked = jnp.concatenate(
            [ext[pl.ds(pl.multiple_of(cols[ids[0], r, j] * size, size), size), :] for j in range(degree)],
            axis=0,
        )
        parts.append(dot(side_by_side(vals_ref, r, degree), picked))
    return jnp.concatenate(parts, axis=0).astype(BF)


def spread_rows(ids, cols, vals_ref, d_agg, d_ext):
    tiles, degree, size = vals_ref.shape[0], vals_ref.shape[1], vals_ref.shape[2]
    d_ext[...] = jnp.zeros_like(d_ext)
    for r in range(tiles):
        pieces = dot(side_by_side(vals_ref, r, degree), d_agg[r * size : (r + 1) * size], TN)
        for j in range(degree):
            rows = pl.ds(pl.multiple_of(cols[ids[0], r, j] * size, size), size)
            d_ext[rows, :] += pieces[j * size : (j + 1) * size]


def to_slot(value_ref, layer, ids, buf_ref, sem):
    return pltpu.make_async_copy(value_ref, buf_ref.at[lax.rem(layer - ids[0] + 4, 4)], sem)


def sigmoid(v):
    return 1.0 / (1.0 + jnp.exp(-v))


def pre_kernel(ids, cols, h_ref, rows_ref, counts_ref, vals_ref, pick_ref, out_ref, h_out, vals_out, pick_far):
    slots, peers = rows_ref.shape
    total, node_rows = pick_ref.shape
    bits = slots.bit_length() - 1
    slot = lax.broadcasted_iota(jnp.int32, (total, peers), 0)
    owner = lax.broadcasted_iota(jnp.int32, (total, peers), 1)
    mine = lax.shift_right_logical(slot, bits) == owner
    wide = dot(mine.astype(F32).astype(BF), rows_ref[...].astype(F32).astype(BF), NT)
    slot_k = lax.broadcasted_iota(jnp.int32, (total, slots), 0) & (slots - 1)
    in_slot = slot_k == lax.broadcasted_iota(jnp.int32, (total, slots), 1)
    row = jnp.sum(jnp.where(in_slot, wide, 0.0), axis=1, keepdims=True)
    counts = jnp.broadcast_to(counts_ref[...].astype(F32), (total, peers))
    count = jnp.sum(jnp.where(mine, counts, 0.0), axis=1, keepdims=True)
    k = (lax.broadcasted_iota(jnp.int32, (total, 1), 0) & (slots - 1)).astype(F32)
    row = jnp.where(k < count, row, -1.0)
    place = lax.broadcasted_iota(jnp.int32, (total, node_rows), 1).astype(F32)
    pick = (place == row).astype(F32).astype(BF)
    pick_ref[...] = pick
    pick_far[...] = pick
    out_ref[...] = dot(pick, h_ref[...]).astype(BF)
    h_out[...] = h_ref[...]
    vals_out[...] = vals_ref[...]


def forward_math(ids, cols, h_ref, arr_ref, vals_ref, w_ref, ext, ready=None):
    rows = h_ref.shape[0]
    ext[0:rows, :] = h_ref[...]
    ext[rows : 2 * rows, :] = arr_ref[...]
    agg = aggregate_rows(ids, cols, vals_ref, ext)
    if ready is not None:
        ready()
    pre = dot(h_ref[...], w_ref[0]) + dot(agg, w_ref[1])
    sig = sigmoid(pre)
    return agg, pre, sig, (pre * sig).astype(BF)


def forward_kernel(layer, ids, cols, h_ref, arr_ref, vals_ref, pick_ref, *rest):
    w_refs, rest = rest[:8], rest[8:]
    first = layer == 0
    w_ref, rest = (rest[6], rest) if first else (rest[0], rest[2:])
    agg_ref, pre_ref, hid_ref, out_ref, buf_ref, next_ref = rest[:6]
    ext, buf_sem, sems = rest[-3:]
    ready = None
    if first:
        here = (layer, ids, w_refs, w_ref, sems.at[0])
        start_weights(*here)
        ready = lambda: wait_weights(*here)
    ahead = (layer + 1, ids, w_refs, next_ref, sems.at[1])
    start_weights(*ahead)
    agg, pre, _, hid = forward_math(ids, cols, h_ref, arr_ref, vals_ref, w_ref, ext, ready)
    hid_ref[...] = hid
    copy = to_slot(hid_ref, layer, ids, buf_ref, buf_sem)
    copy.start()
    out_ref[...] = dot(pick_ref[...], hid).astype(BF)
    agg_ref[...] = agg
    pre_ref[...] = pre
    copy.wait()
    wait_weights(*ahead)


def backward_math(ids, cols, d_pre, vals_ref, w_ref, d_ext):
    d_agg = dot(d_pre, w_ref[1], NT).astype(BF)
    spread_rows(ids, cols, vals_ref, d_agg, d_ext)
    return dot(d_pre, w_ref[0], NT)


def weight_partials(ids, h_ref, agg, d_pre, keep_ref, send_ref):
    on_rows = dot(h_ref[...], d_pre, TN).astype(BF)
    on_agg = dot(agg, d_pre, TN).astype(BF)

    @pl.when(ids[1] == 0)
    def _():
        keep_ref[...] = on_rows
        send_ref[...] = on_agg

    @pl.when(ids[1] != 0)
    def _():
        keep_ref[...] = on_agg
        send_ref[...] = on_rows


def top_kernel(layer, ids, cols, h_ref, arr_ref, vals_ref, wout_ref, lab_ref, mask_ref, w_ref, *rest):
    remote_ref, part_ref, keep_ref, send_ref, buf_ref, hid_ref, ext, d_ext, buf_sem = rest[1:]
    rows = h_ref.shape[0]
    agg, pre, sig, hid = forward_math(ids, cols, h_ref, arr_ref, vals_ref, w_ref, ext)
    hid_ref[...] = hid
    copy = to_slot(hid_ref, layer, ids, buf_ref, buf_sem)
    copy.start()
    logits = dot(wout_ref[...], hid, NT)
    expo = jnp.exp(logits)
    probs = expo / jnp.sum(expo, axis=0, keepdims=True)
    label = lab_ref[pl.ds(ids[0], 1), :]
    onehot = (label == lax.broadcasted_iota(jnp.int32, logits.shape, 0)).astype(F32)
    live = mask_ref[pl.ds(ids[0], 1), :].astype(F32)
    g_logits = (live * (probs - onehot)).astype(BF)
    d_out = dot(g_logits, wout_ref[...], TN).astype(BF)
    d_pre = (d_out.astype(F32) * (sig * (1.0 + pre * (1.0 - sig)))).astype(BF)
    back = backward_math(ids, cols, d_pre, vals_ref, w_ref, d_ext)
    remote_ref[...] = d_ext[rows : 2 * rows, :].astype(BF).reshape(remote_ref.shape)
    part_ref[...] = back + d_ext[0:rows, :]
    weight_partials(ids, h_ref, agg, d_pre, keep_ref, send_ref)
    copy.wait()


def chunk_sum(block):
    total = block[0:2].astype(F32)
    for n in range(2, block.shape[0], 2):
        total = total + block[n : n + 2].astype(F32)
    return total


def slope_math(ids, layer, ret_ref, part_in, pre_ref, pick_ref, dout_ref, buf_ref, buf_sem):
    rows, feat = part_in.shape
    returned = ret_ref[:, 0 : rows // ret_ref.shape[0], :].reshape(rows, feat)
    d_out = (part_in[...] + dot(pick_ref[...], returned, TN)).astype(BF)
    dout_ref[...] = d_out
    copy = to_slot(dout_ref, layer + 1, ids, buf_ref, buf_sem)
    copy.start()
    pre = pre_ref[...]
    sig = sigmoid(pre)
    return (d_out.astype(F32) * (sig * (1.0 + pre * (1.0 - sig)))).astype(BF), copy


def backward_kernel(layer, carry, ids, cols, ret_ref, part_in, pre_ref, h_ref, agg_ref, *rest):
    (vals_ref, pick_ref, w_ref), rest = rest[:3], rest[3:]
    if carry:
        keep_in, recv_in, rest = rest[0], rest[1], rest[3:]
    out_ref, part_ref, buf_ref, keep_ref, send_ref, dout_ref, d_ext, buf_sem = rest
    rows, feat = part_in.shape
    d_pre, copy = slope_math(
        ids, layer, ret_ref, part_in, pre_ref, pick_ref, dout_ref, buf_ref, buf_sem
    )
    back = backward_math(ids, cols, d_pre, vals_ref, w_ref, d_ext)
    peers, slots = out_ref.shape[0], rows // out_ref.shape[0]
    out_ref[:, 0:slots, :] = d_ext[rows : 2 * rows, :].astype(BF).reshape(peers, slots, feat)
    if carry:
        put_carry(keep_in, recv_in, out_ref, slots)
    part_ref[...] = back + d_ext[0:rows, :]
    weight_partials(ids, h_ref, agg_ref[...], d_pre, keep_ref, send_ref)
    copy.wait()


def last_slope_kernel(
    ids, cols, ret_ref, part_in, pre_ref, h_ref, agg_ref, pick_ref, buf_in,
    dpre_ref, buf_ref, keep_ref, send_ref, chunk_ref, dout_ref, buf_sem,
):
    d_pre, copy = slope_math(
        ids, 0, ret_ref, part_in, pre_ref, pick_ref, dout_ref, buf_ref, buf_sem
    )
    dpre_ref[...] = d_pre
    weight_partials(ids, h_ref, agg_ref[...], d_pre, keep_ref, send_ref)
    slots = part_in.shape[0] // ret_ref.shape[0]
    chunk_ref[...] = chunk_sum(ret_ref[:, slots:, :]).astype(BF)
    copy.wait()


def last_spread_kernel(
    ids, cols, dpre_ref, vals_ref, w_ref, keep_a, recv_a, keep_b, recv_b,
    out_ref, part_ref, d_ext, local, sem,
):
    rows, feat = dpre_ref.shape
    peers, used = local.shape[0], local.shape[1]
    slots, size = rows // peers, keep_a.shape[0] // peers
    put_carry(keep_a, recv_a, local, slots)
    put_carry(keep_b, recv_b, local, slots + size)
    back = backward_math(ids, cols, dpre_ref[...], vals_ref, w_ref, d_ext)
    local[:, 0:slots, :] = d_ext[rows : 2 * rows, :].astype(BF).reshape(peers, slots, feat)
    away = pltpu.make_async_copy(local, out_ref.at[:, pl.ds(0, used), :], sem)
    away.start()
    part_ref[...] = back + d_ext[0:rows, :]
    away.wait()


def put_carry(keep_ref, recv_ref, out_ref, first):
    peers, feat = out_ref.shape[0], out_ref.shape[2]
    size = keep_ref.shape[0] // peers
    total = (keep_ref[...].astype(F32) + recv_ref[...].astype(F32)).astype(BF)
    out_ref[:, first : first + size, :] = total.reshape(peers, size, feat)


def join_kernel(ids, cols, keep_ref, recv_ref, buf_in, out_ref, local, sem):
    size = local.shape[1]
    put_carry(keep_ref, recv_ref, local, 0)
    first = out_ref.shape[1] - size
    copy = pltpu.make_async_copy(local, out_ref.at[:, pl.ds(first, size), :], sem)
    copy.start()
    copy.wait()


def chunk_kernel(ids, cols, ret_ref, c_3, out_ref):
    size = c_3.shape[1]
    slots = ret_ref.shape[1] - 3 * size
    out_ref[3] = c_3[...]
    for n, layer in enumerate((2, 1, 0)):
        first = slots + n * size
        out_ref[layer] = chunk_sum(ret_ref[:, first : first + size, :]).astype(BF)


def end_kernel(ids, cols, ret_ref, part_in, pick_ref, buf_in, buf_ref, dout_ref, buf_sem):
    rows, feat = part_in.shape
    returned = ret_ref[:, 0 : rows // ret_ref.shape[0], :].reshape(rows, feat)
    dout_ref[...] = (part_in[...] + dot(pick_ref[...], returned, TN)).astype(BF)
    copy = to_slot(dout_ref, 0, ids, buf_ref, buf_sem)
    copy.start()
    copy.wait()


def layer_sum_kernel(ids, cols, sums_ref, out_ref):
    total = sums_ref[0].astype(F32)
    for span in range(1, sums_ref.shape[0]):
        total = total + sums_ref[span].astype(F32)
    total = total.astype(BF)
    for n in range(0, out_ref.shape[0], 2):
        out_ref[n : n + 2] = total


def final_kernel(scale, ids, cols, mine_ref, other_ref, own, one, two, three, late, home_ref, self_ref, neigh_ref):
    home_kernel(ids, cols, own, one, two, three, home_ref)

    @pl.when(ids[0] == 0)
    def _():
        home_ref[0, 2] = late[...]

    mine = mine_ref[...].astype(F32) * scale
    other = other_ref[...].astype(F32) * scale

    @pl.when(ids[1] == 0)
    def _():
        self_ref[0] = mine
        neigh_ref[0] = other

    @pl.when(ids[1] != 0)
    def _():
        self_ref[0] = other
        neigh_ref[0] = mine


def home_kernel(ids, cols, *refs):
    pieces, out_ref = refs[:-1], refs[-1]
    for s, piece in enumerate(pieces):
        out_ref[0, lax.rem(ids[0] + 4 - s, 4)] = piece[...]


def body(
    features,
    w_self,
    w_neigh,
    w_out,
    labels,
    train_mask,
    tile_cols,
    tile_vals,
    send_rows,
    send_counts,
):
    home = lax.axis_index("layer")
    node = lax.axis_index("node")
    core = lax.rem(node, 2)
    spans, rows, feat = features.shape
    peers, slots = send_rows.shape[2], send_rows.shape[3]
    tiles, degree, size = tile_vals.shape[2], tile_vals.shape[3], tile_vals.shape[4]
    scale = 1.0 / (spans * rows * peers)
    scalars = (jnp.stack([home, core]).astype(jnp.int32), tile_cols.reshape(spans, tiles, degree))
    act, wide, square = near((rows, feat)), near((rows, feat), F32), near((feat, feat))
    ext_scratch = pltpu.VMEM((2 * rows, feat), BF)
    d_ext_scratch = pltpu.VMEM((2 * rows, feat), F32)
    all_shifts = range(1, spans)

    mine = jnp.where(core == 0, w_self[0], w_neigh[0])
    left, right, far = (shift(mine, "layer", s) for s in (1, -1, 2))
    pick, outgoing, features_0, vals, pick_far = run(
        pre_kernel,
        "gather_rows",
        scalars,
        [
            (features, of_span((rows, feat))),
            (send_rows.reshape(spans, peers, slots).swapaxes(1, 2), of_span((slots, peers))),
            (send_counts.reshape(spans, 1, peers), of_span((1, peers))),
            (
                tile_vals.reshape(spans, tiles, degree, size, size),
                of_span((tiles, degree, size, size)),
            ),
        ],
        [
            near((peers * slots, rows)),
            act,
            act,
            near((tiles, degree, size, size)),
            far_block((peers * slots, rows)),
        ],
        flops=10**8,
        moved=10**6,
    )
    arrived = exchange(outgoing.reshape(peers, slots, feat))
    arrived, left, right, far = tie(arrived, left, right, far)
    sources = [(w_self[0], FAR), (w_neigh[0], FAR), left, sibling(left), right, sibling(right)]
    sources += [far, sibling(far)]
    weight = near((2, feat, feat))

    hidden, aggs, pres, weights = [features_0], [], [], []
    top = spans - 1
    stack = (pltpu.HBM((spans, rows, feat), BF), FAR)
    buf_sem = pltpu.SemaphoreType.DMA
    acts_buf = None
    for layer in range(top):
        ins = [hidden[layer], arrived.reshape(rows, feat), vals, pick, *sources]
        if layer:
            ins += [weights[layer], (acts_buf, FAR)]
        agg, pre, hid, outgoing, acts_buf, *arranged = run(
            functools.partial(forward_kernel, layer),
            f"layer_forward_{layer}",
            scalars,
            ins,
            [act, wide, act, act, stack] + [weight] * (2 if layer == 0 else 1),
            [ext_scratch, buf_sem, pltpu.SemaphoreType.DMA((2, 2))],
            {len(ins) - 1: 4} if layer else None,
            flops=6 * 10**8,
            moved=4 * 10**6,
        )
        hidden.append(hid)
        aggs.append(agg)
        pres.append(pre)
        weights += arranged[::-1]
        arrived = exchange(outgoing.reshape(peers, slots, feat))

    ins = [
        hidden[top],
        arrived.reshape(rows, feat),
        vals,
        w_out.T,
        labels,
        train_mask,
        weights[top],
        (acts_buf, FAR),
    ]
    remote, part, keep, send, acts_buf = run(
        functools.partial(top_kernel, top),
        "top_layer",
        scalars,
        ins,
        [near((peers, slots, feat)), wide, square, square, stack],
        [
            pltpu.VMEM((rows, feat), BF),
            ext_scratch,
            d_ext_scratch,
            buf_sem,
        ],
        {len(ins) - 1: 4},
        flops=10**9,
        moved=5 * 10**6,
    )

    def travel(buf):
        return [shift(buf[s], "layer", s) for s in all_shifts]

    def put_home(buf, *pieces):
        block = pl.BlockSpec((None, rows, feat), lambda i, ids, cols: (0, 0, 0))
        shape = (1, spans, rows, feat)
        return run(
            home_kernel,
            "put_home",
            scalars,
            [(buf, block), *pieces],
            [far_block(shape)],
            moved=2 * 10**6,
        )[0]

    chunk_rows = feat // peers
    pairs, grads_buf = [], None
    for layer in range(top - 1, 0, -1):
        returned, send = tie(exchange(remote), send)
        pairs.append((keep, sibling(send)))
        carry = layer < top - 1
        width = slots + chunk_rows * carry
        ins = [
            returned,
            part,
            pres[layer],
            hidden[layer],
            aggs[layer],
            vals,
            pick,
            weights[layer],
        ]
        aliases = None
        if carry:
            ins += [*pairs[-2], (grads_buf, FAR)]
            aliases = {len(ins) - 1: 2}
        remote, part, grads_buf, keep, send = run(
            functools.partial(backward_kernel, layer, carry),
            f"layer_backward_{layer}",
            scalars,
            ins,
            [near((peers, width, feat)), wide, stack, square, square],
            [pltpu.VMEM((rows, feat), BF), d_ext_scratch, buf_sem],
            aliases,
            flops=10**9,
            moved=5 * 10**6,
        )
        remote, recv = tie(remote, pairs[-1][1])
        pairs[-1] = (pairs[-1][0], recv)

    returned, send = tie(exchange(remote), send)
    recv_1, keep_1 = sibling(send), keep
    d_pre, grads_buf, keep, send, c_3 = run(
        last_slope_kernel,
        "last_slope",
        scalars,
        [returned, part, pres[0], hidden[0], aggs[0], pick, (grads_buf, FAR)],
        [act, stack, square, square, far_block((2, chunk_rows, feat))],
        [pltpu.VMEM((rows, feat), BF), buf_sem],
        {6: 1},
        flops=4 * 10**8,
        moved=3 * 10**6,
    )
    d_pre, recv_1, send = tie(d_pre, recv_1, send)
    recv = sibling(send)
    width = slots + 3 * chunk_rows
    operand = (pltpu.HBM((peers, width, feat), BF), FAR)
    remote, part = run(
        last_spread_kernel,
        "last_spread",
        scalars,
        [d_pre, vals, weights[0], *pairs[-1], keep_1, recv_1],
        [operand, far_block((rows, feat), F32)],
        [d_ext_scratch, pltpu.VMEM((peers, width - chunk_rows, feat), BF), buf_sem],
        flops=5 * 10**8,
        moved=4 * 10**6,
    )
    remote, recv = tie(remote, recv)
    joined = run(
        join_kernel,
        "join_rows",
        scalars,
        [keep, recv, (remote, FAR)],
        [operand],
        [pltpu.VMEM((peers, chunk_rows, feat), BF), buf_sem],
        aliases={2: 0},
        moved=2 * 10**6,
    )[0]
    joined, acts_buf, grads_buf = tie(joined, acts_buf, grads_buf)
    acts = travel(acts_buf)
    early = lax.ppermute(grads_buf[2], "layer", [(0, 2), (1, 3), (3, 1)])
    returned, early, *acts = tie(exchange(joined), early, *acts)
    sums = run(
        chunk_kernel,
        "sum_chunks",
        scalars,
        [returned, (c_3, whole(c_3.shape))],
        [far_block((spans, 2, chunk_rows, feat))],
        moved=10**6,
    )[0]
    sums = lax.all_to_all(sums, "layer", split_axis=0, concat_axis=0, tiled=True)
    grads_buf, d_out = run(
        end_kernel,
        "input_grads",
        scalars,
        [
            returned,
            (part, whole((rows, feat))),
            (pick_far, whole(pick_far.shape)),
            (grads_buf, FAR),
        ],
        [stack, far_block((rows, feat))],
        [buf_sem],
        {3: 0},
        flops=10**8,
        moved=10**6,
    )
    sums, grads_buf, d_out = tie(sums, grads_buf, d_out)
    spread = run(
        layer_sum_kernel,
        "sum_over_layer",
        scalars,
        [sums],
        [far_block((peers, chunk_rows, feat))],
        moved=10**6,
    )[0]
    layer_acts = put_home(acts_buf, *acts)
    grads = [shift(grads_buf[s], "layer", s) for s in (1, 3)]
    late = lax.ppermute(d_out, "layer", [(2, 0)])
    gathered, layer_acts, late, *grads = tie(exchange(spread), layer_acts, late, *grads)
    gathered = gathered.reshape(feat, feat)
    out_square, shape = (1, feat, feat), (1, spans, rows, feat)
    act_grads, grad_self, grad_neigh = run(
        functools.partial(final_kernel, scale),
        "final_outputs",
        scalars,
        [
            gathered,
            sibling(gathered),
            (grads_buf, pl.BlockSpec((None, rows, feat), lambda i, ids, cols: (0, 0, 0))),
            grads[0],
            early,
            grads[1],
            late,
        ],
        [far_block(shape), far_block(out_square, F32), far_block(out_square, F32)],
        moved=6 * 10**6,
    )
    return (layer_acts, act_grads, grad_self, grad_neigh)


def solution(mesh):
    in_specs = (
        P(None, "node", None),
        P("layer", None, None),
        P("layer", None, None),
        P(),
        P(None, "node"),
        P(None, "node"),
        P(None, "node", None, None),
        P(None, "node", None, None, None, None),
        P(None, "node", None, None),
        P(None, "node", None),
    )
    out_specs = (
        P("layer", None, "node", None),
        P("layer", None, "node", None),
        P("layer", None, None),
        P("layer", None, None),
    )
    return jax.shard_map(body, mesh=mesh, in_specs=in_specs, out_specs=out_specs, check_vma=False)
```

```python
import functools

import jax
import jax.numpy as jnp
from jax import lax
from jax.experimental import pallas as pl
from jax.experimental.pallas import tpu as pltpu
from jax.sharding import PartitionSpec as P

BF = jnp.bfloat16
F32 = jnp.float32
NN = (((1,), (0,)), ((), ()))
NT = (((1,), (1,)), ((), ()))
TN = (((0,), (0,)), ((), ()))
FAR = pl.BlockSpec(memory_space=pltpu.HBM)
LOCAL = pl.BlockSpec(memory_space=pltpu.VMEM)
VMEM_BYTES = 16 * 1024 * 1024


def dot(a, b, dims=NN):
    return lax.dot_general(a, b, dims, preferred_element_type=F32)


def shift(value, axis, steps):
    count = lax.axis_size(axis)
    return lax.ppermute(value, axis, [(i, (i + steps) % count) for i in range(count)])


def sibling(value):
    count = lax.axis_size("node")
    return lax.ppermute(value, "node", [(i, i ^ 1) for i in range(count)])


def exchange(value):
    return lax.all_to_all(value, "node", split_axis=0, concat_axis=0, tiled=True)


def of_span(shape):
    return pl.BlockSpec((None, *shape), lambda i, ids, cols: (ids[0], *((0,) * len(shape))))


def whole(shape):
    return pl.BlockSpec(shape, lambda i, ids, cols: (0,) * len(shape))


def near(shape, dtype=BF):
    return pltpu.VMEM(shape, dtype), LOCAL


def far_block(shape, dtype=BF):
    return pltpu.HBM(shape, dtype), whole(shape)


def run(kernel, name, scalars, ins, outs, scratch=(), aliases=None, flops=0, moved=0):
    ins = [v if isinstance(v, tuple) else (v, LOCAL) for v in ins]
    arrays = [
        pltpu.with_memory_space_constraint(a, pltpu.VMEM if s is LOCAL else pltpu.HBM)
        for a, s in ins
    ]
    return pl.pallas_call(
        kernel,
        name=name,
        grid_spec=pltpu.PrefetchScalarGridSpec(
            num_scalar_prefetch=2,
            grid=(1,),
            in_specs=[s for _, s in ins],
            out_specs=[s for _, s in outs],
            scratch_shapes=list(scratch),
        ),
        out_shape=[o for o, _ in outs],
        input_output_aliases={} if aliases is None else {k + 2: v for k, v in aliases.items()},
        compiler_params=pltpu.CompilerParams(vmem_limit_bytes=VMEM_BYTES),
        cost_estimate=pl.CostEstimate(flops=flops, bytes_accessed=moved, transcendentals=0),
    )(*scalars, *arrays)


def tie(*values):
    return lax.optimization_barrier(values)


def weight_copies(layer, ids, w_refs, w_scr, sems, act):
    own_s, own_n, left, left_x, right, right_x, far, far_x = w_refs
    core = ids[1]
    pairs = [
        [(own_s, 0), (own_n, 1)],
        [(right, core), (right_x, 1 - core)],
        [(far, core), (far_x, 1 - core)],
        [(left, core), (left_x, 1 - core)],
    ]
    which = lax.rem(layer - ids[0] + 4, 4)
    for option, pair in enumerate(pairs):

        @pl.when(which == option)
        def _():
            for n, (ref, place) in enumerate(pair):
                act(pltpu.make_async_copy(ref, w_scr.at[place], sems.at[n]))


def start_weights(*args):
    weight_copies(*args, lambda copy: copy.start())


def wait_weights(*args):
    weight_copies(*args, lambda copy: copy.wait())


def side_by_side(vals_ref, r, degree):
    return jnp.concatenate([vals_ref[r, j] for j in range(degree)], axis=1)


def aggregate_rows(ids, cols, vals_ref, ext):
    tiles, degree, size = vals_ref.shape[0], vals_ref.shape[1], vals_ref.shape[2]
    parts = []
    for r in range(tiles):
        picked = jnp.concatenate(
            [ext[pl.ds(pl.multiple_of(cols[ids[0], r, j] * size, size), size), :] for j in range(degree)],
            axis=0,
        )
        parts.append(dot(side_by_side(vals_ref, r, degree), picked))
    return jnp.concatenate(parts, axis=0).astype(BF)


def spread_rows(ids, cols, vals_ref, d_agg, d_ext):
    tiles, degree, size = vals_ref.shape[0], vals_ref.shape[1], vals_ref.shape[2]
    d_ext[...] = jnp.zeros_like(d_ext)
    for r in range(tiles):
        pieces = dot(side_by_side(vals_ref, r, degree), d_agg[r * size : (r + 1) * size], TN)
        for j in range(degree):
            rows = pl.ds(pl.multiple_of(cols[ids[0], r, j] * size, size), size)
            d_ext[rows, :] += pieces[j * size : (j + 1) * size]


def to_slot(value_ref, layer, ids, buf_ref, sem):
    return pltpu.make_async_copy(value_ref, buf_ref.at[lax.rem(layer - ids[0] + 4, 4)], sem)


def sigmoid(v):
    return 1.0 / (1.0 + jnp.exp(-v))


def pre_kernel(ids, cols, h_ref, rows_ref, counts_ref, vals_ref, pick_ref, out_ref, h_out, vals_out, pick_far):
    slots, peers = rows_ref.shape
    total, node_rows = pick_ref.shape
    bits = slots.bit_length() - 1
    slot = lax.broadcasted_iota(jnp.int32, (total, peers), 0)
    owner = lax.broadcasted_iota(jnp.int32, (total, peers), 1)
    mine = lax.shift_right_logical(slot, bits) == owner
    wide = dot(mine.astype(F32).astype(BF), rows_ref[...].astype(F32).astype(BF), NT)
    slot_k = lax.broadcasted_iota(jnp.int32, (total, slots), 0) & (slots - 1)
    in_slot = slot_k == lax.broadcasted_iota(jnp.int32, (total, slots), 1)
    row = jnp.sum(jnp.where(in_slot, wide, 0.0), axis=1, keepdims=True)
    counts = jnp.broadcast_to(counts_ref[...].astype(F32), (total, peers))
    count = jnp.sum(jnp.where(mine, counts, 0.0), axis=1, keepdims=True)
    k = (lax.broadcasted_iota(jnp.int32, (total, 1), 0) & (slots - 1)).astype(F32)
    row = jnp.where(k < count, row, -1.0)
    place = lax.broadcasted_iota(jnp.int32, (total, node_rows), 1).astype(F32)
    pick = (place == row).astype(F32).astype(BF)
    pick_ref[...] = pick
    pick_far[...] = pick
    out_ref[...] = dot(pick, h_ref[...]).astype(BF)
    h_out[...] = h_ref[...]
    vals_out[...] = vals_ref[...]


def forward_math(ids, cols, h_ref, arr_ref, vals_ref, w_ref, ext, ready=None):
    rows = h_ref.shape[0]
    ext[0:rows, :] = h_ref[...]
    ext[rows : 2 * rows, :] = arr_ref[...]
    agg = aggregate_rows(ids, cols, vals_ref, ext)
    if ready is not None:
        ready()
    pre = dot(h_ref[...], w_ref[0]) + dot(agg, w_ref[1])
    sig = sigmoid(pre)
    return agg, pre, sig, (pre * sig).astype(BF)


def forward_kernel(layer, ids, cols, h_ref, arr_ref, vals_ref, pick_ref, *rest):
    w_refs, rest = rest[:8], rest[8:]
    first = layer == 0
    if first:
        agg_ref, pre_ref, hid_ref, out_ref, next_ref, w_ref = rest[:6]
    else:
        w_ref, *rest = rest[0:1] + rest[1 + (layer > 1) :]
        agg_ref, pre_ref, hid_ref, out_ref, next_ref, buf_ref = rest[:6]
    ext, buf_sem, sems = rest[-3:]
    if not first:
        copy = to_slot(h_ref, layer - 1, ids, buf_ref, buf_sem)
        copy.start()
    ready = None
    if first:
        here = (layer, ids, w_refs, w_ref, sems.at[0])
        start_weights(*here)
        ready = lambda: wait_weights(*here)
    ahead = (layer + 1, ids, w_refs, next_ref, sems.at[1])
    start_weights(*ahead)
    agg, pre, _, hid = forward_math(ids, cols, h_ref, arr_ref, vals_ref, w_ref, ext, ready)
    hid_ref[...] = hid
    out_ref[...] = dot(pick_ref[...], hid).astype(BF)
    agg_ref[...] = agg
    pre_ref[...] = pre
    if not first:
        copy.wait()
    wait_weights(*ahead)


def backward_math(ids, cols, d_pre, vals_ref, w_ref, d_ext):
    d_agg = dot(d_pre, w_ref[1], NT).astype(BF)
    spread_rows(ids, cols, vals_ref, d_agg, d_ext)
    return dot(d_pre, w_ref[0], NT)


def weight_partials(ids, h_ref, agg, d_pre, keep_ref, send_ref):
    on_rows = dot(h_ref[...], d_pre, TN).astype(BF)
    on_agg = dot(agg, d_pre, TN).astype(BF)

    @pl.when(ids[1] == 0)
    def _():
        keep_ref[...] = on_rows
        send_ref[...] = on_agg

    @pl.when(ids[1] != 0)
    def _():
        keep_ref[...] = on_agg
        send_ref[...] = on_rows


def top_kernel(layer, ids, cols, h_ref, arr_ref, vals_ref, wout_ref, lab_ref, mask_ref, w_ref, *rest):
    remote_ref, part_ref, keep_ref, send_ref, buf_ref, hid_ref, ext, d_ext, buf_sem = rest[1:]
    copy = to_slot(h_ref, layer - 1, ids, buf_ref, buf_sem)
    copy.start()
    rows = h_ref.shape[0]
    agg, pre, sig, hid = forward_math(ids, cols, h_ref, arr_ref, vals_ref, w_ref, ext)
    hid_ref[...] = hid
    last = to_slot(hid_ref, layer, ids, buf_ref, buf_sem)
    copy.wait()
    last.start()
    logits = dot(wout_ref[...], hid, NT)
    expo = jnp.exp(logits)
    probs = expo / jnp.sum(expo, axis=0, keepdims=True)
    label = lab_ref[pl.ds(ids[0], 1), :]
    onehot = (label == lax.broadcasted_iota(jnp.int32, logits.shape, 0)).astype(F32)
    live = mask_ref[pl.ds(ids[0], 1), :].astype(F32)
    g_logits = (live * (probs - onehot)).astype(BF)
    d_out = dot(g_logits, wout_ref[...], TN).astype(BF)
    d_pre = (d_out.astype(F32) * (sig * (1.0 + pre * (1.0 - sig)))).astype(BF)
    back = backward_math(ids, cols, d_pre, vals_ref, w_ref, d_ext)
    remote_ref[...] = d_ext[rows : 2 * rows, :].astype(BF).reshape(remote_ref.shape)
    part_ref[...] = back + d_ext[0:rows, :]
    weight_partials(ids, h_ref, agg, d_pre, keep_ref, send_ref)
    last.wait()


def chunk_sum(block):
    total = block[0:2].astype(F32)
    for n in range(2, block.shape[0], 2):
        total = total + block[n : n + 2].astype(F32)
    return total


def backward_kernel(layer, carry, ids, cols, ret_ref, part_in, pre_ref, h_ref, agg_ref, *rest):
    (vals_ref, pick_ref, w_ref), rest = rest[:3], rest[3:]
    if carry:
        keep_in, recv_in, rest = rest[0], rest[1], rest[2:]
    if layer < 2:
        rest = rest[1:]
    out_ref, part_ref, buf_ref, keep_ref, send_ref, *rest = rest
    if not layer:
        *rest, local, local_sem = rest
    *chunk, dout_ref, d_ext, buf_sem = rest
    rows, feat = part_in.shape
    peers = out_ref.shape[0]
    slots = rows // peers
    returned = ret_ref[:, 0:slots, :].reshape(rows, feat)
    d_out = (part_in[...] + dot(pick_ref[...], returned, TN)).astype(BF)
    dout_ref[...] = d_out
    copy = to_slot(dout_ref, layer + 1, ids, buf_ref, buf_sem)
    copy.start()
    pre = pre_ref[...]
    sig = sigmoid(pre)
    d_pre = (d_out.astype(F32) * (sig * (1.0 + pre * (1.0 - sig)))).astype(BF)
    back = backward_math(ids, cols, d_pre, vals_ref, w_ref, d_ext)
    target = out_ref if layer else local
    target[:, 0:slots, :] = d_ext[rows : 2 * rows, :].astype(BF).reshape(peers, slots, feat)
    if carry:
        put_carry(keep_in, recv_in, target, slots)
    if not layer:
        away = pltpu.make_async_copy(local, out_ref.at[:, pl.ds(0, local.shape[1]), :], local_sem)
        away.start()
    part_ref[...] = back + d_ext[0:rows, :]
    weight_partials(ids, h_ref, agg_ref[...], d_pre, keep_ref, send_ref)
    if chunk:
        chunk[0][...] = chunk_sum(ret_ref[:, slots:, :]).astype(BF)
    copy.wait()
    if not layer:
        away.wait()


def put_carry(keep_ref, recv_ref, out_ref, first):
    peers, feat = out_ref.shape[0], out_ref.shape[2]
    size = keep_ref.shape[0] // peers
    total = (keep_ref[...].astype(F32) + recv_ref[...].astype(F32)).astype(BF)
    out_ref[:, first : first + size, :] = total.reshape(peers, size, feat)


def join_kernel(ids, cols, keep_a, recv_a, keep_b, recv_b, buf_in, out_ref, local, sem):
    size = local.shape[1] // 2
    first = out_ref.shape[1] - 2 * size
    put_carry(keep_a, recv_a, local, 0)
    put_carry(keep_b, recv_b, local, size)
    copy = pltpu.make_async_copy(local, out_ref.at[:, pl.ds(first, 2 * size), :], sem)
    copy.start()
    copy.wait()


def chunk_kernel(ids, cols, ret_ref, c_3, out_ref):
    size = c_3.shape[1]
    slots = ret_ref.shape[1] - 3 * size
    out_ref[3] = c_3[...]
    for n, layer in enumerate((2, 1, 0)):
        first = slots + n * size
        out_ref[layer] = chunk_sum(ret_ref[:, first : first + size, :]).astype(BF)


def end_kernel(ids, cols, ret_ref, part_in, pick_ref, buf_in, buf_ref, dout_ref, buf_sem):
    rows, feat = part_in.shape
    returned = ret_ref[:, 0 : rows // ret_ref.shape[0], :].reshape(rows, feat)
    dout_ref[...] = (part_in[...] + dot(pick_ref[...], returned, TN)).astype(BF)
    copy = to_slot(dout_ref, 0, ids, buf_ref, buf_sem)
    copy.start()
    copy.wait()


def layer_sum_kernel(ids, cols, sums_ref, out_ref):
    total = sums_ref[0].astype(F32)
    for span in range(1, sums_ref.shape[0]):
        total = total + sums_ref[span].astype(F32)
    total = total.astype(BF)
    for n in range(0, out_ref.shape[0], 2):
        out_ref[n : n + 2] = total


def scale_kernel(scale, ids, cols, mine_ref, other_ref, self_ref, neigh_ref):
    mine = mine_ref[...].astype(F32) * scale
    other = other_ref[...].astype(F32) * scale

    @pl.when(ids[1] == 0)
    def _():
        self_ref[0] = mine
        neigh_ref[0] = other

    @pl.when(ids[1] != 0)
    def _():
        self_ref[0] = other
        neigh_ref[0] = mine


def home_kernel(ids, cols, *refs):
    pieces, out_ref = refs[:-1], refs[-1]
    for s, piece in enumerate(pieces):
        out_ref[0, lax.rem(ids[0] + 4 - s, 4)] = piece[...]


def body(
    features,
    w_self,
    w_neigh,
    w_out,
    labels,
    train_mask,
    tile_cols,
    tile_vals,
    send_rows,
    send_counts,
):
    home = lax.axis_index("layer")
    node = lax.axis_index("node")
    core = lax.rem(node, 2)
    spans, rows, feat = features.shape
    peers, slots = send_rows.shape[2], send_rows.shape[3]
    tiles, degree, size = tile_vals.shape[2], tile_vals.shape[3], tile_vals.shape[4]
    scale = 1.0 / (spans * rows * peers)
    scalars = (jnp.stack([home, core]).astype(jnp.int32), tile_cols.reshape(spans, tiles, degree))
    act, wide, square = near((rows, feat)), near((rows, feat), F32), near((feat, feat))
    ext_scratch = pltpu.VMEM((2 * rows, feat), BF)
    d_ext_scratch = pltpu.VMEM((2 * rows, feat), F32)
    all_shifts = range(1, spans)

    mine = jnp.where(core == 0, w_self[0], w_neigh[0])
    left, right, far = (shift(mine, "layer", s) for s in (1, -1, 2))
    pick, outgoing, features_0, vals, pick_far = run(
        pre_kernel,
        "gather_rows",
        scalars,
        [
            (features, of_span((rows, feat))),
            (send_rows.reshape(spans, peers, slots).swapaxes(1, 2), of_span((slots, peers))),
            (send_counts.reshape(spans, 1, peers), of_span((1, peers))),
            (
                tile_vals.reshape(spans, tiles, degree, size, size),
                of_span((tiles, degree, size, size)),
            ),
        ],
        [
            near((peers * slots, rows)),
            act,
            act,
            near((tiles, degree, size, size)),
            far_block((peers * slots, rows)),
        ],
        flops=10**8,
        moved=10**6,
    )
    arrived = exchange(outgoing.reshape(peers, slots, feat))
    arrived, left, right, far = tie(arrived, left, right, far)
    sources = [(w_self[0], FAR), (w_neigh[0], FAR), left, sibling(left), right, sibling(right)]
    sources += [far, sibling(far)]
    weight = near((2, feat, feat))

    hidden, aggs, pres, weights = [features_0], [], [], []
    top = spans - 1
    stack = (pltpu.HBM((spans, rows, feat), BF), FAR)
    buf_sem = pltpu.SemaphoreType.DMA
    acts_buf = None
    for layer in range(top):
        ins = [hidden[layer], arrived.reshape(rows, feat), vals, pick, *sources]
        if layer:
            ins.append(weights[layer])
        if layer > 1:
            ins.append((acts_buf, FAR))
        agg, pre, hid, outgoing, arranged, last = run(
            functools.partial(forward_kernel, layer),
            f"layer_forward_{layer}",
            scalars,
            ins,
            [act, wide, act, act, weight, stack if layer else weight],
            [ext_scratch, buf_sem, pltpu.SemaphoreType.DMA((2, 2))],
            {len(ins) - 1: 5} if layer > 1 else None,
            flops=6 * 10**8,
            moved=4 * 10**6,
        )
        if layer:
            acts_buf = last
        else:
            weights.append(last)
        weights.append(arranged)
        hidden.append(hid)
        aggs.append(agg)
        pres.append(pre)
        arrived = exchange(outgoing.reshape(peers, slots, feat))

    ins = [
        hidden[top],
        arrived.reshape(rows, feat),
        vals,
        w_out.T,
        labels,
        train_mask,
        weights[top],
        (acts_buf, FAR),
    ]
    remote, part, keep, send, acts_buf = run(
        functools.partial(top_kernel, top),
        "top_layer",
        scalars,
        ins,
        [near((peers, slots, feat)), wide, square, square, stack],
        [
            pltpu.VMEM((rows, feat), BF),
            ext_scratch,
            d_ext_scratch,
            buf_sem,
        ],
        {len(ins) - 1: 4},
        flops=10**9,
        moved=5 * 10**6,
    )

    def travel(buf):
        return [shift(buf[s], "layer", s) for s in all_shifts]

    def put_home(buf, *pieces):
        block = pl.BlockSpec((None, rows, feat), lambda i, ids, cols: (0, 0, 0))
        shape = (1, spans, rows, feat)
        return run(
            home_kernel,
            "put_home",
            scalars,
            [(buf, block), *pieces],
            [far_block(shape)],
            moved=2 * 10**6,
        )[0]

    chunk_rows = feat // peers
    pairs, grads_buf = [], None
    for layer in range(top - 1, -1, -1):
        returned, send = tie(exchange(remote), send)
        pairs.append((keep, sibling(send)))
        carry = layer < top - 1
        width = slots + chunk_rows * (carry + 2 * (layer == 0))
        ins = [
            returned,
            part,
            pres[layer],
            hidden[layer],
            aggs[layer],
            vals,
            pick,
            weights[layer],
        ]
        if carry:
            ins += pairs[-2]
        aliases = None
        if grads_buf is not None:
            ins.append((grads_buf, FAR))
            aliases = {len(ins) - 1: 2}
        last = far_block if layer == 0 else near
        operand = near((peers, width, feat))
        scratch = [pltpu.VMEM((rows, feat), BF), d_ext_scratch, buf_sem]
        if layer == 0:
            operand = (pltpu.HBM((peers, width, feat), BF), FAR)
            scratch += [pltpu.VMEM((peers, slots + chunk_rows, feat), BF), buf_sem]
        outs = [operand, last((rows, feat), F32), stack, square, square]
        if layer == 0:
            outs.append(far_block((2, chunk_rows, feat)))
        remote, part, grads_buf, keep, send, *c_3 = run(
            functools.partial(backward_kernel, layer, carry),
            f"layer_backward_{layer}",
            scalars,
            ins,
            outs,
            scratch,
            aliases,
            flops=10**9,
            moved=5 * 10**6,
        )
        if layer:
            remote, recv = tie(remote, pairs[-1][1])
            pairs[-1] = (pairs[-1][0], recv)

    joined = run(
        join_kernel,
        "join_rows",
        scalars,
        [*pairs[-1], keep, sibling(send), (remote, FAR)],
        [(pltpu.HBM((peers, slots + 3 * chunk_rows, feat), BF), FAR)],
        [pltpu.VMEM((peers, 2 * chunk_rows, feat), BF), buf_sem],
        aliases={4: 0},
        moved=3 * 10**6,
    )[0]
    joined, acts_buf = tie(joined, acts_buf)
    acts = travel(acts_buf)
    layer_acts = put_home(acts_buf, *acts)
    returned, layer_acts = tie(exchange(joined), layer_acts)
    sums = run(
        chunk_kernel,
        "sum_chunks",
        scalars,
        [returned, (c_3[0], whole(c_3[0].shape))],
        [far_block((spans, 2, chunk_rows, feat))],
        moved=10**6,
    )[0]
    sums = lax.all_to_all(sums, "layer", split_axis=0, concat_axis=0, tiled=True)
    grads_buf = run(
        end_kernel,
        "input_grads",
        scalars,
        [
            returned,
            (part, whole((rows, feat))),
            (pick_far, whole(pick_far.shape)),
            (grads_buf, FAR),
        ],
        [stack],
        [pltpu.VMEM((rows, feat), BF), buf_sem],
        {3: 0},
        flops=10**8,
        moved=10**6,
    )[0]
    sums, *to_send = tie(sums, *[grads_buf[s] for s in all_shifts])
    spread = run(
        layer_sum_kernel,
        "sum_over_layer",
        scalars,
        [sums],
        [far_block((peers, chunk_rows, feat))],
        moved=10**6,
    )[0]
    grads = [shift(v, "layer", s) for s, v in zip(all_shifts, to_send)]
    gathered, *grads = tie(exchange(spread), *grads)
    gathered = gathered.reshape(feat, feat)
    other = sibling(gathered)
    act_grads = put_home(grads_buf, *grads)
    out_square = (1, feat, feat)
    grad_self, grad_neigh = run(
        functools.partial(scale_kernel, scale),
        "scale_grads",
        scalars,
        [gathered, other],
        [(pltpu.HBM(out_square, F32), whole(out_square))] * 2,
        moved=3 * 10**6,
    )
    return (layer_acts, act_grads, grad_self, grad_neigh)


def solution(mesh):
    in_specs = (
        P(None, "node", None),
        P("layer", None, None),
        P("layer", None, None),
        P(),
        P(None, "node"),
        P(None, "node"),
        P(None, "node", None, None),
        P(None, "node", None, None, None, None),
        P(None, "node", None, None),
        P(None, "node", None),
    )
    out_specs = (
        P("layer", None, "node", None),
        P("layer", None, "node", None),
        P("layer", None, None),
        P("layer", None, None),
    )
    return jax.shard_map(body, mesh=mesh, in_specs=in_specs, out_specs=out_specs, check_vma=False)
```

```python
import functools

import jax
import jax.numpy as jnp
from jax import lax
from jax.experimental import pallas as pl
from jax.experimental.pallas import tpu as pltpu
from jax.sharding import PartitionSpec as P

BF = jnp.bfloat16
F32 = jnp.float32
NN = (((1,), (0,)), ((), ()))
NT = (((1,), (1,)), ((), ()))
TN = (((0,), (0,)), ((), ()))
FAR = pl.BlockSpec(memory_space=pltpu.HBM)
LOCAL = pl.BlockSpec(memory_space=pltpu.VMEM)
VMEM_BYTES = 16 * 1024 * 1024


def dot(a, b, dims=NN):
    return lax.dot_general(a, b, dims, preferred_element_type=F32)


def shift(value, axis, steps):
    count = lax.axis_size(axis)
    return lax.ppermute(value, axis, [(i, (i + steps) % count) for i in range(count)])


def sibling(value):
    count = lax.axis_size("node")
    return lax.ppermute(value, "node", [(i, i ^ 1) for i in range(count)])


def exchange(value):
    return lax.all_to_all(value, "node", split_axis=0, concat_axis=0, tiled=True)


def of_span(shape):
    return pl.BlockSpec((None, *shape), lambda i, ids, cols: (ids[0], *((0,) * len(shape))))


def whole(shape):
    return pl.BlockSpec(shape, lambda i, ids, cols: (0,) * len(shape))


def near(shape, dtype=BF):
    return pltpu.VMEM(shape, dtype), LOCAL


def far_block(shape, dtype=BF):
    return pltpu.HBM(shape, dtype), whole(shape)


def run(kernel, name, scalars, ins, outs, scratch=(), aliases=None, flops=0, moved=0):
    ins = [v if isinstance(v, tuple) else (v, LOCAL) for v in ins]
    arrays = [
        pltpu.with_memory_space_constraint(a, pltpu.VMEM if s is LOCAL else pltpu.HBM)
        for a, s in ins
    ]
    return pl.pallas_call(
        kernel,
        name=name,
        grid_spec=pltpu.PrefetchScalarGridSpec(
            num_scalar_prefetch=2,
            grid=(1,),
            in_specs=[s for _, s in ins],
            out_specs=[s for _, s in outs],
            scratch_shapes=list(scratch),
        ),
        out_shape=[o for o, _ in outs],
        input_output_aliases={} if aliases is None else {k + 2: v for k, v in aliases.items()},
        compiler_params=pltpu.CompilerParams(vmem_limit_bytes=VMEM_BYTES),
        cost_estimate=pl.CostEstimate(flops=flops, bytes_accessed=moved, transcendentals=0),
    )(*scalars, *arrays)


def tie(*values):
    return lax.optimization_barrier(values)


def weight_copies(layer, ids, w_refs, w_scr, sems, act):
    own_s, own_n, left, left_x, right, right_x, far, far_x = w_refs
    core = ids[1]
    pairs = [
        [(own_s, 0), (own_n, 1)],
        [(right, core), (right_x, 1 - core)],
        [(far, core), (far_x, 1 - core)],
        [(left, core), (left_x, 1 - core)],
    ]
    which = lax.rem(layer - ids[0] + 4, 4)
    for option, pair in enumerate(pairs):

        @pl.when(which == option)
        def _():
            for n, (ref, place) in enumerate(pair):
                act(pltpu.make_async_copy(ref, w_scr.at[place], sems.at[n]))


def start_weights(*args):
    weight_copies(*args, lambda copy: copy.start())


def wait_weights(*args):
    weight_copies(*args, lambda copy: copy.wait())


def side_by_side(vals_ref, r, degree):
    return jnp.concatenate([vals_ref[r, j] for j in range(degree)], axis=1)


def aggregate_rows(ids, cols, vals_ref, ext):
    tiles, degree, size = vals_ref.shape[0], vals_ref.shape[1], vals_ref.shape[2]
    parts = []
    for r in range(tiles):
        picked = jnp.concatenate(
            [ext[pl.ds(pl.multiple_of(cols[ids[0], r, j] * size, size), size), :] for j in range(degree)],
            axis=0,
        )
        parts.append(dot(side_by_side(vals_ref, r, degree), picked))
    return jnp.concatenate(parts, axis=0).astype(BF)


def spread_rows(ids, cols, vals_ref, d_agg, d_ext):
    tiles, degree, size = vals_ref.shape[0], vals_ref.shape[1], vals_ref.shape[2]
    d_ext[...] = jnp.zeros_like(d_ext)
    for r in range(tiles):
        pieces = dot(side_by_side(vals_ref, r, degree), d_agg[r * size : (r + 1) * size], TN)
        for j in range(degree):
            rows = pl.ds(pl.multiple_of(cols[ids[0], r, j] * size, size), size)
            d_ext[rows, :] += pieces[j * size : (j + 1) * size]


def to_slot(value_ref, layer, ids, buf_ref, sem):
    return pltpu.make_async_copy(value_ref, buf_ref.at[lax.rem(layer - ids[0] + 4, 4)], sem)


def sigmoid(v):
    return 1.0 / (1.0 + jnp.exp(-v))


def pre_kernel(ids, cols, h_ref, rows_ref, counts_ref, vals_ref, pick_ref, out_ref, h_out, vals_out, pick_far):
    slots, peers = rows_ref.shape
    total, node_rows = pick_ref.shape
    bits = slots.bit_length() - 1
    slot = lax.broadcasted_iota(jnp.int32, (total, peers), 0)
    owner = lax.broadcasted_iota(jnp.int32, (total, peers), 1)
    mine = lax.shift_right_logical(slot, bits) == owner
    wide = dot(mine.astype(F32).astype(BF), rows_ref[...].astype(F32).astype(BF), NT)
    slot_k = lax.broadcasted_iota(jnp.int32, (total, slots), 0) & (slots - 1)
    in_slot = slot_k == lax.broadcasted_iota(jnp.int32, (total, slots), 1)
    row = jnp.sum(jnp.where(in_slot, wide, 0.0), axis=1, keepdims=True)
    counts = jnp.broadcast_to(counts_ref[...].astype(F32), (total, peers))
    count = jnp.sum(jnp.where(mine, counts, 0.0), axis=1, keepdims=True)
    k = (lax.broadcasted_iota(jnp.int32, (total, 1), 0) & (slots - 1)).astype(F32)
    row = jnp.where(k < count, row, -1.0)
    place = lax.broadcasted_iota(jnp.int32, (total, node_rows), 1).astype(F32)
    pick = (place == row).astype(F32).astype(BF)
    pick_ref[...] = pick
    pick_far[...] = pick
    out_ref[...] = dot(pick, h_ref[...]).astype(BF)
    h_out[...] = h_ref[...]
    vals_out[...] = vals_ref[...]


def forward_math(ids, cols, h_ref, arr_ref, vals_ref, w_ref, ext, ready=None):
    rows = h_ref.shape[0]
    ext[0:rows, :] = h_ref[...]
    ext[rows : 2 * rows, :] = arr_ref[...]
    agg = aggregate_rows(ids, cols, vals_ref, ext)
    if ready is not None:
        ready()
    pre = dot(h_ref[...], w_ref[0]) + dot(agg, w_ref[1])
    sig = sigmoid(pre)
    return agg, pre, sig, (pre * sig).astype(BF)


def forward_kernel(layer, ids, cols, h_ref, arr_ref, vals_ref, pick_ref, *rest):
    w_refs, rest = rest[:8], rest[8:]
    first = layer == 0
    if first:
        agg_ref, pre_ref, hid_ref, out_ref, next_ref, w_ref = rest[:6]
    else:
        w_ref, *rest = rest[0:1] + rest[1 + (layer > 1) :]
        agg_ref, pre_ref, hid_ref, out_ref, next_ref, buf_ref = rest[:6]
    ext, buf_sem, sems = rest[-3:]
    if not first:
        copy = to_slot(h_ref, layer - 1, ids, buf_ref, buf_sem)
        copy.start()
    ready = None
    if first:
        here = (layer, ids, w_refs, w_ref, sems.at[0])
        start_weights(*here)
        ready = lambda: wait_weights(*here)
    ahead = (layer + 1, ids, w_refs, next_ref, sems.at[1])
    start_weights(*ahead)
    agg, pre, _, hid = forward_math(ids, cols, h_ref, arr_ref, vals_ref, w_ref, ext, ready)
    hid_ref[...] = hid
    out_ref[...] = dot(pick_ref[...], hid).astype(BF)
    agg_ref[...] = agg
    pre_ref[...] = pre
    if not first:
        copy.wait()
    wait_weights(*ahead)


def backward_math(ids, cols, d_pre, vals_ref, w_ref, d_ext):
    d_agg = dot(d_pre, w_ref[1], NT).astype(BF)
    spread_rows(ids, cols, vals_ref, d_agg, d_ext)
    return dot(d_pre, w_ref[0], NT)


def weight_partials(ids, h_ref, agg, d_pre, keep_ref, send_ref):
    on_rows = dot(h_ref[...], d_pre, TN).astype(BF)
    on_agg = dot(agg, d_pre, TN).astype(BF)

    @pl.when(ids[1] == 0)
    def _():
        keep_ref[...] = on_rows
        send_ref[...] = on_agg

    @pl.when(ids[1] != 0)
    def _():
        keep_ref[...] = on_agg
        send_ref[...] = on_rows


def top_kernel(layer, ids, cols, h_ref, arr_ref, vals_ref, wout_ref, lab_ref, mask_ref, w_ref, *rest):
    remote_ref, part_ref, keep_ref, send_ref, buf_ref, hid_ref, ext, d_ext, buf_sem = rest[1:]
    copy = to_slot(h_ref, layer - 1, ids, buf_ref, buf_sem)
    copy.start()
    rows = h_ref.shape[0]
    agg, pre, sig, hid = forward_math(ids, cols, h_ref, arr_ref, vals_ref, w_ref, ext)
    hid_ref[...] = hid
    last = to_slot(hid_ref, layer, ids, buf_ref, buf_sem)
    copy.wait()
    last.start()
    logits = dot(wout_ref[...], hid, NT)
    expo = jnp.exp(logits)
    probs = expo / jnp.sum(expo, axis=0, keepdims=True)
    label = lab_ref[pl.ds(ids[0], 1), :]
    onehot = (label == lax.broadcasted_iota(jnp.int32, logits.shape, 0)).astype(F32)
    live = mask_ref[pl.ds(ids[0], 1), :].astype(F32)
    g_logits = (live * (probs - onehot)).astype(BF)
    d_out = dot(g_logits, wout_ref[...], TN).astype(BF)
    d_pre = (d_out.astype(F32) * (sig * (1.0 + pre * (1.0 - sig)))).astype(BF)
    back = backward_math(ids, cols, d_pre, vals_ref, w_ref, d_ext)
    remote_ref[...] = d_ext[rows : 2 * rows, :].astype(BF).reshape(remote_ref.shape)
    part_ref[...] = back + d_ext[0:rows, :]
    weight_partials(ids, h_ref, agg, d_pre, keep_ref, send_ref)
    last.wait()


def chunk_sum(block):
    total = block[0:2].astype(F32)
    for n in range(2, block.shape[0], 2):
        total = total + block[n : n + 2].astype(F32)
    return total


def slope_math(ids, layer, ret_ref, part_in, pre_ref, pick_ref, dout_ref, buf_ref, buf_sem):
    rows, feat = part_in.shape
    returned = ret_ref[:, 0 : rows // ret_ref.shape[0], :].reshape(rows, feat)
    d_out = (part_in[...] + dot(pick_ref[...], returned, TN)).astype(BF)
    dout_ref[...] = d_out
    copy = to_slot(dout_ref, layer + 1, ids, buf_ref, buf_sem)
    copy.start()
    pre = pre_ref[...]
    sig = sigmoid(pre)
    return (d_out.astype(F32) * (sig * (1.0 + pre * (1.0 - sig)))).astype(BF), copy


def backward_kernel(layer, carry, ids, cols, ret_ref, part_in, pre_ref, h_ref, agg_ref, *rest):
    (vals_ref, pick_ref, w_ref), rest = rest[:3], rest[3:]
    if carry:
        keep_in, recv_in, rest = rest[0], rest[1], rest[3:]
    out_ref, part_ref, buf_ref, keep_ref, send_ref, dout_ref, d_ext, buf_sem = rest
    rows, feat = part_in.shape
    d_pre, copy = slope_math(
        ids, layer, ret_ref, part_in, pre_ref, pick_ref, dout_ref, buf_ref, buf_sem
    )
    back = backward_math(ids, cols, d_pre, vals_ref, w_ref, d_ext)
    peers, slots = out_ref.shape[0], rows // out_ref.shape[0]
    out_ref[:, 0:slots, :] = d_ext[rows : 2 * rows, :].astype(BF).reshape(peers, slots, feat)
    if carry:
        put_carry(keep_in, recv_in, out_ref, slots)
    part_ref[...] = back + d_ext[0:rows, :]
    weight_partials(ids, h_ref, agg_ref[...], d_pre, keep_ref, send_ref)
    copy.wait()


def last_slope_kernel(
    ids, cols, ret_ref, part_in, pre_ref, h_ref, agg_ref, pick_ref, buf_in,
    dpre_ref, buf_ref, keep_ref, send_ref, chunk_ref, dout_ref, buf_sem,
):
    d_pre, copy = slope_math(
        ids, 0, ret_ref, part_in, pre_ref, pick_ref, dout_ref, buf_ref, buf_sem
    )
    dpre_ref[...] = d_pre
    weight_partials(ids, h_ref, agg_ref[...], d_pre, keep_ref, send_ref)
    slots = part_in.shape[0] // ret_ref.shape[0]
    chunk_ref[...] = chunk_sum(ret_ref[:, slots:, :]).astype(BF)
    copy.wait()


def last_spread_kernel(
    ids, cols, dpre_ref, vals_ref, w_ref, keep_a, recv_a, keep_b, recv_b, c_in,
    out_ref, part_ref, c_ref, d_ext, part, carried, local, sems,
):
    rows, feat = dpre_ref.shape
    peers, slots = local.shape[0], local.shape[1]
    size = keep_a.shape[0] // peers
    copies = [
        pltpu.make_async_copy(c_in, c_ref.at[3], sems.at[0]),
        pltpu.make_async_copy(
            carried, out_ref.at[:, pl.ds(slots, 2 * size), :], sems.at[1]
        ),
        pltpu.make_async_copy(local, out_ref.at[:, pl.ds(0, slots), :], sems.at[2]),
        pltpu.make_async_copy(part, part_ref, sems.at[3]),
    ]
    copies[0].start()
    put_carry(keep_a, recv_a, carried, 0)
    put_carry(keep_b, recv_b, carried, size)
    copies[1].start()
    back = backward_math(ids, cols, dpre_ref[...], vals_ref, w_ref, d_ext)
    local[...] = d_ext[rows : 2 * rows, :].astype(BF).reshape(local.shape)
    copies[2].start()
    part[...] = back + d_ext[0:rows, :]
    copies[3].start()
    for copy in copies:
        copy.wait()


def put_carry(keep_ref, recv_ref, out_ref, first):
    peers, feat = out_ref.shape[0], out_ref.shape[2]
    size = keep_ref.shape[0] // peers
    total = (keep_ref[...].astype(F32) + recv_ref[...].astype(F32)).astype(BF)
    out_ref[:, first : first + size, :] = total.reshape(peers, size, feat)


def join_kernel(ids, cols, keep_ref, recv_ref, buf_in, out_ref, local, sem):
    size = local.shape[1]
    put_carry(keep_ref, recv_ref, local, 0)
    first = out_ref.shape[1] - size
    copy = pltpu.make_async_copy(local, out_ref.at[:, pl.ds(first, size), :], sem)
    copy.start()
    copy.wait()


def chunk_kernel(ids, cols, ret_ref, buf_in, out_ref, sums, sem):
    size = sums.shape[2]
    slots = ret_ref.shape[1] - 3 * size
    for n, layer in enumerate((2, 1, 0)):
        first = slots + n * size
        sums[layer] = chunk_sum(ret_ref[:, first : first + size, :]).astype(BF)
    copy = pltpu.make_async_copy(sums, out_ref.at[pl.ds(0, 3)], sem)
    copy.start()
    copy.wait()


def end_kernel(ids, cols, ret_ref, part_in, pick_ref, buf_in, buf_ref, dout_ref, buf_sem):
    rows, feat = part_in.shape
    returned = ret_ref[:, 0 : rows // ret_ref.shape[0], :].reshape(rows, feat)
    dout_ref[...] = (part_in[...] + dot(pick_ref[...], returned, TN)).astype(BF)
    copy = to_slot(dout_ref, 0, ids, buf_ref, buf_sem)
    copy.start()
    copy.wait()


def layer_sum_kernel(ids, cols, sums_ref, out_ref):
    total = sums_ref[0].astype(F32)
    for span in range(1, sums_ref.shape[0]):
        total = total + sums_ref[span].astype(F32)
    total = total.astype(BF)
    for n in range(0, out_ref.shape[0], 2):
        out_ref[n : n + 2] = total


def scale_kernel(scale, ids, cols, mine_ref, other_ref, self_ref, neigh_ref):
    mine = mine_ref[...].astype(F32) * scale
    other = other_ref[...].astype(F32) * scale

    @pl.when(ids[1] == 0)
    def _():
        self_ref[0] = mine
        neigh_ref[0] = other

    @pl.when(ids[1] != 0)
    def _():
        self_ref[0] = other
        neigh_ref[0] = mine


def home_kernel(ids, cols, *refs):
    pieces, out_ref = refs[:-1], refs[-1]
    for s, piece in enumerate(pieces):
        out_ref[0, lax.rem(ids[0] + 4 - s, 4)] = piece[...]


def body(
    features,
    w_self,
    w_neigh,
    w_out,
    labels,
    train_mask,
    tile_cols,
    tile_vals,
    send_rows,
    send_counts,
):
    home = lax.axis_index("layer")
    node = lax.axis_index("node")
    core = lax.rem(node, 2)
    spans, rows, feat = features.shape
    peers, slots = send_rows.shape[2], send_rows.shape[3]
    tiles, degree, size = tile_vals.shape[2], tile_vals.shape[3], tile_vals.shape[4]
    scale = 1.0 / (spans * rows * peers)
    scalars = (jnp.stack([home, core]).astype(jnp.int32), tile_cols.reshape(spans, tiles, degree))
    act, wide, square = near((rows, feat)), near((rows, feat), F32), near((feat, feat))
    ext_scratch = pltpu.VMEM((2 * rows, feat), BF)
    d_ext_scratch = pltpu.VMEM((2 * rows, feat), F32)
    all_shifts = range(1, spans)

    mine = jnp.where(core == 0, w_self[0], w_neigh[0])
    left, right, far = (shift(mine, "layer", s) for s in (1, -1, 2))
    pick, outgoing, features_0, vals, pick_far = run(
        pre_kernel,
        "gather_rows",
        scalars,
        [
            (features, of_span((rows, feat))),
            (send_rows.reshape(spans, peers, slots).swapaxes(1, 2), of_span((slots, peers))),
            (send_counts.reshape(spans, 1, peers), of_span((1, peers))),
            (
                tile_vals.reshape(spans, tiles, degree, size, size),
                of_span((tiles, degree, size, size)),
            ),
        ],
        [
            near((peers * slots, rows)),
            act,
            act,
            near((tiles, degree, size, size)),
            far_block((peers * slots, rows)),
        ],
        flops=10**8,
        moved=10**6,
    )
    arrived = exchange(outgoing.reshape(peers, slots, feat))
    arrived, left, right, far = tie(arrived, left, right, far)
    sources = [w_self[0], w_neigh[0], left, sibling(left), right, sibling(right)]
    sources += [far, sibling(far)]
    weight = near((2, feat, feat))

    hidden, aggs, pres, weights = [features_0], [], [], []
    top = spans - 1
    stack = (pltpu.HBM((spans, rows, feat), BF), FAR)
    buf_sem = pltpu.SemaphoreType.DMA
    acts_buf = None
    for layer in range(top):
        ins = [hidden[layer], arrived.reshape(rows, feat), vals, pick, *sources]
        if layer:
            ins.append(weights[layer])
        if layer > 1:
            ins.append((acts_buf, FAR))
        agg, pre, hid, outgoing, arranged, last = run(
            functools.partial(forward_kernel, layer),
            f"layer_forward_{layer}",
            scalars,
            ins,
            [act, wide, act, act, weight, stack if layer else weight],
            [ext_scratch, buf_sem, pltpu.SemaphoreType.DMA((2, 2))],
            {len(ins) - 1: 5} if layer > 1 else None,
            flops=6 * 10**8,
            moved=4 * 10**6,
        )
        if layer:
            acts_buf = last
        else:
            weights.append(last)
        weights.append(arranged)
        hidden.append(hid)
        aggs.append(agg)
        pres.append(pre)
        arrived = exchange(outgoing.reshape(peers, slots, feat))

    ins = [
        hidden[top],
        arrived.reshape(rows, feat),
        vals,
        w_out.T,
        labels,
        train_mask,
        weights[top],
        (acts_buf, FAR),
    ]
    remote, part, keep, send, acts_buf = run(
        functools.partial(top_kernel, top),
        "top_layer",
        scalars,
        ins,
        [near((peers, slots, feat)), wide, square, square, stack],
        [
            pltpu.VMEM((rows, feat), BF),
            ext_scratch,
            d_ext_scratch,
            buf_sem,
        ],
        {len(ins) - 1: 4},
        flops=10**9,
        moved=5 * 10**6,
    )

    def travel(buf):
        return [shift(buf[s], "layer", s) for s in all_shifts]

    first_block = pl.BlockSpec((None, rows, feat), lambda i, ids, cols: (0, 0, 0))

    def put_home(buf, *pieces):
        shape = (1, spans, rows, feat)
        return run(
            home_kernel,
            "put_home",
            scalars,
            [(buf, first_block), *pieces],
            [far_block(shape)],
            moved=2 * 10**6,
        )[0]

    chunk_rows = feat // peers
    pairs, grads_buf = [], None
    for layer in range(top - 1, 0, -1):
        returned, send = tie(exchange(remote), send)
        pairs.append((keep, sibling(send)))
        carry = layer < top - 1
        width = slots + chunk_rows * carry
        ins = [
            returned,
            part,
            pres[layer],
            hidden[layer],
            aggs[layer],
            vals,
            pick,
            weights[layer],
        ]
        aliases = None
        if carry:
            ins += [*pairs[-2], (grads_buf, FAR)]
            aliases = {len(ins) - 1: 2}
        remote, part, grads_buf, keep, send = run(
            functools.partial(backward_kernel, layer, carry),
            f"layer_backward_{layer}",
            scalars,
            ins,
            [near((peers, width, feat)), wide, stack, square, square],
            [pltpu.VMEM((rows, feat), BF), d_ext_scratch, buf_sem],
            aliases,
            flops=10**9,
            moved=5 * 10**6,
        )
        remote, recv = tie(remote, pairs[-1][1])
        pairs[-1] = (pairs[-1][0], recv)

    returned, send = tie(exchange(remote), send)
    recv_1, keep_1 = sibling(send), keep
    chunk_shape = (2, chunk_rows, feat)
    d_pre, grads_buf, keep, send, c_3 = run(
        last_slope_kernel,
        "last_slope",
        scalars,
        [returned, part, pres[0], hidden[0], aggs[0], pick, (grads_buf, FAR)],
        [act, stack, square, square, near(chunk_shape)],
        [pltpu.VMEM((rows, feat), BF), buf_sem],
        {6: 1},
        flops=4 * 10**8,
        moved=3 * 10**6,
    )
    d_pre, recv_1, send = tie(d_pre, recv_1, send)
    recv = sibling(send)
    width = slots + 3 * chunk_rows
    operand = (pltpu.HBM((peers, width, feat), BF), FAR)
    sums_out = (pltpu.HBM((spans, *chunk_shape), BF), FAR)
    remote, part, sums = run(
        last_spread_kernel,
        "last_spread",
        scalars,
        [d_pre, vals, weights[0], *pairs[-1], keep_1, recv_1, c_3],
        [operand, (pltpu.HBM((rows, feat), F32), FAR), sums_out],
        [
            d_ext_scratch,
            pltpu.VMEM((rows, feat), F32),
            pltpu.VMEM((peers, 2 * chunk_rows, feat), BF),
            pltpu.VMEM((peers, slots, feat), BF),
            pltpu.SemaphoreType.DMA((4,)),
        ],
        flops=5 * 10**8,
        moved=4 * 10**6,
    )
    remote, recv = tie(remote, recv)
    joined = run(
        join_kernel,
        "join_rows",
        scalars,
        [keep, recv, (remote, FAR)],
        [operand],
        [pltpu.VMEM((peers, chunk_rows, feat), BF), buf_sem],
        aliases={2: 0},
        moved=2 * 10**6,
    )[0]
    joined, acts_buf = tie(joined, acts_buf)
    acts = travel(acts_buf)
    layer_acts = put_home(acts_buf, *acts)
    returned, layer_acts = tie(exchange(joined), layer_acts)
    sums = run(
        chunk_kernel,
        "sum_chunks",
        scalars,
        [returned, (sums, FAR)],
        [sums_out],
        [pltpu.VMEM((3, *chunk_shape), BF), buf_sem],
        aliases={1: 0},
        moved=10**6,
    )[0]
    sums = lax.all_to_all(sums, "layer", split_axis=0, concat_axis=0, tiled=True)
    grads_buf = run(
        end_kernel,
        "input_grads",
        scalars,
        [
            returned,
            (part, whole((rows, feat))),
            (pick_far, whole(pick_far.shape)),
            (grads_buf, FAR),
        ],
        [stack],
        [pltpu.VMEM((rows, feat), BF), buf_sem],
        {3: 0},
        flops=10**8,
        moved=10**6,
    )[0]
    sums, *to_send = tie(sums, *[grads_buf[s] for s in all_shifts])
    spread = run(
        layer_sum_kernel,
        "sum_over_layer",
        scalars,
        [sums],
        [far_block((peers, chunk_rows, feat))],
        moved=10**6,
    )[0]
    grads = [shift(v, "layer", s) for s, v in zip(all_shifts, to_send)]
    gathered, *grads = tie(exchange(spread), *grads)
    gathered = gathered.reshape(feat, feat)
    other = sibling(gathered)
    act_grads = put_home(grads_buf, *grads)
    out_square = (1, feat, feat)
    grad_self, grad_neigh = run(
        functools.partial(scale_kernel, scale),
        "scale_grads",
        scalars,
        [gathered, other],
        [(pltpu.HBM(out_square, F32), whole(out_square))] * 2,
        moved=3 * 10**6,
    )
    return (layer_acts, act_grads, grad_self, grad_neigh)


def solution(mesh):
    in_specs = (
        P(None, "node", None),
        P("layer", None, None),
        P("layer", None, None),
        P(),
        P(None, "node"),
        P(None, "node"),
        P(None, "node", None, None),
        P(None, "node", None, None, None, None),
        P(None, "node", None, None),
        P(None, "node", None),
    )
    out_specs = (
        P("layer", None, "node", None),
        P("layer", None, "node", None),
        P("layer", None, None),
        P("layer", None, None),
    )
    return jax.shard_map(body, mesh=mesh, in_specs=in_specs, out_specs=out_specs, check_vma=False)
```

```python
import functools

import jax
import jax.numpy as jnp
from jax import lax
from jax.experimental import pallas as pl
from jax.experimental.pallas import tpu as pltpu
from jax.sharding import PartitionSpec as P

BF = jnp.bfloat16
F32 = jnp.float32
NN = (((1,), (0,)), ((), ()))
NT = (((1,), (1,)), ((), ()))
TN = (((0,), (0,)), ((), ()))
FAR = pl.BlockSpec(memory_space=pltpu.HBM)
LOCAL = pl.BlockSpec(memory_space=pltpu.VMEM)
VMEM_BYTES = 16 * 1024 * 1024


def dot(a, b, dims=NN):
    return lax.dot_general(a, b, dims, preferred_element_type=F32)


def shift(value, axis, steps):
    count = lax.axis_size(axis)
    return lax.ppermute(value, axis, [(i, (i + steps) % count) for i in range(count)])


def sibling(value):
    count = lax.axis_size("node")
    return lax.ppermute(value, "node", [(i, i ^ 1) for i in range(count)])


def exchange(value):
    return lax.all_to_all(value, "node", split_axis=0, concat_axis=0, tiled=True)


def of_span(shape):
    return pl.BlockSpec((None, *shape), lambda i, ids: (ids[0], *((0,) * len(shape))))


def whole(shape):
    return pl.BlockSpec(shape, lambda i, ids: (0,) * len(shape))


def near(shape, dtype=BF):
    return pltpu.VMEM(shape, dtype), LOCAL


def far_block(shape, dtype=BF):
    return pltpu.HBM(shape, dtype), whole(shape)


def run(kernel, name, scalars, ins, outs, scratch=(), aliases=None, flops=0, moved=0):
    ins = [v if isinstance(v, tuple) else (v, LOCAL) for v in ins]
    arrays = [
        pltpu.with_memory_space_constraint(a, pltpu.VMEM if s is LOCAL else pltpu.HBM)
        for a, s in ins
    ]
    return pl.pallas_call(
        kernel,
        name=name,
        grid_spec=pltpu.PrefetchScalarGridSpec(
            num_scalar_prefetch=1,
            grid=(1,),
            in_specs=[s for _, s in ins],
            out_specs=[s for _, s in outs],
            scratch_shapes=list(scratch),
        ),
        out_shape=[o for o, _ in outs],
        input_output_aliases={} if aliases is None else {k + 1: v for k, v in aliases.items()},
        compiler_params=pltpu.CompilerParams(vmem_limit_bytes=VMEM_BYTES),
        cost_estimate=pl.CostEstimate(flops=flops, bytes_accessed=moved, transcendentals=0),
    )(scalars, *arrays)


def tie(*values):
    return lax.optimization_barrier(values)


def weight_copies(layer, ids, w_refs, w_scr, sems, act):
    own_s, own_n, left, left_x, right, right_x, far, far_x = w_refs
    core = ids[1]
    pairs = [
        [(own_s, 0), (own_n, 1)],
        [(right, core), (right_x, 1 - core)],
        [(far, core), (far_x, 1 - core)],
        [(left, core), (left_x, 1 - core)],
    ]
    which = lax.rem(layer - ids[0] + 4, 4)
    for option, pair in enumerate(pairs):

        @pl.when(which == option)
        def _():
            for n, (ref, place) in enumerate(pair):
                act(pltpu.make_async_copy(ref, w_scr.at[place], sems.at[n]))


def start_weights(*args):
    weight_copies(*args, lambda copy: copy.start())


def wait_weights(*args):
    weight_copies(*args, lambda copy: copy.wait())


def side_by_side(vals_ref, r, degree):
    return jnp.concatenate([vals_ref[r, j] for j in range(degree)], axis=1)


def aggregate_rows(ids, vals_ref, ext):
    tiles, degree, size = vals_ref.shape[0], vals_ref.shape[1], vals_ref.shape[2]
    parts = []
    for r in range(tiles):
        picked = jnp.concatenate(
            [ext[pl.ds(pl.multiple_of(ids[2 + r * degree + j] * size, size), size), :] for j in range(degree)],
            axis=0,
        )
        parts.append(dot(side_by_side(vals_ref, r, degree), picked))
    return jnp.concatenate(parts, axis=0).astype(BF)


def spread_rows(ids, vals_ref, d_agg, d_ext):
    tiles, degree, size = vals_ref.shape[0], vals_ref.shape[1], vals_ref.shape[2]
    d_ext[...] = jnp.zeros_like(d_ext)
    for r in range(tiles):
        pieces = dot(side_by_side(vals_ref, r, degree), d_agg[r * size : (r + 1) * size], TN)
        for j in range(degree):
            rows = pl.ds(pl.multiple_of(ids[2 + r * degree + j] * size, size), size)
            d_ext[rows, :] += pieces[j * size : (j + 1) * size]


def to_slot(value_ref, layer, ids, buf_ref, sem):
    return pltpu.make_async_copy(value_ref, buf_ref.at[lax.rem(layer - ids[0] + 4, 4)], sem)


def sigmoid(v):
    return 1.0 / (1.0 + jnp.exp(-v))


def pre_kernel(ids, h_ref, rows_ref, counts_ref, vals_ref, pick_ref, out_ref, h_out, vals_out, pick_far):
    slots, peers = rows_ref.shape
    total, node_rows = pick_ref.shape
    bits = slots.bit_length() - 1
    slot = lax.broadcasted_iota(jnp.int32, (total, peers), 0)
    owner = lax.broadcasted_iota(jnp.int32, (total, peers), 1)
    mine = lax.shift_right_logical(slot, bits) == owner
    wide = dot(mine.astype(F32).astype(BF), rows_ref[...].astype(F32).astype(BF), NT)
    slot_k = lax.broadcasted_iota(jnp.int32, (total, slots), 0) & (slots - 1)
    in_slot = slot_k == lax.broadcasted_iota(jnp.int32, (total, slots), 1)
    row = jnp.sum(jnp.where(in_slot, wide, 0.0), axis=1, keepdims=True)
    counts = jnp.broadcast_to(counts_ref[...].astype(F32), (total, peers))
    count = jnp.sum(jnp.where(mine, counts, 0.0), axis=1, keepdims=True)
    k = (lax.broadcasted_iota(jnp.int32, (total, 1), 0) & (slots - 1)).astype(F32)
    row = jnp.where(k < count, row, -1.0)
    place = lax.broadcasted_iota(jnp.int32, (total, node_rows), 1).astype(F32)
    pick = (place == row).astype(F32).astype(BF)
    pick_ref[...] = pick
    pick_far[...] = pick
    out_ref[...] = dot(pick, h_ref[...]).astype(BF)
    h_out[...] = h_ref[...]
    vals_out[...] = vals_ref[...]


def forward_math(ids, h_ref, arr_ref, vals_ref, w_ref, ext, ready=None):
    rows = h_ref.shape[0]
    ext[0:rows, :] = h_ref[...]
    ext[rows : 2 * rows, :] = arr_ref[...]
    agg = aggregate_rows(ids, vals_ref, ext)
    if ready is not None:
        ready()
    pre = dot(h_ref[...], w_ref[0]) + dot(agg, w_ref[1])
    sig = sigmoid(pre)
    return agg, pre, sig, (pre * sig).astype(BF)


def forward_kernel(layer, ids, h_ref, arr_ref, vals_ref, pick_ref, *rest):
    w_refs, rest = rest[:8], rest[8:]
    first = layer == 0
    if first:
        agg_ref, pre_ref, hid_ref, out_ref, next_ref, w_ref = rest[:6]
    else:
        w_ref, *rest = rest[0:1] + rest[1 + (layer > 1) :]
        agg_ref, pre_ref, hid_ref, out_ref, next_ref, buf_ref = rest[:6]
    ext, buf_sem, sems = rest[-3:]
    if not first:
        copy = to_slot(h_ref, layer - 1, ids, buf_ref, buf_sem)
        copy.start()
    ready = None
    if first:
        here = (layer, ids, w_refs, w_ref, sems.at[0])
        start_weights(*here)
        ready = lambda: wait_weights(*here)
    ahead = (layer + 1, ids, w_refs, next_ref, sems.at[1])
    start_weights(*ahead)
    agg, pre, _, hid = forward_math(ids, h_ref, arr_ref, vals_ref, w_ref, ext, ready)
    hid_ref[...] = hid
    out_ref[...] = dot(pick_ref[...], hid).astype(BF)
    agg_ref[...] = agg
    pre_ref[...] = pre
    if not first:
        copy.wait()
    wait_weights(*ahead)


def backward_math(ids, d_pre, vals_ref, w_ref, d_ext):
    d_agg = dot(d_pre, w_ref[1], NT).astype(BF)
    spread_rows(ids, vals_ref, d_agg, d_ext)
    return dot(d_pre, w_ref[0], NT)


def weight_partials(ids, h_ref, agg, d_pre, keep_ref, send_ref):
    on_rows = dot(h_ref[...], d_pre, TN).astype(BF)
    on_agg = dot(agg, d_pre, TN).astype(BF)

    @pl.when(ids[1] == 0)
    def _():
        keep_ref[...] = on_rows
        send_ref[...] = on_agg

    @pl.when(ids[1] != 0)
    def _():
        keep_ref[...] = on_agg
        send_ref[...] = on_rows


def top_kernel(layer, ids, h_ref, arr_ref, vals_ref, wout_ref, lab_ref, mask_ref, w_ref, *rest):
    remote_ref, part_ref, keep_ref, send_ref, buf_ref, hid_ref, ext, d_ext, buf_sem = rest[1:]
    copy = to_slot(h_ref, layer - 1, ids, buf_ref, buf_sem)
    copy.start()
    rows = h_ref.shape[0]
    agg, pre, sig, hid = forward_math(ids, h_ref, arr_ref, vals_ref, w_ref, ext)
    hid_ref[...] = hid
    last = to_slot(hid_ref, layer, ids, buf_ref, buf_sem)
    copy.wait()
    last.start()
    logits = dot(wout_ref[...], hid, NT)
    expo = jnp.exp(logits)
    probs = expo / jnp.sum(expo, axis=0, keepdims=True)
    label = lab_ref[pl.ds(ids[0], 1), :]
    onehot = (label == lax.broadcasted_iota(jnp.int32, logits.shape, 0)).astype(F32)
    live = mask_ref[pl.ds(ids[0], 1), :].astype(F32)
    g_logits = (live * (probs - onehot)).astype(BF)
    d_out = dot(g_logits, wout_ref[...], TN).astype(BF)
    d_pre = (d_out.astype(F32) * (sig * (1.0 + pre * (1.0 - sig)))).astype(BF)
    back = backward_math(ids, d_pre, vals_ref, w_ref, d_ext)
    remote_ref[...] = d_ext[rows : 2 * rows, :].astype(BF).reshape(remote_ref.shape)
    part_ref[...] = back + d_ext[0:rows, :]
    weight_partials(ids, h_ref, agg, d_pre, keep_ref, send_ref)
    last.wait()


def chunk_sum(block):
    total = block[0:2].astype(F32)
    for n in range(2, block.shape[0], 2):
        total = total + block[n : n + 2].astype(F32)
    return total


def slope_math(ids, layer, ret_ref, part_in, pre_ref, pick_ref, dout_ref, buf_ref, buf_sem):
    rows, feat = part_in.shape
    returned = ret_ref[:, 0 : rows // ret_ref.shape[0], :].reshape(rows, feat)
    d_out = (part_in[...] + dot(pick_ref[...], returned, TN)).astype(BF)
    dout_ref[...] = d_out
    copy = to_slot(dout_ref, layer + 1, ids, buf_ref, buf_sem)
    copy.start()
    pre = pre_ref[...]
    sig = sigmoid(pre)
    return (d_out.astype(F32) * (sig * (1.0 + pre * (1.0 - sig)))).astype(BF), copy


def backward_kernel(layer, carry, ids, ret_ref, part_in, pre_ref, h_ref, agg_ref, *rest):
    (vals_ref, pick_ref, w_ref), rest = rest[:3], rest[3:]
    if carry:
        keep_in, recv_in, rest = rest[0], rest[1], rest[3:]
    out_ref, part_ref, buf_ref, keep_ref, send_ref, dout_ref, d_ext, buf_sem = rest
    rows, feat = part_in.shape
    d_pre, copy = slope_math(
        ids, layer, ret_ref, part_in, pre_ref, pick_ref, dout_ref, buf_ref, buf_sem
    )
    back = backward_math(ids, d_pre, vals_ref, w_ref, d_ext)
    peers, slots = out_ref.shape[0], rows // out_ref.shape[0]
    out_ref[:, 0:slots, :] = d_ext[rows : 2 * rows, :].astype(BF).reshape(peers, slots, feat)
    if carry:
        put_carry(keep_in, recv_in, out_ref, slots)
    part_ref[...] = back + d_ext[0:rows, :]
    weight_partials(ids, h_ref, agg_ref[...], d_pre, keep_ref, send_ref)
    copy.wait()


def last_slope_kernel(
    ids, ret_ref, part_in, pre_ref, h_ref, agg_ref, pick_ref, buf_in,
    dpre_ref, buf_ref, keep_ref, send_ref, chunk_ref, dout_ref, buf_sem,
):
    d_pre, copy = slope_math(
        ids, 0, ret_ref, part_in, pre_ref, pick_ref, dout_ref, buf_ref, buf_sem
    )
    dpre_ref[...] = d_pre
    weight_partials(ids, h_ref, agg_ref[...], d_pre, keep_ref, send_ref)
    slots = part_in.shape[0] // ret_ref.shape[0]
    chunk_ref[...] = chunk_sum(ret_ref[:, slots:, :]).astype(BF)
    copy.wait()


def last_spread_kernel(
    ids, dpre_ref, vals_ref, w_ref, keep_a, recv_a, keep_b, recv_b, c_in,
    out_ref, part_ref, local_ref, c_ref, d_ext, carried, sems,
):
    rows, feat = dpre_ref.shape
    peers, slots = local_ref.shape[0], local_ref.shape[1]
    size = keep_a.shape[0] // peers
    copies = [
        pltpu.make_async_copy(c_in, c_ref.at[3], sems.at[0]),
        pltpu.make_async_copy(
            carried, out_ref.at[:, pl.ds(slots, 2 * size), :], sems.at[1]
        ),
    ]
    copies[0].start()
    put_carry(keep_a, recv_a, carried, 0)
    put_carry(keep_b, recv_b, carried, size)
    copies[1].start()
    back = backward_math(ids, dpre_ref[...], vals_ref, w_ref, d_ext)
    local_ref[...] = d_ext[rows : 2 * rows, :].astype(BF).reshape(local_ref.shape)
    part_ref[...] = back + d_ext[0:rows, :]
    for copy in copies:
        copy.wait()


def put_carry(keep_ref, recv_ref, out_ref, first):
    peers, feat = out_ref.shape[0], out_ref.shape[2]
    size = keep_ref.shape[0] // peers
    total = (keep_ref[...].astype(F32) + recv_ref[...].astype(F32)).astype(BF)
    out_ref[:, first : first + size, :] = total.reshape(peers, size, feat)


def join_kernel(ids, keep_ref, recv_ref, local_ref, part_ref, buf_in, out_ref, part_out, both, sems):
    size, slots = both.shape[1], local_ref.shape[1]
    first = out_ref.shape[1] - size
    copies = [
        pltpu.make_async_copy(part_ref, part_out, sems.at[0]),
        pltpu.make_async_copy(local_ref, out_ref.at[:, pl.ds(0, slots), :], sems.at[1]),
        pltpu.make_async_copy(both, out_ref.at[:, pl.ds(first, size), :], sems.at[2]),
    ]
    copies[0].start()
    copies[1].start()
    put_carry(keep_ref, recv_ref, both, 0)
    copies[2].start()
    for copy in copies:
        copy.wait()


def chunk_kernel(ids, ret_ref, buf_in, out_ref, sums, sem):
    size = sums.shape[2]
    slots = ret_ref.shape[1] - 3 * size
    for n, layer in enumerate((2, 1, 0)):
        first = slots + n * size
        sums[layer] = chunk_sum(ret_ref[:, first : first + size, :]).astype(BF)
    copy = pltpu.make_async_copy(sums, out_ref.at[pl.ds(0, 3)], sem)
    copy.start()
    copy.wait()


def end_kernel(ids, ret_ref, part_in, pick_ref, buf_in, buf_ref, dout_ref, buf_sem):
    rows, feat = part_in.shape
    returned = ret_ref[:, 0 : rows // ret_ref.shape[0], :].reshape(rows, feat)
    dout_ref[...] = (part_in[...] + dot(pick_ref[...], returned, TN)).astype(BF)
    copy = to_slot(dout_ref, 0, ids, buf_ref, buf_sem)
    copy.start()
    copy.wait()


def layer_sum_kernel(ids, sums_ref, out_ref):
    total = sums_ref[0].astype(F32)
    for span in range(1, sums_ref.shape[0]):
        total = total + sums_ref[span].astype(F32)
    total = total.astype(BF)
    for n in range(0, out_ref.shape[0], 2):
        out_ref[n : n + 2] = total


def scale_kernel(scale, ids, mine_ref, other_ref, self_ref, neigh_ref, mine, other, sems):
    core = ids[1]
    size = mine_ref.shape[0] // 4
    for step in range(4):
        rows = pl.ds(step * size, size)
        mine[rows, :] = mine_ref[rows, :].astype(F32) * scale
        other[rows, :] = other_ref[rows, :].astype(F32) * scale
        for value, place, sem in ((mine, core, 0), (other, 1 - core, 1)):
            for target, out_ref in enumerate((self_ref, neigh_ref)):

                @pl.when(place == target)
                def _():
                    pltpu.make_async_copy(
                        value.at[rows], out_ref.at[0, rows], sems.at[sem, step]
                    ).start()

    for step in range(4):
        rows = pl.ds(step * size, size)
        for value, sem in ((mine, 0), (other, 1)):
            pltpu.make_async_copy(value.at[rows], self_ref.at[0, rows], sems.at[sem, step]).wait()


def home_kernel(ids, *refs):
    pieces, out_ref = refs[:-1], refs[-1]
    for s, piece in enumerate(pieces):
        out_ref[0, lax.rem(ids[0] + 4 - s, 4)] = piece[...]


def body(
    features,
    w_self,
    w_neigh,
    w_out,
    labels,
    train_mask,
    tile_cols,
    tile_vals,
    send_rows,
    send_counts,
):
    home = lax.axis_index("layer")
    node = lax.axis_index("node")
    core = lax.rem(node, 2)
    spans, rows, feat = features.shape
    peers, slots = send_rows.shape[2], send_rows.shape[3]
    tiles, degree, size = tile_vals.shape[2], tile_vals.shape[3], tile_vals.shape[4]
    scale = 1.0 / (spans * rows * peers)
    own_cols = lax.dynamic_index_in_dim(tile_cols.reshape(spans, tiles * degree), home, 0, False)
    scalars = jnp.concatenate([jnp.stack([home, core]).astype(jnp.int32), own_cols])
    act, wide, square = near((rows, feat)), near((rows, feat), F32), near((feat, feat))
    ext_scratch = pltpu.VMEM((2 * rows, feat), BF)
    d_ext_scratch = pltpu.VMEM((2 * rows, feat), F32)
    all_shifts = range(1, spans)

    mine = jnp.where(core == 0, w_self[0], w_neigh[0])
    left, right, far = (shift(mine, "layer", s) for s in (1, -1, 2))
    pick, outgoing, features_0, vals, pick_far = run(
        pre_kernel,
        "gather_rows",
        scalars,
        [
            (features, of_span((rows, feat))),
            (send_rows.reshape(spans, peers, slots).swapaxes(1, 2), of_span((slots, peers))),
            (send_counts.reshape(spans, 1, peers), of_span((1, peers))),
            (
                tile_vals.reshape(spans, tiles, degree, size, size),
                of_span((tiles, degree, size, size)),
            ),
        ],
        [
            near((peers * slots, rows)),
            act,
            act,
            near((tiles, degree, size, size)),
            far_block((peers * slots, rows)),
        ],
        flops=10**8,
        moved=10**6,
    )
    arrived = exchange(outgoing.reshape(peers, slots, feat))
    arrived, left, right, far = tie(arrived, left, right, far)
    sources = [w_self[0], w_neigh[0], left, sibling(left), right, sibling(right)]
    sources += [far, sibling(far)]
    weight = near((2, feat, feat))

    hidden, aggs, pres, weights = [features_0], [], [], []
    top = spans - 1
    stack = (pltpu.HBM((spans, rows, feat), BF), FAR)
    buf_sem = pltpu.SemaphoreType.DMA
    acts_buf = None
    for layer in range(top):
        ins = [hidden[layer], arrived.reshape(rows, feat), vals, pick, *sources]
        if layer:
            ins.append(weights[layer])
        if layer > 1:
            ins.append((acts_buf, FAR))
        agg, pre, hid, outgoing, arranged, last = run(
            functools.partial(forward_kernel, layer),
            f"layer_forward_{layer}",
            scalars,
            ins,
            [act, wide, act, act, weight, stack if layer else weight],
            [ext_scratch, buf_sem, pltpu.SemaphoreType.DMA((2, 2))],
            {len(ins) - 1: 5} if layer > 1 else None,
            flops=6 * 10**8,
            moved=4 * 10**6,
        )
        if layer:
            acts_buf = last
        else:
            weights.append(last)
        weights.append(arranged)
        hidden.append(hid)
        aggs.append(agg)
        pres.append(pre)
        arrived = exchange(outgoing.reshape(peers, slots, feat))

    ins = [
        hidden[top],
        arrived.reshape(rows, feat),
        vals,
        w_out.T,
        labels,
        train_mask,
        weights[top],
        (acts_buf, FAR),
    ]
    remote, part, keep, send, acts_buf = run(
        functools.partial(top_kernel, top),
        "top_layer",
        scalars,
        ins,
        [near((peers, slots, feat)), wide, square, square, stack],
        [
            pltpu.VMEM((rows, feat), BF),
            ext_scratch,
            d_ext_scratch,
            buf_sem,
        ],
        {len(ins) - 1: 4},
        flops=10**9,
        moved=5 * 10**6,
    )

    def travel(buf):
        return [shift(buf[s], "layer", s) for s in all_shifts]

    first_block = pl.BlockSpec((None, rows, feat), lambda i, ids: (0, 0, 0))

    def put_home(buf, *pieces):
        shape = (1, spans, rows, feat)
        return run(
            home_kernel,
            "put_home",
            scalars,
            [(buf, first_block), *pieces],
            [far_block(shape)],
            moved=2 * 10**6,
        )[0]

    chunk_rows = feat // peers
    pairs, grads_buf = [], None
    for layer in range(top - 1, 0, -1):
        returned, send = tie(exchange(remote), send)
        pairs.append((keep, sibling(send)))
        carry = layer < top - 1
        width = slots + chunk_rows * carry
        ins = [
            returned,
            part,
            pres[layer],
            hidden[layer],
            aggs[layer],
            vals,
            pick,
            weights[layer],
        ]
        aliases = None
        if carry:
            ins += [*pairs[-2], (grads_buf, FAR)]
            aliases = {len(ins) - 1: 2}
        remote, part, grads_buf, keep, send = run(
            functools.partial(backward_kernel, layer, carry),
            f"layer_backward_{layer}",
            scalars,
            ins,
            [near((peers, width, feat)), wide, stack, square, square],
            [pltpu.VMEM((rows, feat), BF), d_ext_scratch, buf_sem],
            aliases,
            flops=10**9,
            moved=5 * 10**6,
        )
        remote, recv = tie(remote, pairs[-1][1])
        pairs[-1] = (pairs[-1][0], recv)

    returned, send = tie(exchange(remote), send)
    recv_1, keep_1 = sibling(send), keep
    chunk_shape = (2, chunk_rows, feat)
    d_pre, grads_buf, keep, send, c_3 = run(
        last_slope_kernel,
        "last_slope",
        scalars,
        [returned, part, pres[0], hidden[0], aggs[0], pick, (grads_buf, FAR)],
        [act, stack, square, square, near(chunk_shape)],
        [pltpu.VMEM((rows, feat), BF), buf_sem],
        {6: 1},
        flops=4 * 10**8,
        moved=3 * 10**6,
    )
    d_pre, recv_1, send = tie(d_pre, recv_1, send)
    recv = sibling(send)
    width = slots + 3 * chunk_rows
    operand = (pltpu.HBM((peers, width, feat), BF), FAR)
    sums_out = (pltpu.HBM((spans, *chunk_shape), BF), FAR)
    remote, part, local, sums = run(
        last_spread_kernel,
        "last_spread",
        scalars,
        [d_pre, vals, weights[0], *pairs[-1], keep_1, recv_1, c_3],
        [operand, wide, near((peers, slots, feat)), sums_out],
        [
            d_ext_scratch,
            pltpu.VMEM((peers, 2 * chunk_rows, feat), BF),
            pltpu.SemaphoreType.DMA((2,)),
        ],
        flops=5 * 10**8,
        moved=4 * 10**6,
    )
    remote, recv = tie(remote, recv)
    joined, part = run(
        join_kernel,
        "join_rows",
        scalars,
        [keep, recv, local, part, (remote, FAR)],
        [operand, (pltpu.HBM((rows, feat), F32), FAR)],
        [pltpu.VMEM((peers, chunk_rows, feat), BF), pltpu.SemaphoreType.DMA((3,))],
        aliases={4: 0},
        moved=2 * 10**6,
    )
    joined, acts_buf = tie(joined, acts_buf)
    acts = travel(acts_buf)
    layer_acts = put_home(acts_buf, *acts)
    returned, layer_acts = tie(exchange(joined), layer_acts)
    sums = run(
        chunk_kernel,
        "sum_chunks",
        scalars,
        [returned, (sums, FAR)],
        [sums_out],
        [pltpu.VMEM((3, *chunk_shape), BF), buf_sem],
        aliases={1: 0},
        moved=10**6,
    )[0]
    sums = lax.all_to_all(sums, "layer", split_axis=0, concat_axis=0, tiled=True)
    grads_buf = run(
        end_kernel,
        "input_grads",
        scalars,
        [
            returned,
            (part, whole((rows, feat))),
            (pick_far, whole(pick_far.shape)),
            (grads_buf, FAR),
        ],
        [stack],
        [pltpu.VMEM((rows, feat), BF), buf_sem],
        {3: 0},
        flops=10**8,
        moved=10**6,
    )[0]
    sums, *to_send = tie(sums, *[grads_buf[s] for s in all_shifts])
    spread = run(
        layer_sum_kernel,
        "sum_over_layer",
        scalars,
        [sums],
        [far_block((peers, chunk_rows, feat))],
        moved=10**6,
    )[0]
    grads = [shift(v, "layer", s) for s, v in zip(all_shifts, to_send)]
    gathered, *grads = tie(exchange(spread), *grads)
    gathered = gathered.reshape(feat, feat)
    other = sibling(gathered)
    act_grads = put_home(grads_buf, *grads)
    out_square = (1, feat, feat)
    grad_self, grad_neigh = run(
        functools.partial(scale_kernel, scale),
        "scale_grads",
        scalars,
        [gathered, other],
        [(pltpu.HBM(out_square, F32), FAR)] * 2,
        [pltpu.VMEM((feat, feat), F32)] * 2 + [pltpu.SemaphoreType.DMA((2, 4))],
        moved=3 * 10**6,
    )
    return (layer_acts, act_grads, grad_self, grad_neigh)


def solution(mesh):
    in_specs = (
        P(None, "node", None),
        P("layer", None, None),
        P("layer", None, None),
        P(),
        P(None, "node"),
        P(None, "node"),
        P(None, "node", None, None),
        P(None, "node", None, None, None, None),
        P(None, "node", None, None),
        P(None, "node", None),
    )
    out_specs = (
        P("layer", None, "node", None),
        P("layer", None, "node", None),
        P("layer", None, None),
        P("layer", None, None),
    )
    return jax.shard_map(body, mesh=mesh, in_specs=in_specs, out_specs=out_specs, check_vma=False)
```

```python
import functools

import jax
import jax.numpy as jnp
from jax import lax
from jax.experimental import pallas as pl
from jax.experimental.pallas import tpu as pltpu
from jax.sharding import PartitionSpec as P

BF = jnp.bfloat16
F32 = jnp.float32
NN = (((1,), (0,)), ((), ()))
NT = (((1,), (1,)), ((), ()))
TN = (((0,), (0,)), ((), ()))
FAR = pl.BlockSpec(memory_space=pltpu.HBM)
LOCAL = pl.BlockSpec(memory_space=pltpu.VMEM)
VMEM_BYTES = 16 * 1024 * 1024


def dot(a, b, dims=NN):
    return lax.dot_general(a, b, dims, preferred_element_type=F32)


def shift(value, axis, steps):
    count = lax.axis_size(axis)
    return lax.ppermute(value, axis, [(i, (i + steps) % count) for i in range(count)])


def sibling(value):
    count = lax.axis_size("node")
    return lax.ppermute(value, "node", [(i, i ^ 1) for i in range(count)])


def exchange(value):
    return lax.all_to_all(value, "node", split_axis=0, concat_axis=0, tiled=True)


def of_span(shape):
    return pl.BlockSpec((None, *shape), lambda i, ids: (ids[0], *((0,) * len(shape))))


def whole(shape):
    return pl.BlockSpec(shape, lambda i, ids: (0,) * len(shape))


def near(shape, dtype=BF):
    return pltpu.VMEM(shape, dtype), LOCAL


def far_block(shape, dtype=BF):
    return pltpu.HBM(shape, dtype), whole(shape)


def run(kernel, name, scalars, ins, outs, scratch=(), aliases=None, flops=0, moved=0):
    ins = [v if isinstance(v, tuple) else (v, LOCAL) for v in ins]
    arrays = [
        pltpu.with_memory_space_constraint(a, pltpu.VMEM if s is LOCAL else pltpu.HBM)
        for a, s in ins
    ]
    return pl.pallas_call(
        kernel,
        name=name,
        grid_spec=pltpu.PrefetchScalarGridSpec(
            num_scalar_prefetch=1,
            grid=(1,),
            in_specs=[s for _, s in ins],
            out_specs=[s for _, s in outs],
            scratch_shapes=list(scratch),
        ),
        out_shape=[o for o, _ in outs],
        input_output_aliases={} if aliases is None else {k + 1: v for k, v in aliases.items()},
        compiler_params=pltpu.CompilerParams(vmem_limit_bytes=VMEM_BYTES),
        cost_estimate=pl.CostEstimate(flops=flops, bytes_accessed=moved, transcendentals=0),
    )(scalars, *arrays)


def tie(*values):
    return lax.optimization_barrier(values)


def weight_copies(layer, ids, w_refs, w_scr, sems, act):
    own_s, own_n, left, left_x, right, right_x, far, far_x = w_refs
    core = ids[1]
    pairs = [
        [(own_s, 0), (own_n, 1)],
        [(right, core), (right_x, 1 - core)],
        [(far, core), (far_x, 1 - core)],
        [(left, core), (left_x, 1 - core)],
    ]
    which = lax.rem(layer - ids[0] + 4, 4)
    for option, pair in enumerate(pairs):

        @pl.when(which == option)
        def _():
            for n, (ref, place) in enumerate(pair):
                act(pltpu.make_async_copy(ref, w_scr.at[place], sems.at[n]))


def start_weights(*args):
    weight_copies(*args, lambda copy: copy.start())


def wait_weights(*args):
    weight_copies(*args, lambda copy: copy.wait())


def side_by_side(vals_ref, r, degree):
    return jnp.concatenate([vals_ref[r, j] for j in range(degree)], axis=1)


def aggregate_rows(ids, vals_ref, ext):
    tiles, degree, size = vals_ref.shape[0], vals_ref.shape[1], vals_ref.shape[2]
    parts = []
    for r in range(tiles):
        picked = jnp.concatenate(
            [ext[pl.ds(pl.multiple_of(ids[2 + r * degree + j] * size, size), size), :] for j in range(degree)],
            axis=0,
        )
        parts.append(dot(side_by_side(vals_ref, r, degree), picked))
    return jnp.concatenate(parts, axis=0).astype(BF)


def spread_rows(ids, vals_ref, d_agg, d_ext):
    tiles, degree, size = vals_ref.shape[0], vals_ref.shape[1], vals_ref.shape[2]
    d_ext[...] = jnp.zeros_like(d_ext)
    for r in range(tiles):
        pieces = dot(side_by_side(vals_ref, r, degree), d_agg[r * size : (r + 1) * size], TN)
        for j in range(degree):
            rows = pl.ds(pl.multiple_of(ids[2 + r * degree + j] * size, size), size)
            d_ext[rows, :] += pieces[j * size : (j + 1) * size]


def to_slot(value_ref, layer, ids, buf_ref, sem):
    return pltpu.make_async_copy(value_ref, buf_ref.at[lax.rem(layer - ids[0] + 4, 4)], sem)


def sigmoid(v):
    return 1.0 / (1.0 + jnp.exp(-v))


def pre_kernel(ids, h_ref, rows_ref, counts_ref, vals_ref, pick_ref, out_ref, h_out, vals_out, pick_far):
    slots, peers = rows_ref.shape
    total, node_rows = pick_ref.shape
    bits = slots.bit_length() - 1
    slot = lax.broadcasted_iota(jnp.int32, (total, peers), 0)
    owner = lax.broadcasted_iota(jnp.int32, (total, peers), 1)
    mine = lax.shift_right_logical(slot, bits) == owner
    wide = dot(mine.astype(F32).astype(BF), rows_ref[...].astype(F32).astype(BF), NT)
    slot_k = lax.broadcasted_iota(jnp.int32, (total, slots), 0) & (slots - 1)
    in_slot = slot_k == lax.broadcasted_iota(jnp.int32, (total, slots), 1)
    row = jnp.sum(jnp.where(in_slot, wide, 0.0), axis=1, keepdims=True)
    counts = jnp.broadcast_to(counts_ref[...].astype(F32), (total, peers))
    count = jnp.sum(jnp.where(mine, counts, 0.0), axis=1, keepdims=True)
    k = (lax.broadcasted_iota(jnp.int32, (total, 1), 0) & (slots - 1)).astype(F32)
    row = jnp.where(k < count, row, -1.0)
    place = lax.broadcasted_iota(jnp.int32, (total, node_rows), 1).astype(F32)
    pick = (place == row).astype(F32).astype(BF)
    pick_ref[...] = pick
    pick_far[...] = pick
    out_ref[...] = dot(pick, h_ref[...]).astype(BF)
    h_out[...] = h_ref[...]
    vals_out[...] = vals_ref[...]


def forward_math(ids, h_ref, arr_ref, vals_ref, w_ref, ext, ready=None):
    rows = h_ref.shape[0]
    ext[0:rows, :] = h_ref[...]
    ext[rows : 2 * rows, :] = arr_ref[...]
    agg = aggregate_rows(ids, vals_ref, ext)
    if ready is not None:
        ready()
    pre = dot(h_ref[...], w_ref[0]) + dot(agg, w_ref[1])
    sig = sigmoid(pre)
    return agg, pre, sig, (pre * sig).astype(BF)


def forward_kernel(layer, ids, h_ref, arr_ref, vals_ref, pick_ref, *rest):
    w_refs, rest = rest[:8], rest[8:]
    first = layer == 0
    if first:
        agg_ref, pre_ref, hid_ref, out_ref, next_ref, w_ref = rest[:6]
    else:
        w_ref, *rest = rest[0:1] + rest[1 + (layer > 1) :]
        agg_ref, pre_ref, hid_ref, out_ref, next_ref, buf_ref = rest[:6]
    ext, buf_sem, sems = rest[-3:]
    if not first:
        copy = to_slot(h_ref, layer - 1, ids, buf_ref, buf_sem)
        copy.start()
    ready = None
    if first:
        here = (layer, ids, w_refs, w_ref, sems.at[0])
        start_weights(*here)
        ready = lambda: wait_weights(*here)
    ahead = (layer + 1, ids, w_refs, next_ref, sems.at[1])
    start_weights(*ahead)
    agg, pre, _, hid = forward_math(ids, h_ref, arr_ref, vals_ref, w_ref, ext, ready)
    hid_ref[...] = hid
    out_ref[...] = dot(pick_ref[...], hid).astype(BF)
    agg_ref[...] = agg
    pre_ref[...] = pre
    if not first:
        copy.wait()
    wait_weights(*ahead)


def backward_math(ids, d_pre, vals_ref, w_ref, d_ext):
    d_agg = dot(d_pre, w_ref[1], NT).astype(BF)
    spread_rows(ids, vals_ref, d_agg, d_ext)
    return dot(d_pre, w_ref[0], NT)


def weight_partials(ids, h_ref, agg, d_pre, keep_ref, send_ref):
    on_rows = dot(h_ref[...], d_pre, TN).astype(BF)
    on_agg = dot(agg, d_pre, TN).astype(BF)

    @pl.when(ids[1] == 0)
    def _():
        keep_ref[...] = on_rows
        send_ref[...] = on_agg

    @pl.when(ids[1] != 0)
    def _():
        keep_ref[...] = on_agg
        send_ref[...] = on_rows


def top_kernel(layer, ids, h_ref, arr_ref, vals_ref, wout_ref, lab_ref, mask_ref, w_ref, *rest):
    remote_ref, part_ref, keep_ref, send_ref, buf_ref, hid_ref, ext, d_ext, buf_sem = rest[1:]
    copy = to_slot(h_ref, layer - 1, ids, buf_ref, buf_sem)
    copy.start()
    rows = h_ref.shape[0]
    agg, pre, sig, hid = forward_math(ids, h_ref, arr_ref, vals_ref, w_ref, ext)
    hid_ref[...] = hid
    last = to_slot(hid_ref, layer, ids, buf_ref, buf_sem)
    copy.wait()
    last.start()
    logits = dot(wout_ref[...], hid, NT)
    expo = jnp.exp(logits)
    probs = expo / jnp.sum(expo, axis=0, keepdims=True)
    label = lab_ref[pl.ds(ids[0], 1), :]
    onehot = (label == lax.broadcasted_iota(jnp.int32, logits.shape, 0)).astype(F32)
    live = mask_ref[pl.ds(ids[0], 1), :].astype(F32)
    g_logits = (live * (probs - onehot)).astype(BF)
    d_out = dot(g_logits, wout_ref[...], TN).astype(BF)
    d_pre = (d_out.astype(F32) * (sig * (1.0 + pre * (1.0 - sig)))).astype(BF)
    back = backward_math(ids, d_pre, vals_ref, w_ref, d_ext)
    remote_ref[...] = d_ext[rows : 2 * rows, :].astype(BF).reshape(remote_ref.shape)
    part_ref[...] = back + d_ext[0:rows, :]
    weight_partials(ids, h_ref, agg, d_pre, keep_ref, send_ref)
    last.wait()


def chunk_sum(block):
    total = block[0:2].astype(F32)
    for n in range(2, block.shape[0], 2):
        total = total + block[n : n + 2].astype(F32)
    return total


def slope_math(ids, layer, ret_ref, part_in, pre_ref, pick_ref, dout_ref, buf_ref, buf_sem):
    rows, feat = part_in.shape
    returned = ret_ref[:, 0 : rows // ret_ref.shape[0], :].reshape(rows, feat)
    d_out = (part_in[...] + dot(pick_ref[...], returned, TN)).astype(BF)
    dout_ref[...] = d_out
    copy = to_slot(dout_ref, layer + 1, ids, buf_ref, buf_sem)
    copy.start()
    pre = pre_ref[...]
    sig = sigmoid(pre)
    return (d_out.astype(F32) * (sig * (1.0 + pre * (1.0 - sig)))).astype(BF), copy


def backward_kernel(layer, carry, ids, ret_ref, part_in, pre_ref, h_ref, agg_ref, *rest):
    (vals_ref, pick_ref, w_ref), rest = rest[:3], rest[3:]
    if carry:
        keep_in, recv_in, rest = rest[0], rest[1], rest[3:]
    out_ref, part_ref, buf_ref, keep_ref, send_ref, dout_ref, d_ext, buf_sem = rest
    rows, feat = part_in.shape
    d_pre, copy = slope_math(
        ids, layer, ret_ref, part_in, pre_ref, pick_ref, dout_ref, buf_ref, buf_sem
    )
    back = backward_math(ids, d_pre, vals_ref, w_ref, d_ext)
    peers, slots = out_ref.shape[0], rows // out_ref.shape[0]
    out_ref[:, 0:slots, :] = d_ext[rows : 2 * rows, :].astype(BF).reshape(peers, slots, feat)
    if carry:
        put_carry(keep_in, recv_in, out_ref, slots)
    part_ref[...] = back + d_ext[0:rows, :]
    weight_partials(ids, h_ref, agg_ref[...], d_pre, keep_ref, send_ref)
    copy.wait()


def last_slope_kernel(
    ids, ret_ref, part_in, pre_ref, h_ref, agg_ref, pick_ref, buf_in,
    dpre_ref, buf_ref, keep_ref, send_ref, chunk_ref, dout_ref, buf_sem,
):
    d_pre, copy = slope_math(
        ids, 0, ret_ref, part_in, pre_ref, pick_ref, dout_ref, buf_ref, buf_sem
    )
    dpre_ref[...] = d_pre
    weight_partials(ids, h_ref, agg_ref[...], d_pre, keep_ref, send_ref)
    slots = part_in.shape[0] // ret_ref.shape[0]
    chunk_ref[...] = chunk_sum(ret_ref[:, slots:, :]).astype(BF)
    copy.wait()


def last_spread_kernel(
    ids, dpre_ref, vals_ref, w_ref, keep_a, recv_a, keep_b, recv_b, c_in,
    out_ref, part_ref, local_ref, c_ref, d_ext, carried, sems,
):
    rows, feat = dpre_ref.shape
    peers, slots = local_ref.shape[0], local_ref.shape[1]
    size = keep_a.shape[0] // peers
    copies = [
        pltpu.make_async_copy(c_in, c_ref.at[3], sems.at[0]),
        pltpu.make_async_copy(
            carried, out_ref.at[:, pl.ds(slots, 2 * size), :], sems.at[1]
        ),
    ]
    copies[0].start()
    put_carry(keep_a, recv_a, carried, 0)
    put_carry(keep_b, recv_b, carried, size)
    copies[1].start()
    back = backward_math(ids, dpre_ref[...], vals_ref, w_ref, d_ext)
    local_ref[...] = d_ext[rows : 2 * rows, :].astype(BF).reshape(local_ref.shape)
    part_ref[...] = back + d_ext[0:rows, :]
    for copy in copies:
        copy.wait()


def put_carry(keep_ref, recv_ref, out_ref, first):
    peers, feat = out_ref.shape[0], out_ref.shape[2]
    size = keep_ref.shape[0] // peers
    total = (keep_ref[...].astype(F32) + recv_ref[...].astype(F32)).astype(BF)
    out_ref[:, first : first + size, :] = total.reshape(peers, size, feat)


def join_kernel(ids, keep_ref, recv_ref, local_ref, part_ref, buf_in, out_ref, part_out, both, sems):
    size, slots = both.shape[1], local_ref.shape[1]
    first = out_ref.shape[1] - size
    copies = [
        pltpu.make_async_copy(part_ref, part_out, sems.at[0]),
        pltpu.make_async_copy(local_ref, out_ref.at[:, pl.ds(0, slots), :], sems.at[1]),
        pltpu.make_async_copy(both, out_ref.at[:, pl.ds(first, size), :], sems.at[2]),
    ]
    copies[0].start()
    copies[1].start()
    put_carry(keep_ref, recv_ref, both, 0)
    copies[2].start()
    for copy in copies:
        copy.wait()


def chunk_kernel(ids, ret_ref, buf_in, out_ref, sums, sem):
    size = sums.shape[2]
    slots = ret_ref.shape[1] - 3 * size
    for n, layer in enumerate((2, 1, 0)):
        first = slots + n * size
        sums[layer] = chunk_sum(ret_ref[:, first : first + size, :]).astype(BF)
    copy = pltpu.make_async_copy(sums, out_ref.at[pl.ds(0, 3)], sem)
    copy.start()
    copy.wait()


def end_kernel(ids, ret_ref, part_in, pick_ref, buf_in, buf_ref, dout_ref, buf_sem):
    rows, feat = part_in.shape
    returned = ret_ref[:, 0 : rows // ret_ref.shape[0], :].reshape(rows, feat)
    dout_ref[...] = (part_in[...] + dot(pick_ref[...], returned, TN)).astype(BF)
    copy = to_slot(dout_ref, 0, ids, buf_ref, buf_sem)
    copy.start()
    copy.wait()


def layer_sum_kernel(ids, sums_ref, out_ref):
    total = sums_ref[0].astype(F32)
    for span in range(1, sums_ref.shape[0]):
        total = total + sums_ref[span].astype(F32)
    total = total.astype(BF)
    for n in range(0, out_ref.shape[0], 2):
        out_ref[n : n + 2] = total


def scale_kernel(scale, ids, mine_ref, other_ref, self_ref, neigh_ref, mine, other, sems):
    core = ids[1]
    size = mine_ref.shape[0] // 4
    for step in range(4):
        rows = pl.ds(step * size, size)
        mine[rows, :] = mine_ref[rows, :].astype(F32) * scale
        other[rows, :] = other_ref[rows, :].astype(F32) * scale
        for value, place, sem in ((mine, core, 0), (other, 1 - core, 1)):
            for target, out_ref in enumerate((self_ref, neigh_ref)):

                @pl.when(place == target)
                def _():
                    pltpu.make_async_copy(
                        value.at[rows], out_ref.at[0, rows], sems.at[sem, step]
                    ).start()

    for step in range(4):
        rows = pl.ds(step * size, size)
        for value, sem in ((mine, 0), (other, 1)):
            pltpu.make_async_copy(value.at[rows], self_ref.at[0, rows], sems.at[sem, step]).wait()


def home_kernel(ids, *refs):
    pieces, out_ref = refs[:-1], refs[-1]
    for s, piece in enumerate(pieces):
        out_ref[0, lax.rem(ids[0] + 4 - s, 4)] = piece[...]


def body(
    features,
    w_self,
    w_neigh,
    w_out,
    labels,
    train_mask,
    tile_cols,
    tile_vals,
    send_rows,
    send_counts,
):
    home = lax.axis_index("layer")
    node = lax.axis_index("node")
    core = lax.rem(node, 2)
    spans, rows, feat = features.shape
    peers, slots = send_rows.shape[2], send_rows.shape[3]
    tiles, degree, size = tile_vals.shape[2], tile_vals.shape[3], tile_vals.shape[4]
    scale = 1.0 / (spans * rows * peers)
    own_cols = lax.dynamic_index_in_dim(tile_cols.reshape(spans, tiles * degree), home, 0, False)
    scalars = jnp.concatenate([jnp.stack([home, core]).astype(jnp.int32), own_cols])
    act, wide, square = near((rows, feat)), near((rows, feat), F32), near((feat, feat))
    ext_scratch = pltpu.VMEM((2 * rows, feat), BF)
    d_ext_scratch = pltpu.VMEM((2 * rows, feat), F32)
    all_shifts = range(1, spans)

    mine = jnp.where(core == 0, w_self[0], w_neigh[0])
    left, right, far = (shift(mine, "layer", s) for s in (1, -1, 2))
    pick, outgoing, features_0, vals, pick_far = run(
        pre_kernel,
        "gather_rows",
        scalars,
        [
            (features, of_span((rows, feat))),
            (send_rows.reshape(spans, peers, slots).swapaxes(1, 2), of_span((slots, peers))),
            (send_counts.reshape(spans, 1, peers), of_span((1, peers))),
            (
                tile_vals.reshape(spans, tiles, degree, size, size),
                of_span((tiles, degree, size, size)),
            ),
        ],
        [
            near((peers * slots, rows)),
            act,
            act,
            near((tiles, degree, size, size)),
            far_block((peers * slots, rows)),
        ],
        flops=10**8,
        moved=10**6,
    )
    arrived = exchange(outgoing.reshape(peers, slots, feat))
    arrived, left, right = tie(arrived, left, right)
    left_x, right_x, far = tie(sibling(left), sibling(right), far)
    sources = [w_self[0], w_neigh[0], left, left_x, right, right_x, far, sibling(far)]
    weight = near((2, feat, feat))

    hidden, aggs, pres, weights = [features_0], [], [], []
    top = spans - 1
    stack = (pltpu.HBM((spans, rows, feat), BF), FAR)
    buf_sem = pltpu.SemaphoreType.DMA
    acts_buf = None
    for layer in range(top):
        ins = [hidden[layer], arrived.reshape(rows, feat), vals, pick, *sources]
        if layer:
            ins.append(weights[layer])
        if layer > 1:
            ins.append((acts_buf, FAR))
        agg, pre, hid, outgoing, arranged, last = run(
            functools.partial(forward_kernel, layer),
            f"layer_forward_{layer}",
            scalars,
            ins,
            [act, wide, act, act, weight, stack if layer else weight],
            [ext_scratch, buf_sem, pltpu.SemaphoreType.DMA((2, 2))],
            {len(ins) - 1: 5} if layer > 1 else None,
            flops=6 * 10**8,
            moved=4 * 10**6,
        )
        if layer:
            acts_buf = last
        else:
            weights.append(last)
        weights.append(arranged)
        hidden.append(hid)
        aggs.append(agg)
        pres.append(pre)
        arrived = exchange(outgoing.reshape(peers, slots, feat))

    ins = [
        hidden[top],
        arrived.reshape(rows, feat),
        vals,
        w_out.T,
        labels,
        train_mask,
        weights[top],
        (acts_buf, FAR),
    ]
    remote, part, keep, send, acts_buf = run(
        functools.partial(top_kernel, top),
        "top_layer",
        scalars,
        ins,
        [near((peers, slots, feat)), wide, square, square, stack],
        [
            pltpu.VMEM((rows, feat), BF),
            ext_scratch,
            d_ext_scratch,
            buf_sem,
        ],
        {len(ins) - 1: 4},
        flops=10**9,
        moved=5 * 10**6,
    )

    def travel(buf):
        return [shift(buf[s], "layer", s) for s in all_shifts]

    first_block = pl.BlockSpec((None, rows, feat), lambda i, ids: (0, 0, 0))

    def put_home(buf, *pieces):
        shape = (1, spans, rows, feat)
        return run(
            home_kernel,
            "put_home",
            scalars,
            [(buf, first_block), *pieces],
            [far_block(shape)],
            moved=2 * 10**6,
        )[0]

    chunk_rows = feat // peers
    pairs, grads_buf = [], None
    for layer in range(top - 1, 0, -1):
        returned, send = tie(exchange(remote), send)
        pairs.append((keep, sibling(send)))
        carry = layer < top - 1
        width = slots + chunk_rows * carry
        ins = [
            returned,
            part,
            pres[layer],
            hidden[layer],
            aggs[layer],
            vals,
            pick,
            weights[layer],
        ]
        aliases = None
        if carry:
            ins += [*pairs[-2], (grads_buf, FAR)]
            aliases = {len(ins) - 1: 2}
        remote, part, grads_buf, keep, send = run(
            functools.partial(backward_kernel, layer, carry),
            f"layer_backward_{layer}",
            scalars,
            ins,
            [near((peers, width, feat)), wide, stack, square, square],
            [pltpu.VMEM((rows, feat), BF), d_ext_scratch, buf_sem],
            aliases,
            flops=10**9,
            moved=5 * 10**6,
        )
        remote, recv = tie(remote, pairs[-1][1])
        pairs[-1] = (pairs[-1][0], recv)

    returned, send = tie(exchange(remote), send)
    recv_1, keep_1 = sibling(send), keep
    chunk_shape = (2, chunk_rows, feat)
    d_pre, grads_buf, keep, send, c_3 = run(
        last_slope_kernel,
        "last_slope",
        scalars,
        [returned, part, pres[0], hidden[0], aggs[0], pick, (grads_buf, FAR)],
        [act, stack, square, square, near(chunk_shape)],
        [pltpu.VMEM((rows, feat), BF), buf_sem],
        {6: 1},
        flops=4 * 10**8,
        moved=3 * 10**6,
    )
    d_pre, recv_1, send = tie(d_pre, recv_1, send)
    recv = sibling(send)
    width = slots + 3 * chunk_rows
    operand = (pltpu.HBM((peers, width, feat), BF), FAR)
    sums_out = (pltpu.HBM((spans, *chunk_shape), BF), FAR)
    remote, part, local, sums = run(
        last_spread_kernel,
        "last_spread",
        scalars,
        [d_pre, vals, weights[0], *pairs[-1], keep_1, recv_1, c_3],
        [operand, wide, near((peers, slots, feat)), sums_out],
        [
            d_ext_scratch,
            pltpu.VMEM((peers, 2 * chunk_rows, feat), BF),
            pltpu.SemaphoreType.DMA((2,)),
        ],
        flops=5 * 10**8,
        moved=4 * 10**6,
    )
    remote, recv = tie(remote, recv)
    joined, part = run(
        join_kernel,
        "join_rows",
        scalars,
        [keep, recv, local, part, (remote, FAR)],
        [operand, (pltpu.HBM((rows, feat), F32), FAR)],
        [pltpu.VMEM((peers, chunk_rows, feat), BF), pltpu.SemaphoreType.DMA((3,))],
        aliases={4: 0},
        moved=2 * 10**6,
    )
    joined, acts_buf = tie(joined, acts_buf)
    acts = travel(acts_buf)
    layer_acts = put_home(acts_buf, *acts)
    returned, layer_acts = tie(exchange(joined), layer_acts)
    sums = run(
        chunk_kernel,
        "sum_chunks",
        scalars,
        [returned, (sums, FAR)],
        [sums_out],
        [pltpu.VMEM((3, *chunk_shape), BF), buf_sem],
        aliases={1: 0},
        moved=10**6,
    )[0]
    sums = lax.all_to_all(sums, "layer", split_axis=0, concat_axis=0, tiled=True)
    grads_buf = run(
        end_kernel,
        "input_grads",
        scalars,
        [
            returned,
            (part, whole((rows, feat))),
            (pick_far, whole(pick_far.shape)),
            (grads_buf, FAR),
        ],
        [stack],
        [pltpu.VMEM((rows, feat), BF), buf_sem],
        {3: 0},
        flops=10**8,
        moved=10**6,
    )[0]
    sums, *to_send = tie(sums, *[grads_buf[s] for s in all_shifts])
    spread = run(
        layer_sum_kernel,
        "sum_over_layer",
        scalars,
        [sums],
        [far_block((peers, chunk_rows, feat))],
        moved=10**6,
    )[0]
    grads = [shift(v, "layer", s) for s, v in zip(all_shifts, to_send)]
    gathered, *grads = tie(exchange(spread), *grads)
    gathered = gathered.reshape(feat, feat)
    other = sibling(gathered)
    act_grads = put_home(grads_buf, *grads)
    out_square = (1, feat, feat)
    grad_self, grad_neigh = run(
        functools.partial(scale_kernel, scale),
        "scale_grads",
        scalars,
        [gathered, other],
        [(pltpu.HBM(out_square, F32), FAR)] * 2,
        [pltpu.VMEM((feat, feat), F32)] * 2 + [pltpu.SemaphoreType.DMA((2, 4))],
        moved=3 * 10**6,
    )
    return (layer_acts, act_grads, grad_self, grad_neigh)


def solution(mesh):
    in_specs = (
        P(None, "node", None),
        P("layer", None, None),
        P("layer", None, None),
        P(),
        P(None, "node"),
        P(None, "node"),
        P(None, "node", None, None),
        P(None, "node", None, None, None, None),
        P(None, "node", None, None),
        P(None, "node", None),
    )
    out_specs = (
        P("layer", None, "node", None),
        P("layer", None, "node", None),
        P("layer", None, None),
        P("layer", None, None),
    )
    return jax.shard_map(body, mesh=mesh, in_specs=in_specs, out_specs=out_specs, check_vma=False)
```

```python
import functools

import jax
import jax.numpy as jnp
from jax import lax
from jax.experimental import pallas as pl
from jax.experimental.pallas import tpu as pltpu
from jax.sharding import PartitionSpec as P

BF = jnp.bfloat16
F32 = jnp.float32
NN = (((1,), (0,)), ((), ()))
NT = (((1,), (1,)), ((), ()))
TN = (((0,), (0,)), ((), ()))
FAR = pl.BlockSpec(memory_space=pltpu.HBM)
LOCAL = pl.BlockSpec(memory_space=pltpu.VMEM)
VMEM_BYTES = 16 * 1024 * 1024


def dot(a, b, dims=NN):
    return lax.dot_general(a, b, dims, preferred_element_type=F32)


def shift(value, axis, steps):
    count = lax.axis_size(axis)
    return lax.ppermute(value, axis, [(i, (i + steps) % count) for i in range(count)])


def sibling(value):
    count = lax.axis_size("node")
    return lax.ppermute(value, "node", [(i, i ^ 1) for i in range(count)])


def exchange(value):
    return lax.all_to_all(value, "node", split_axis=0, concat_axis=0, tiled=True)


def of_span(shape):
    return pl.BlockSpec((None, *shape), lambda i, ids: (ids[0], *((0,) * len(shape))))


def whole(shape):
    return pl.BlockSpec(shape, lambda i, ids: (0,) * len(shape))


def near(shape, dtype=BF):
    return pltpu.VMEM(shape, dtype), LOCAL


def far_block(shape, dtype=BF):
    return pltpu.HBM(shape, dtype), whole(shape)


def run(kernel, name, scalars, ins, outs, scratch=(), aliases=None, flops=0, moved=0):
    ins = [v if isinstance(v, tuple) else (v, LOCAL) for v in ins]
    arrays = [
        pltpu.with_memory_space_constraint(a, pltpu.VMEM if s is LOCAL else pltpu.HBM)
        for a, s in ins
    ]
    return pl.pallas_call(
        kernel,
        name=name,
        grid_spec=pltpu.PrefetchScalarGridSpec(
            num_scalar_prefetch=1,
            grid=(1,),
            in_specs=[s for _, s in ins],
            out_specs=[s for _, s in outs],
            scratch_shapes=list(scratch),
        ),
        out_shape=[o for o, _ in outs],
        input_output_aliases={} if aliases is None else {k + 1: v for k, v in aliases.items()},
        compiler_params=pltpu.CompilerParams(vmem_limit_bytes=VMEM_BYTES),
        cost_estimate=pl.CostEstimate(flops=flops, bytes_accessed=moved, transcendentals=0),
    )(scalars, *arrays)


def tie(*values):
    return lax.optimization_barrier(values)


def weight_copies(layer, ids, w_refs, w_scr, sems, act):
    own_s, own_n, left, left_x, right, right_x, far, far_x = w_refs
    core = ids[1]
    pairs = [
        [(own_s, 0), (own_n, 1)],
        [(right, core), (right_x, 1 - core)],
        [(far, core), (far_x, 1 - core)],
        [(left, core), (left_x, 1 - core)],
    ]
    which = lax.rem(layer - ids[0] + 4, 4)
    for option, pair in enumerate(pairs):

        @pl.when(which == option)
        def _():
            for n, (ref, place) in enumerate(pair):
                act(pltpu.make_async_copy(ref, w_scr.at[place], sems.at[n]))


def start_weights(*args):
    weight_copies(*args, lambda copy: copy.start())


def wait_weights(*args):
    weight_copies(*args, lambda copy: copy.wait())


def side_by_side(vals_ref, r, degree):
    return jnp.concatenate([vals_ref[r, j] for j in range(degree)], axis=1)


def aggregate_rows(ids, vals_ref, ext):
    tiles, degree, size = vals_ref.shape[0], vals_ref.shape[1], vals_ref.shape[2]
    parts = []
    for r in range(tiles):
        picked = jnp.concatenate(
            [ext[pl.ds(pl.multiple_of(ids[2 + r * degree + j] * size, size), size), :] for j in range(degree)],
            axis=0,
        )
        parts.append(dot(side_by_side(vals_ref, r, degree), picked))
    return jnp.concatenate(parts, axis=0).astype(BF)


def spread_rows(ids, vals_t, d_agg, d_ext):
    tiles, size = vals_t.shape[0], vals_t.shape[2]
    degree = vals_t.shape[1] // size
    d_ext[...] = jnp.zeros_like(d_ext)
    for r in range(tiles):
        pieces = dot(vals_t[r], d_agg[r * size : (r + 1) * size])
        for j in range(degree):
            rows = pl.ds(pl.multiple_of(ids[2 + r * degree + j] * size, size), size)
            d_ext[rows, :] += pieces[j * size : (j + 1) * size]


def to_slot(value_ref, layer, ids, buf_ref, sem):
    return pltpu.make_async_copy(value_ref, buf_ref.at[lax.rem(layer - ids[0] + 4, 4)], sem)


def sigmoid(v):
    return 1.0 / (1.0 + jnp.exp(-v))


def pre_kernel(ids, h_ref, rows_ref, counts_ref, vals_ref, pick_ref, out_ref, h_out, vals_out, vals_t, pick_t, pick_far):
    slots, peers = rows_ref.shape
    total, node_rows = pick_ref.shape
    bits = slots.bit_length() - 1
    slot = lax.broadcasted_iota(jnp.int32, (total, peers), 0)
    owner = lax.broadcasted_iota(jnp.int32, (total, peers), 1)
    mine = lax.shift_right_logical(slot, bits) == owner
    wide = dot(mine.astype(F32).astype(BF), rows_ref[...].astype(F32).astype(BF), NT)
    slot_k = lax.broadcasted_iota(jnp.int32, (total, slots), 0) & (slots - 1)
    in_slot = slot_k == lax.broadcasted_iota(jnp.int32, (total, slots), 1)
    row = jnp.sum(jnp.where(in_slot, wide, 0.0), axis=1, keepdims=True)
    counts = jnp.broadcast_to(counts_ref[...].astype(F32), (total, peers))
    count = jnp.sum(jnp.where(mine, counts, 0.0), axis=1, keepdims=True)
    k = (lax.broadcasted_iota(jnp.int32, (total, 1), 0) & (slots - 1)).astype(F32)
    row = jnp.where(k < count, row, -1.0)
    place = lax.broadcasted_iota(jnp.int32, (total, node_rows), 1).astype(F32)
    pick = (place == row).astype(F32).astype(BF)
    pick_ref[...] = pick
    turned = jnp.transpose(pick)
    pick_t[...] = turned
    pick_far[...] = turned
    out_ref[...] = dot(pick, h_ref[...]).astype(BF)
    h_out[...] = h_ref[...]
    vals_out[...] = vals_ref[...]
    for r in range(vals_ref.shape[0]):
        vals_t[r] = jnp.transpose(side_by_side(vals_ref, r, vals_ref.shape[1]))


def forward_math(ids, h_ref, arr_ref, vals_ref, w_ref, ext, ready=None):
    rows = h_ref.shape[0]
    ext[0:rows, :] = h_ref[...]
    ext[rows : 2 * rows, :] = arr_ref[...]
    agg = aggregate_rows(ids, vals_ref, ext)
    if ready is not None:
        ready()
    pre = dot(h_ref[...], w_ref[0]) + dot(agg, w_ref[1])
    sig = sigmoid(pre)
    return agg, pre, sig, (pre * sig).astype(BF)


def forward_kernel(layer, ids, h_ref, arr_ref, vals_ref, pick_ref, *rest):
    w_refs, rest = rest[:8], rest[8:]
    first = layer == 0
    if first:
        agg_ref, pre_ref, hid_ref, out_ref, next_ref, w_ref = rest[:6]
    else:
        w_ref, *rest = rest[0:1] + rest[1 + (layer > 1) :]
        agg_ref, pre_ref, hid_ref, out_ref, next_ref, buf_ref = rest[:6]
    ext, buf_sem, sems = rest[-3:]
    if not first:
        copy = to_slot(h_ref, layer - 1, ids, buf_ref, buf_sem)
        copy.start()
    ready = None
    if first:
        here = (layer, ids, w_refs, w_ref, sems.at[0])
        start_weights(*here)
        ready = lambda: wait_weights(*here)
    ahead = (layer + 1, ids, w_refs, next_ref, sems.at[1])
    start_weights(*ahead)
    agg, pre, _, hid = forward_math(ids, h_ref, arr_ref, vals_ref, w_ref, ext, ready)
    hid_ref[...] = hid
    out_ref[...] = dot(pick_ref[...], hid).astype(BF)
    agg_ref[...] = agg
    pre_ref[...] = pre
    if not first:
        copy.wait()
    wait_weights(*ahead)


def backward_math(ids, d_pre, vals_ref, w_ref, d_ext):
    d_agg = dot(d_pre, w_ref[1], NT).astype(BF)
    spread_rows(ids, vals_ref, d_agg, d_ext)
    return dot(d_pre, w_ref[0], NT)


def weight_partials(ids, h_ref, agg, d_pre, keep_ref, send_ref):
    on_rows = dot(h_ref[...], d_pre, TN).astype(BF)
    on_agg = dot(agg, d_pre, TN).astype(BF)

    @pl.when(ids[1] == 0)
    def _():
        keep_ref[...] = on_rows
        send_ref[...] = on_agg

    @pl.when(ids[1] != 0)
    def _():
        keep_ref[...] = on_agg
        send_ref[...] = on_rows


def top_kernel(layer, ids, h_ref, arr_ref, vals_ref, vals_t, wout_ref, lab_ref, mask_ref, w_ref, *rest):
    remote_ref, part_ref, keep_ref, send_ref, buf_ref, hid_ref, ext, d_ext, buf_sem = rest[1:]
    copy = to_slot(h_ref, layer - 1, ids, buf_ref, buf_sem)
    copy.start()
    rows = h_ref.shape[0]
    agg, pre, sig, hid = forward_math(ids, h_ref, arr_ref, vals_ref, w_ref, ext)
    hid_ref[...] = hid
    last = to_slot(hid_ref, layer, ids, buf_ref, buf_sem)
    copy.wait()
    last.start()
    logits = dot(wout_ref[...], hid, NT)
    expo = jnp.exp(logits)
    probs = expo / jnp.sum(expo, axis=0, keepdims=True)
    label = lab_ref[pl.ds(ids[0], 1), :]
    onehot = (label == lax.broadcasted_iota(jnp.int32, logits.shape, 0)).astype(F32)
    live = mask_ref[pl.ds(ids[0], 1), :].astype(F32)
    g_logits = (live * (probs - onehot)).astype(BF)
    d_out = dot(g_logits, wout_ref[...], TN).astype(BF)
    d_pre = (d_out.astype(F32) * (sig * (1.0 + pre * (1.0 - sig)))).astype(BF)
    back = backward_math(ids, d_pre, vals_t, w_ref, d_ext)
    remote_ref[...] = d_ext[rows : 2 * rows, :].astype(BF).reshape(remote_ref.shape)
    part_ref[...] = back + d_ext[0:rows, :]
    weight_partials(ids, h_ref, agg, d_pre, keep_ref, send_ref)
    last.wait()


def chunk_sum(block):
    total = block[0:2].astype(F32)
    for n in range(2, block.shape[0], 2):
        total = total + block[n : n + 2].astype(F32)
    return total


def slope_math(ids, layer, ret_ref, part_in, pre_ref, pick_ref, dout_ref, buf_ref, buf_sem):
    rows, feat = part_in.shape
    returned = ret_ref[:, 0 : rows // ret_ref.shape[0], :].reshape(rows, feat)
    d_out = (part_in[...] + dot(pick_ref[...], returned)).astype(BF)
    dout_ref[...] = d_out
    copy = to_slot(dout_ref, layer + 1, ids, buf_ref, buf_sem)
    copy.start()
    pre = pre_ref[...]
    sig = sigmoid(pre)
    return (d_out.astype(F32) * (sig * (1.0 + pre * (1.0 - sig)))).astype(BF), copy


def backward_kernel(layer, carry, ids, ret_ref, part_in, pre_ref, h_ref, agg_ref, *rest):
    (vals_ref, pick_ref, w_ref), rest = rest[:3], rest[3:]
    if carry:
        keep_in, recv_in, rest = rest[0], rest[1], rest[3:]
    out_ref, part_ref, buf_ref, keep_ref, send_ref, dout_ref, d_ext, buf_sem = rest
    rows, feat = part_in.shape
    d_pre, copy = slope_math(
        ids, layer, ret_ref, part_in, pre_ref, pick_ref, dout_ref, buf_ref, buf_sem
    )
    back = backward_math(ids, d_pre, vals_ref, w_ref, d_ext)
    peers, slots = out_ref.shape[0], rows // out_ref.shape[0]
    out_ref[:, 0:slots, :] = d_ext[rows : 2 * rows, :].astype(BF).reshape(peers, slots, feat)
    if carry:
        put_carry(keep_in, recv_in, out_ref, slots)
    part_ref[...] = back + d_ext[0:rows, :]
    weight_partials(ids, h_ref, agg_ref[...], d_pre, keep_ref, send_ref)
    copy.wait()


def last_slope_kernel(
    ids, ret_ref, part_in, pre_ref, h_ref, agg_ref, pick_ref, buf_in,
    dpre_ref, buf_ref, keep_ref, send_ref, chunk_ref, dout_ref, buf_sem,
):
    d_pre, copy = slope_math(
        ids, 0, ret_ref, part_in, pre_ref, pick_ref, dout_ref, buf_ref, buf_sem
    )
    dpre_ref[...] = d_pre
    weight_partials(ids, h_ref, agg_ref[...], d_pre, keep_ref, send_ref)
    slots = part_in.shape[0] // ret_ref.shape[0]
    chunk_ref[...] = chunk_sum(ret_ref[:, slots:, :]).astype(BF)
    copy.wait()


def last_spread_kernel(
    ids, dpre_ref, vals_ref, w_ref, keep_a, recv_a, keep_b, recv_b, c_in,
    out_ref, part_ref, local_ref, c_ref, d_ext, carried, sems,
):
    rows, feat = dpre_ref.shape
    peers, slots = local_ref.shape[0], local_ref.shape[1]
    size = keep_a.shape[0] // peers
    copies = [
        pltpu.make_async_copy(c_in, c_ref.at[3], sems.at[0]),
        pltpu.make_async_copy(
            carried, out_ref.at[:, pl.ds(slots, 2 * size), :], sems.at[1]
        ),
    ]
    copies[0].start()
    put_carry(keep_a, recv_a, carried, 0)
    put_carry(keep_b, recv_b, carried, size)
    copies[1].start()
    back = backward_math(ids, dpre_ref[...], vals_ref, w_ref, d_ext)
    local_ref[...] = d_ext[rows : 2 * rows, :].astype(BF).reshape(local_ref.shape)
    part_ref[...] = back + d_ext[0:rows, :]
    for copy in copies:
        copy.wait()


def put_carry(keep_ref, recv_ref, out_ref, first):
    peers, feat = out_ref.shape[0], out_ref.shape[2]
    size = keep_ref.shape[0] // peers
    total = (keep_ref[...].astype(F32) + recv_ref[...].astype(F32)).astype(BF)
    out_ref[:, first : first + size, :] = total.reshape(peers, size, feat)


def join_kernel(ids, keep_ref, recv_ref, local_ref, part_ref, buf_in, out_ref, part_out, both, sems):
    size, slots = both.shape[1], local_ref.shape[1]
    first = out_ref.shape[1] - size
    copies = [
        pltpu.make_async_copy(part_ref, part_out, sems.at[0]),
        pltpu.make_async_copy(local_ref, out_ref.at[:, pl.ds(0, slots), :], sems.at[1]),
        pltpu.make_async_copy(both, out_ref.at[:, pl.ds(first, size), :], sems.at[2]),
    ]
    copies[0].start()
    copies[1].start()
    put_carry(keep_ref, recv_ref, both, 0)
    copies[2].start()
    for copy in copies:
        copy.wait()


def chunk_kernel(ids, ret_ref, buf_in, out_ref, sums, sem):
    size = sums.shape[2]
    slots = ret_ref.shape[1] - 3 * size
    for n, layer in enumerate((2, 1, 0)):
        first = slots + n * size
        sums[layer] = chunk_sum(ret_ref[:, first : first + size, :]).astype(BF)
    copy = pltpu.make_async_copy(sums, out_ref.at[pl.ds(0, 3)], sem)
    copy.start()
    copy.wait()


def end_kernel(ids, ret_ref, part_in, pick_ref, buf_in, buf_ref, dout_ref, buf_sem):
    rows, feat = part_in.shape
    returned = ret_ref[:, 0 : rows // ret_ref.shape[0], :].reshape(rows, feat)
    dout_ref[...] = (part_in[...] + dot(pick_ref[...], returned)).astype(BF)
    copy = to_slot(dout_ref, 0, ids, buf_ref, buf_sem)
    copy.start()
    copy.wait()


def layer_sum_kernel(ids, sums_ref, out_ref):
    total = sums_ref[0].astype(F32)
    for span in range(1, sums_ref.shape[0]):
        total = total + sums_ref[span].astype(F32)
    total = total.astype(BF)
    for n in range(0, out_ref.shape[0], 2):
        out_ref[n : n + 2] = total


def scale_kernel(scale, ids, mine_ref, other_ref, self_ref, neigh_ref, mine, other, sems):
    core = ids[1]
    size = mine_ref.shape[0] // 4
    for step in range(4):
        rows = pl.ds(step * size, size)
        mine[rows, :] = mine_ref[rows, :].astype(F32) * scale
        other[rows, :] = other_ref[rows, :].astype(F32) * scale
        for value, place, sem in ((mine, core, 0), (other, 1 - core, 1)):
            for target, out_ref in enumerate((self_ref, neigh_ref)):

                @pl.when(place == target)
                def _():
                    pltpu.make_async_copy(
                        value.at[rows], out_ref.at[0, rows], sems.at[sem, step]
                    ).start()

    for step in range(4):
        rows = pl.ds(step * size, size)
        for value, sem in ((mine, 0), (other, 1)):
            pltpu.make_async_copy(value.at[rows], self_ref.at[0, rows], sems.at[sem, step]).wait()


def home_kernel(ids, *refs):
    pieces, out_ref = refs[:-1], refs[-1]
    for s, piece in enumerate(pieces):
        out_ref[0, lax.rem(ids[0] + 4 - s, 4)] = piece[...]


def body(
    features,
    w_self,
    w_neigh,
    w_out,
    labels,
    train_mask,
    tile_cols,
    tile_vals,
    send_rows,
    send_counts,
):
    home = lax.axis_index("layer")
    node = lax.axis_index("node")
    core = lax.rem(node, 2)
    spans, rows, feat = features.shape
    peers, slots = send_rows.shape[2], send_rows.shape[3]
    tiles, degree, size = tile_vals.shape[2], tile_vals.shape[3], tile_vals.shape[4]
    scale = 1.0 / (spans * rows * peers)
    own_cols = lax.dynamic_index_in_dim(tile_cols.reshape(spans, tiles * degree), home, 0, False)
    scalars = jnp.concatenate([jnp.stack([home, core]).astype(jnp.int32), own_cols])
    act, wide, square = near((rows, feat)), near((rows, feat), F32), near((feat, feat))
    ext_scratch = pltpu.VMEM((2 * rows, feat), BF)
    d_ext_scratch = pltpu.VMEM((2 * rows, feat), F32)
    all_shifts = range(1, spans)

    mine = jnp.where(core == 0, w_self[0], w_neigh[0])
    left, right, far = (shift(mine, "layer", s) for s in (1, -1, 2))
    pick, outgoing, features_0, vals, vals_t, pick_t, pick_far = run(
        pre_kernel,
        "gather_rows",
        scalars,
        [
            (features, of_span((rows, feat))),
            (send_rows.reshape(spans, peers, slots).swapaxes(1, 2), of_span((slots, peers))),
            (send_counts.reshape(spans, 1, peers), of_span((1, peers))),
            (
                tile_vals.reshape(spans, tiles, degree, size, size),
                of_span((tiles, degree, size, size)),
            ),
        ],
        [
            near((peers * slots, rows)),
            act,
            act,
            near((tiles, degree, size, size)),
            near((tiles, degree * size, size)),
            near((rows, peers * slots)),
            far_block((rows, peers * slots)),
        ],
        flops=10**8,
        moved=10**6,
    )
    arrived = exchange(outgoing.reshape(peers, slots, feat))
    arrived, left, right, far = tie(arrived, left, right, far)
    sources = [w_self[0], w_neigh[0], left, sibling(left), right, sibling(right)]
    sources += [far, sibling(far)]
    weight = near((2, feat, feat))

    hidden, aggs, pres, weights = [features_0], [], [], []
    top = spans - 1
    stack = (pltpu.HBM((spans, rows, feat), BF), FAR)
    buf_sem = pltpu.SemaphoreType.DMA
    acts_buf = None
    for layer in range(top):
        ins = [hidden[layer], arrived.reshape(rows, feat), vals, pick, *sources]
        if layer:
            ins.append(weights[layer])
        if layer > 1:
            ins.append((acts_buf, FAR))
        agg, pre, hid, outgoing, arranged, last = run(
            functools.partial(forward_kernel, layer),
            f"layer_forward_{layer}",
            scalars,
            ins,
            [act, wide, act, act, weight, stack if layer else weight],
            [ext_scratch, buf_sem, pltpu.SemaphoreType.DMA((2, 2))],
            {len(ins) - 1: 5} if layer > 1 else None,
            flops=6 * 10**8,
            moved=4 * 10**6,
        )
        if layer:
            acts_buf = last
        else:
            weights.append(last)
        weights.append(arranged)
        hidden.append(hid)
        aggs.append(agg)
        pres.append(pre)
        arrived = exchange(outgoing.reshape(peers, slots, feat))

    ins = [
        hidden[top],
        arrived.reshape(rows, feat),
        vals,
        vals_t,
        w_out.T,
        labels,
        train_mask,
        weights[top],
        (acts_buf, FAR),
    ]
    remote, part, keep, send, acts_buf = run(
        functools.partial(top_kernel, top),
        "top_layer",
        scalars,
        ins,
        [near((peers, slots, feat)), wide, square, square, stack],
        [
            pltpu.VMEM((rows, feat), BF),
            ext_scratch,
            d_ext_scratch,
            buf_sem,
        ],
        {len(ins) - 1: 4},
        flops=10**9,
        moved=5 * 10**6,
    )

    def travel(buf):
        return [shift(buf[s], "layer", s) for s in all_shifts]

    first_block = pl.BlockSpec((None, rows, feat), lambda i, ids: (0, 0, 0))

    def put_home(buf, *pieces):
        shape = (1, spans, rows, feat)
        return run(
            home_kernel,
            "put_home",
            scalars,
            [(buf, first_block), *pieces],
            [far_block(shape)],
            moved=2 * 10**6,
        )[0]

    chunk_rows = feat // peers
    pairs, grads_buf = [], None
    for layer in range(top - 1, 0, -1):
        returned, send = tie(exchange(remote), send)
        pairs.append((keep, sibling(send)))
        carry = layer < top - 1
        width = slots + chunk_rows * carry
        ins = [
            returned,
            part,
            pres[layer],
            hidden[layer],
            aggs[layer],
            vals_t,
            pick_t,
            weights[layer],
        ]
        aliases = None
        if carry:
            ins += [*pairs[-2], (grads_buf, FAR)]
            aliases = {len(ins) - 1: 2}
        remote, part, grads_buf, keep, send = run(
            functools.partial(backward_kernel, layer, carry),
            f"layer_backward_{layer}",
            scalars,
            ins,
            [near((peers, width, feat)), wide, stack, square, square],
            [pltpu.VMEM((rows, feat), BF), d_ext_scratch, buf_sem],
            aliases,
            flops=10**9,
            moved=5 * 10**6,
        )
        remote, recv = tie(remote, pairs[-1][1])
        pairs[-1] = (pairs[-1][0], recv)

    returned, send = tie(exchange(remote), send)
    recv_1, keep_1 = sibling(send), keep
    chunk_shape = (2, chunk_rows, feat)
    d_pre, grads_buf, keep, send, c_3 = run(
        last_slope_kernel,
        "last_slope",
        scalars,
        [returned, part, pres[0], hidden[0], aggs[0], pick_t, (grads_buf, FAR)],
        [act, stack, square, square, near(chunk_shape)],
        [pltpu.VMEM((rows, feat), BF), buf_sem],
        {6: 1},
        flops=4 * 10**8,
        moved=3 * 10**6,
    )
    d_pre, recv_1, send = tie(d_pre, recv_1, send)
    recv = sibling(send)
    width = slots + 3 * chunk_rows
    operand = (pltpu.HBM((peers, width, feat), BF), FAR)
    sums_out = (pltpu.HBM((spans, *chunk_shape), BF), FAR)
    remote, part, local, sums = run(
        last_spread_kernel,
        "last_spread",
        scalars,
        [d_pre, vals_t, weights[0], *pairs[-1], keep_1, recv_1, c_3],
        [operand, wide, near((peers, slots, feat)), sums_out],
        [
            d_ext_scratch,
            pltpu.VMEM((peers, 2 * chunk_rows, feat), BF),
            pltpu.SemaphoreType.DMA((2,)),
        ],
        flops=5 * 10**8,
        moved=4 * 10**6,
    )
    remote, recv = tie(remote, recv)
    joined, part = run(
        join_kernel,
        "join_rows",
        scalars,
        [keep, recv, local, part, (remote, FAR)],
        [operand, (pltpu.HBM((rows, feat), F32), FAR)],
        [pltpu.VMEM((peers, chunk_rows, feat), BF), pltpu.SemaphoreType.DMA((3,))],
        aliases={4: 0},
        moved=2 * 10**6,
    )
    joined, acts_buf = tie(joined, acts_buf)
    acts = travel(acts_buf)
    layer_acts = put_home(acts_buf, *acts)
    returned, layer_acts = tie(exchange(joined), layer_acts)
    sums = run(
        chunk_kernel,
        "sum_chunks",
        scalars,
        [returned, (sums, FAR)],
        [sums_out],
        [pltpu.VMEM((3, *chunk_shape), BF), buf_sem],
        aliases={1: 0},
        moved=10**6,
    )[0]
    sums = lax.all_to_all(sums, "layer", split_axis=0, concat_axis=0, tiled=True)
    grads_buf = run(
        end_kernel,
        "input_grads",
        scalars,
        [
            returned,
            (part, whole((rows, feat))),
            (pick_far, whole(pick_far.shape)),
            (grads_buf, FAR),
        ],
        [stack],
        [pltpu.VMEM((rows, feat), BF), buf_sem],
        {3: 0},
        flops=10**8,
        moved=10**6,
    )[0]
    sums, *to_send = tie(sums, *[grads_buf[s] for s in all_shifts])
    spread = run(
        layer_sum_kernel,
        "sum_over_layer",
        scalars,
        [sums],
        [far_block((peers, chunk_rows, feat))],
        moved=10**6,
    )[0]
    grads = [shift(v, "layer", s) for s, v in zip(all_shifts, to_send)]
    gathered, *grads = tie(exchange(spread), *grads)
    gathered = gathered.reshape(feat, feat)
    other = sibling(gathered)
    act_grads = put_home(grads_buf, *grads)
    out_square = (1, feat, feat)
    grad_self, grad_neigh = run(
        functools.partial(scale_kernel, scale),
        "scale_grads",
        scalars,
        [gathered, other],
        [(pltpu.HBM(out_square, F32), FAR)] * 2,
        [pltpu.VMEM((feat, feat), F32)] * 2 + [pltpu.SemaphoreType.DMA((2, 4))],
        moved=3 * 10**6,
    )
    return (layer_acts, act_grads, grad_self, grad_neigh)


def solution(mesh):
    in_specs = (
        P(None, "node", None),
        P("layer", None, None),
        P("layer", None, None),
        P(),
        P(None, "node"),
        P(None, "node"),
        P(None, "node", None, None),
        P(None, "node", None, None, None, None),
        P(None, "node", None, None),
        P(None, "node", None),
    )
    out_specs = (
        P("layer", None, "node", None),
        P("layer", None, "node", None),
        P("layer", None, None),
        P("layer", None, None),
    )
    return jax.shard_map(body, mesh=mesh, in_specs=in_specs, out_specs=out_specs, check_vma=False)
```

```python
import functools

import jax
import jax.numpy as jnp
from jax import lax
from jax.experimental import pallas as pl
from jax.experimental.pallas import tpu as pltpu
from jax.sharding import PartitionSpec as P

BF = jnp.bfloat16
F32 = jnp.float32
NN = (((1,), (0,)), ((), ()))
NT = (((1,), (1,)), ((), ()))
TN = (((0,), (0,)), ((), ()))
FAR = pl.BlockSpec(memory_space=pltpu.HBM)
LOCAL = pl.BlockSpec(memory_space=pltpu.VMEM)
VMEM_BYTES = 16 * 1024 * 1024


def dot(a, b, dims=NN):
    return lax.dot_general(a, b, dims, preferred_element_type=F32)


def shift(value, axis, steps):
    count = lax.axis_size(axis)
    return lax.ppermute(value, axis, [(i, (i + steps) % count) for i in range(count)])


def sibling(value):
    count = lax.axis_size("node")
    return lax.ppermute(value, "node", [(i, i ^ 1) for i in range(count)])


def exchange(value):
    return lax.all_to_all(value, "node", split_axis=0, concat_axis=0, tiled=True)


def of_span(shape):
    return pl.BlockSpec((None, *shape), lambda i, ids: (ids[0], *((0,) * len(shape))))


def whole(shape):
    return pl.BlockSpec(shape, lambda i, ids: (0,) * len(shape))


def near(shape, dtype=BF):
    return pltpu.VMEM(shape, dtype), LOCAL


def far_block(shape, dtype=BF):
    return pltpu.HBM(shape, dtype), whole(shape)


def run(kernel, name, scalars, ins, outs, scratch=(), aliases=None, flops=0, moved=0):
    ins = [v if isinstance(v, tuple) else (v, LOCAL) for v in ins]
    arrays = [
        pltpu.with_memory_space_constraint(a, pltpu.VMEM if s is LOCAL else pltpu.HBM)
        for a, s in ins
    ]
    return pl.pallas_call(
        kernel,
        name=name,
        grid_spec=pltpu.PrefetchScalarGridSpec(
            num_scalar_prefetch=1,
            grid=(1,),
            in_specs=[s for _, s in ins],
            out_specs=[s for _, s in outs],
            scratch_shapes=list(scratch),
        ),
        out_shape=[o for o, _ in outs],
        input_output_aliases={} if aliases is None else {k + 1: v for k, v in aliases.items()},
        compiler_params=pltpu.CompilerParams(vmem_limit_bytes=VMEM_BYTES),
        cost_estimate=pl.CostEstimate(flops=flops, bytes_accessed=moved, transcendentals=0),
    )(scalars, *arrays)


def tie(*values):
    return lax.optimization_barrier(values)


def weight_copies(layer, ids, w_refs, w_scr, sems, act):
    own_s, own_n, left, left_x, right, right_x, far, far_x = w_refs
    core = ids[1]
    pairs = [
        [(own_s, 0), (own_n, 1)],
        [(right, core), (right_x, 1 - core)],
        [(far, core), (far_x, 1 - core)],
        [(left, core), (left_x, 1 - core)],
    ]
    which = lax.rem(layer - ids[0] + 4, 4)
    for option, pair in enumerate(pairs):

        @pl.when(which == option)
        def _():
            for n, (ref, place) in enumerate(pair):
                act(pltpu.make_async_copy(ref, w_scr.at[place], sems.at[n]))


def start_weights(*args):
    weight_copies(*args, lambda copy: copy.start())


def wait_weights(*args):
    weight_copies(*args, lambda copy: copy.wait())


def side_by_side(vals_ref, r, degree):
    return jnp.concatenate([vals_ref[r, j] for j in range(degree)], axis=1)


def aggregate_rows(ids, vals_ref, ext):
    tiles, degree, size = vals_ref.shape[0], vals_ref.shape[1], vals_ref.shape[2]
    parts = []
    for r in range(tiles):
        picked = jnp.concatenate(
            [ext[pl.ds(pl.multiple_of(ids[2 + r * degree + j] * size, size), size), :] for j in range(degree)],
            axis=0,
        )
        parts.append(dot(side_by_side(vals_ref, r, degree), picked))
    return jnp.concatenate(parts, axis=0).astype(BF)


def spread_rows(ids, vals_t, d_agg, d_ext):
    tiles, size = vals_t.shape[0], vals_t.shape[2]
    degree = vals_t.shape[1] // size
    d_ext[...] = jnp.zeros_like(d_ext)
    for r in range(tiles):
        pieces = dot(vals_t[r], d_agg[r * size : (r + 1) * size])
        for j in range(degree):
            rows = pl.ds(pl.multiple_of(ids[2 + r * degree + j] * size, size), size)
            d_ext[rows, :] += pieces[j * size : (j + 1) * size]


def to_slot(value_ref, layer, ids, buf_ref, sem):
    return pltpu.make_async_copy(value_ref, buf_ref.at[lax.rem(layer - ids[0] + 4, 4)], sem)


def sigmoid(v):
    return 1.0 / (1.0 + jnp.exp(-v))


def pre_kernel(ids, h_ref, rows_ref, counts_ref, vals_ref, pick_ref, out_ref, h_out, vals_out, vals_t, pick_t, pick_far):
    slots, peers = rows_ref.shape
    total, node_rows = pick_ref.shape
    bits = slots.bit_length() - 1
    slot = lax.broadcasted_iota(jnp.int32, (total, peers), 0)
    owner = lax.broadcasted_iota(jnp.int32, (total, peers), 1)
    mine = lax.shift_right_logical(slot, bits) == owner
    wide = dot(mine.astype(F32).astype(BF), rows_ref[...].astype(F32).astype(BF), NT)
    slot_k = lax.broadcasted_iota(jnp.int32, (total, slots), 0) & (slots - 1)
    in_slot = slot_k == lax.broadcasted_iota(jnp.int32, (total, slots), 1)
    row = jnp.sum(jnp.where(in_slot, wide, 0.0), axis=1, keepdims=True)
    counts = jnp.broadcast_to(counts_ref[...].astype(F32), (total, peers))
    count = jnp.sum(jnp.where(mine, counts, 0.0), axis=1, keepdims=True)
    k = (lax.broadcasted_iota(jnp.int32, (total, 1), 0) & (slots - 1)).astype(F32)
    row = jnp.where(k < count, row, -1.0)
    place = lax.broadcasted_iota(jnp.int32, (total, node_rows), 1).astype(F32)
    pick = (place == row).astype(F32).astype(BF)
    pick_ref[...] = pick
    turned = jnp.transpose(pick)
    pick_t[...] = turned
    pick_far[...] = turned
    out_ref[...] = dot(pick, h_ref[...]).astype(BF)
    h_out[...] = h_ref[...]
    vals_out[...] = vals_ref[...]
    for r in range(vals_ref.shape[0]):
        vals_t[r] = jnp.transpose(side_by_side(vals_ref, r, vals_ref.shape[1]))


def forward_math(ids, h_ref, arr_ref, vals_ref, w_ref, ext, ready=None):
    rows = h_ref.shape[0]
    ext[0:rows, :] = h_ref[...]
    ext[rows : 2 * rows, :] = arr_ref[...]
    agg = aggregate_rows(ids, vals_ref, ext)
    if ready is not None:
        ready()
    pre = dot(h_ref[...], w_ref[0]) + dot(agg, w_ref[1])
    sig = sigmoid(pre)
    return agg, pre, sig, (pre * sig).astype(BF)


def forward_kernel(layer, ids, h_ref, arr_ref, vals_ref, pick_ref, *rest):
    w_refs, rest = rest[:8], rest[8:]
    first = layer == 0
    if first:
        agg_ref, pre_ref, hid_ref, out_ref, next_ref, w_ref = rest[:6]
    else:
        w_ref, *rest = rest[0:1] + rest[1 + (layer > 1) :]
        agg_ref, pre_ref, hid_ref, out_ref, next_ref, buf_ref = rest[:6]
    ext, buf_sem, sems = rest[-3:]
    if not first:
        copy = to_slot(h_ref, layer - 1, ids, buf_ref, buf_sem)
        copy.start()
    ready = None
    if first:
        here = (layer, ids, w_refs, w_ref, sems.at[0])
        start_weights(*here)
        ready = lambda: wait_weights(*here)
    ahead = (layer + 1, ids, w_refs, next_ref, sems.at[1])
    start_weights(*ahead)
    agg, pre, _, hid = forward_math(ids, h_ref, arr_ref, vals_ref, w_ref, ext, ready)
    hid_ref[...] = hid
    out_ref[...] = dot(pick_ref[...], hid).astype(BF)
    agg_ref[...] = agg
    pre_ref[...] = pre
    if not first:
        copy.wait()
    wait_weights(*ahead)


def backward_math(ids, d_pre, vals_ref, w_ref, d_ext):
    d_agg = dot(d_pre, w_ref[1], NT).astype(BF)
    spread_rows(ids, vals_ref, d_agg, d_ext)
    return dot(d_pre, w_ref[0], NT)


def weight_partials(ids, h_ref, agg, d_pre, keep_ref, send_ref):
    on_rows = dot(h_ref[...], d_pre, TN).astype(BF)
    on_agg = dot(agg, d_pre, TN).astype(BF)

    @pl.when(ids[1] == 0)
    def _():
        keep_ref[...] = on_rows
        send_ref[...] = on_agg

    @pl.when(ids[1] != 0)
    def _():
        keep_ref[...] = on_agg
        send_ref[...] = on_rows


def top_kernel(layer, ids, h_ref, arr_ref, vals_ref, vals_t, wout_ref, lab_ref, mask_ref, w_ref, *rest):
    remote_ref, part_ref, keep_ref, send_ref, buf_ref, hid_ref, ext, d_ext, buf_sem = rest[1:]
    copy = to_slot(h_ref, layer - 1, ids, buf_ref, buf_sem)
    copy.start()
    rows = h_ref.shape[0]
    agg, pre, sig, hid = forward_math(ids, h_ref, arr_ref, vals_ref, w_ref, ext)
    hid_ref[...] = hid
    last = to_slot(hid_ref, layer, ids, buf_ref, buf_sem)
    copy.wait()
    last.start()
    logits = dot(wout_ref[...], hid, NT)
    expo = jnp.exp(logits)
    probs = expo / jnp.sum(expo, axis=0, keepdims=True)
    label = lab_ref[pl.ds(ids[0], 1), :]
    onehot = (label == lax.broadcasted_iota(jnp.int32, logits.shape, 0)).astype(F32)
    live = mask_ref[pl.ds(ids[0], 1), :].astype(F32)
    g_logits = (live * (probs - onehot)).astype(BF)
    d_out = dot(g_logits, wout_ref[...], TN).astype(BF)
    d_pre = (d_out.astype(F32) * (sig * (1.0 + pre * (1.0 - sig)))).astype(BF)
    back = backward_math(ids, d_pre, vals_t, w_ref, d_ext)
    remote_ref[...] = d_ext[rows : 2 * rows, :].astype(BF).reshape(remote_ref.shape)
    part_ref[...] = back + d_ext[0:rows, :]
    weight_partials(ids, h_ref, agg, d_pre, keep_ref, send_ref)
    last.wait()


def chunk_sum(block):
    total = block[0:2].astype(F32)
    for n in range(2, block.shape[0], 2):
        total = total + block[n : n + 2].astype(F32)
    return total


def slope_math(ids, layer, ret_ref, part_in, pre_ref, pick_ref, dout_ref, buf_ref, buf_sem):
    rows, feat = part_in.shape
    returned = ret_ref[:, 0 : rows // ret_ref.shape[0], :].reshape(rows, feat)
    d_out = (part_in[...] + dot(pick_ref[...], returned)).astype(BF)
    dout_ref[...] = d_out
    copy = to_slot(dout_ref, layer + 1, ids, buf_ref, buf_sem)
    copy.start()
    pre = pre_ref[...]
    sig = sigmoid(pre)
    return (d_out.astype(F32) * (sig * (1.0 + pre * (1.0 - sig)))).astype(BF), copy


def backward_kernel(layer, carry, ids, ret_ref, part_in, pre_ref, h_ref, agg_ref, *rest):
    (vals_ref, pick_ref, w_ref), rest = rest[:3], rest[3:]
    if carry:
        keep_in, recv_in, rest = rest[0], rest[1], rest[3:]
    out_ref, part_ref, buf_ref, keep_ref, send_ref, dout_ref, d_ext, buf_sem = rest
    rows, feat = part_in.shape
    d_pre, copy = slope_math(
        ids, layer, ret_ref, part_in, pre_ref, pick_ref, dout_ref, buf_ref, buf_sem
    )
    back = backward_math(ids, d_pre, vals_ref, w_ref, d_ext)
    peers, slots = out_ref.shape[0], rows // out_ref.shape[0]
    out_ref[:, 0:slots, :] = d_ext[rows : 2 * rows, :].astype(BF).reshape(peers, slots, feat)
    if carry:
        put_carry(keep_in, recv_in, out_ref, slots)
    part_ref[...] = back + d_ext[0:rows, :]
    weight_partials(ids, h_ref, agg_ref[...], d_pre, keep_ref, send_ref)
    copy.wait()


def last_slope_kernel(
    ids, ret_ref, part_in, pre_ref, h_ref, agg_ref, pick_ref, buf_in,
    dpre_ref, buf_ref, keep_ref, send_ref, chunk_ref, dout_ref, buf_sem,
):
    d_pre, copy = slope_math(
        ids, 0, ret_ref, part_in, pre_ref, pick_ref, dout_ref, buf_ref, buf_sem
    )
    dpre_ref[...] = d_pre
    weight_partials(ids, h_ref, agg_ref[...], d_pre, keep_ref, send_ref)
    slots = part_in.shape[0] // ret_ref.shape[0]
    chunk_ref[...] = chunk_sum(ret_ref[:, slots:, :]).astype(BF)
    copy.wait()


def last_spread_kernel(
    ids, dpre_ref, vals_ref, w_ref, keep_a, recv_a, keep_b, recv_b, c_in,
    out_ref, part_ref, local_ref, c_ref, d_ext, carried, sems,
):
    rows, feat = dpre_ref.shape
    peers, slots = local_ref.shape[0], local_ref.shape[1]
    size = keep_a.shape[0] // peers
    copies = [
        pltpu.make_async_copy(c_in, c_ref, sems.at[0]),
        pltpu.make_async_copy(
            carried, out_ref.at[:, pl.ds(slots, 2 * size), :], sems.at[1]
        ),
    ]
    copies[0].start()
    put_carry(keep_a, recv_a, carried, 0)
    put_carry(keep_b, recv_b, carried, size)
    copies[1].start()
    back = backward_math(ids, dpre_ref[...], vals_ref, w_ref, d_ext)
    local_ref[...] = d_ext[rows : 2 * rows, :].astype(BF).reshape(local_ref.shape)
    part_ref[...] = back + d_ext[0:rows, :]
    for copy in copies:
        copy.wait()


def put_carry(keep_ref, recv_ref, out_ref, first):
    peers, feat = out_ref.shape[0], out_ref.shape[2]
    size = keep_ref.shape[0] // peers
    total = (keep_ref[...].astype(F32) + recv_ref[...].astype(F32)).astype(BF)
    out_ref[:, first : first + size, :] = total.reshape(peers, size, feat)


def join_kernel(ids, keep_ref, recv_ref, local_ref, part_ref, buf_in, out_ref, part_out, both, sems):
    size, slots = both.shape[1], local_ref.shape[1]
    first = out_ref.shape[1] - size
    copies = [
        pltpu.make_async_copy(part_ref, part_out, sems.at[0]),
        pltpu.make_async_copy(local_ref, out_ref.at[:, pl.ds(0, slots), :], sems.at[1]),
        pltpu.make_async_copy(both, out_ref.at[:, pl.ds(first, size), :], sems.at[2]),
    ]
    copies[0].start()
    copies[1].start()
    put_carry(keep_ref, recv_ref, both, 0)
    copies[2].start()
    for copy in copies:
        copy.wait()


def chunk_kernel(ids, ret_ref, c_in, o_0, o_1, o_2, o_3, sums, sem):
    copy = pltpu.make_async_copy(c_in, sums.at[3], sem)
    copy.start()
    size = sums.shape[2]
    slots = ret_ref.shape[1] - 3 * size
    for n, layer in enumerate((2, 1, 0)):
        first = slots + n * size
        sums[layer] = chunk_sum(ret_ref[:, first : first + size, :]).astype(BF)
    copy.wait()
    for s, out_ref in enumerate((o_0, o_1, o_2, o_3)):
        out_ref[...] = sums[lax.rem(ids[0] + s, 4)]


def end_kernel(ids, ret_ref, part_in, pick_ref, buf_in, buf_ref, dout_ref, buf_sem):
    rows, feat = part_in.shape
    returned = ret_ref[:, 0 : rows // ret_ref.shape[0], :].reshape(rows, feat)
    dout_ref[...] = (part_in[...] + dot(pick_ref[...], returned)).astype(BF)
    copy = to_slot(dout_ref, 0, ids, buf_ref, buf_sem)
    copy.start()
    copy.wait()


def layer_sum_kernel(ids, own_ref, a_ref, b_ref, c_ref, out_ref):
    total = own_ref[...].astype(F32) + a_ref[...].astype(F32)
    total = (total + b_ref[...].astype(F32) + c_ref[...].astype(F32)).astype(BF)
    for n in range(0, out_ref.shape[0], 2):
        out_ref[n : n + 2] = total


def scale_kernel(scale, ids, mine_ref, other_ref, self_ref, neigh_ref, mine, other, sems):
    core = ids[1]
    size = mine_ref.shape[0] // 4
    for step in range(4):
        rows = pl.ds(step * size, size)
        mine[rows, :] = mine_ref[rows, :].astype(F32) * scale
        other[rows, :] = other_ref[rows, :].astype(F32) * scale
        for value, place, sem in ((mine, core, 0), (other, 1 - core, 1)):
            for target, out_ref in enumerate((self_ref, neigh_ref)):

                @pl.when(place == target)
                def _():
                    pltpu.make_async_copy(
                        value.at[rows], out_ref.at[0, rows], sems.at[sem, step]
                    ).start()

    for step in range(4):
        rows = pl.ds(step * size, size)
        for value, sem in ((mine, 0), (other, 1)):
            pltpu.make_async_copy(value.at[rows], self_ref.at[0, rows], sems.at[sem, step]).wait()


def home_kernel(ids, *refs):
    pieces, out_ref = refs[:-1], refs[-1]
    for s, piece in enumerate(pieces):
        out_ref[0, lax.rem(ids[0] + 4 - s, 4)] = piece[...]


def body(
    features,
    w_self,
    w_neigh,
    w_out,
    labels,
    train_mask,
    tile_cols,
    tile_vals,
    send_rows,
    send_counts,
):
    home = lax.axis_index("layer")
    node = lax.axis_index("node")
    core = lax.rem(node, 2)
    spans, rows, feat = features.shape
    peers, slots = send_rows.shape[2], send_rows.shape[3]
    tiles, degree, size = tile_vals.shape[2], tile_vals.shape[3], tile_vals.shape[4]
    scale = 1.0 / (spans * rows * peers)
    own_cols = lax.dynamic_index_in_dim(tile_cols.reshape(spans, tiles * degree), home, 0, False)
    scalars = jnp.concatenate([jnp.stack([home, core]).astype(jnp.int32), own_cols])
    act, wide, square = near((rows, feat)), near((rows, feat), F32), near((feat, feat))
    ext_scratch = pltpu.VMEM((2 * rows, feat), BF)
    d_ext_scratch = pltpu.VMEM((2 * rows, feat), F32)
    all_shifts = range(1, spans)

    mine = jnp.where(core == 0, w_self[0], w_neigh[0])
    left, right, far = (shift(mine, "layer", s) for s in (1, -1, 2))
    pick, outgoing, features_0, vals, vals_t, pick_t, pick_far = run(
        pre_kernel,
        "gather_rows",
        scalars,
        [
            (features, of_span((rows, feat))),
            (send_rows.reshape(spans, peers, slots).swapaxes(1, 2), of_span((slots, peers))),
            (send_counts.reshape(spans, 1, peers), of_span((1, peers))),
            (
                tile_vals.reshape(spans, tiles, degree, size, size),
                of_span((tiles, degree, size, size)),
            ),
        ],
        [
            near((peers * slots, rows)),
            act,
            act,
            near((tiles, degree, size, size)),
            near((tiles, degree * size, size)),
            near((rows, peers * slots)),
            far_block((rows, peers * slots)),
        ],
        flops=10**8,
        moved=10**6,
    )
    arrived = exchange(outgoing.reshape(peers, slots, feat))
    arrived, left, right, far = tie(arrived, left, right, far)
    sources = [w_self[0], w_neigh[0], left, sibling(left), right, sibling(right)]
    sources += [far, sibling(far)]
    weight = near((2, feat, feat))

    hidden, aggs, pres, weights = [features_0], [], [], []
    top = spans - 1
    stack = (pltpu.HBM((spans, rows, feat), BF), FAR)
    buf_sem = pltpu.SemaphoreType.DMA
    acts_buf = None
    for layer in range(top):
        ins = [hidden[layer], arrived.reshape(rows, feat), vals, pick, *sources]
        if layer:
            ins.append(weights[layer])
        if layer > 1:
            ins.append((acts_buf, FAR))
        agg, pre, hid, outgoing, arranged, last = run(
            functools.partial(forward_kernel, layer),
            f"layer_forward_{layer}",
            scalars,
            ins,
            [act, wide, act, act, weight, stack if layer else weight],
            [ext_scratch, buf_sem, pltpu.SemaphoreType.DMA((2, 2))],
            {len(ins) - 1: 5} if layer > 1 else None,
            flops=6 * 10**8,
            moved=4 * 10**6,
        )
        if layer:
            acts_buf = last
        else:
            weights.append(last)
        weights.append(arranged)
        hidden.append(hid)
        aggs.append(agg)
        pres.append(pre)
        arrived = exchange(outgoing.reshape(peers, slots, feat))

    ins = [
        hidden[top],
        arrived.reshape(rows, feat),
        vals,
        vals_t,
        w_out.T,
        labels,
        train_mask,
        weights[top],
        (acts_buf, FAR),
    ]
    remote, part, keep, send, acts_buf = run(
        functools.partial(top_kernel, top),
        "top_layer",
        scalars,
        ins,
        [near((peers, slots, feat)), wide, square, square, stack],
        [
            pltpu.VMEM((rows, feat), BF),
            ext_scratch,
            d_ext_scratch,
            buf_sem,
        ],
        {len(ins) - 1: 4},
        flops=10**9,
        moved=5 * 10**6,
    )

    def travel(buf):
        return [shift(buf[s], "layer", s) for s in all_shifts]

    first_block = pl.BlockSpec((None, rows, feat), lambda i, ids: (0, 0, 0))

    def put_home(buf, *pieces):
        shape = (1, spans, rows, feat)
        return run(
            home_kernel,
            "put_home",
            scalars,
            [(buf, first_block), *pieces],
            [far_block(shape)],
            moved=2 * 10**6,
        )[0]

    chunk_rows = feat // peers
    pairs, grads_buf = [], None
    for layer in range(top - 1, 0, -1):
        returned, send = tie(exchange(remote), send)
        pairs.append((keep, sibling(send)))
        carry = layer < top - 1
        width = slots + chunk_rows * carry
        ins = [
            returned,
            part,
            pres[layer],
            hidden[layer],
            aggs[layer],
            vals_t,
            pick_t,
            weights[layer],
        ]
        aliases = None
        if carry:
            ins += [*pairs[-2], (grads_buf, FAR)]
            aliases = {len(ins) - 1: 2}
        remote, part, grads_buf, keep, send = run(
            functools.partial(backward_kernel, layer, carry),
            f"layer_backward_{layer}",
            scalars,
            ins,
            [near((peers, width, feat)), wide, stack, square, square],
            [pltpu.VMEM((rows, feat), BF), d_ext_scratch, buf_sem],
            aliases,
            flops=10**9,
            moved=5 * 10**6,
        )
        remote, recv = tie(remote, pairs[-1][1])
        pairs[-1] = (pairs[-1][0], recv)

    returned, send = tie(exchange(remote), send)
    recv_1, keep_1 = sibling(send), keep
    chunk_shape = (2, chunk_rows, feat)
    d_pre, grads_buf, keep, send, c_3 = run(
        last_slope_kernel,
        "last_slope",
        scalars,
        [returned, part, pres[0], hidden[0], aggs[0], pick_t, (grads_buf, FAR)],
        [act, stack, square, square, near(chunk_shape)],
        [pltpu.VMEM((rows, feat), BF), buf_sem],
        {6: 1},
        flops=4 * 10**8,
        moved=3 * 10**6,
    )
    d_pre, recv_1, send = tie(d_pre, recv_1, send)
    recv = sibling(send)
    width = slots + 3 * chunk_rows
    operand = (pltpu.HBM((peers, width, feat), BF), FAR)
    sums_out = (pltpu.HBM(chunk_shape, BF), FAR)
    remote, part, local, sums = run(
        last_spread_kernel,
        "last_spread",
        scalars,
        [d_pre, vals_t, weights[0], *pairs[-1], keep_1, recv_1, c_3],
        [operand, wide, near((peers, slots, feat)), sums_out],
        [
            d_ext_scratch,
            pltpu.VMEM((peers, 2 * chunk_rows, feat), BF),
            pltpu.SemaphoreType.DMA((2,)),
        ],
        flops=5 * 10**8,
        moved=4 * 10**6,
    )
    remote, recv = tie(remote, recv)
    joined, part = run(
        join_kernel,
        "join_rows",
        scalars,
        [keep, recv, local, part, (remote, FAR)],
        [operand, (pltpu.HBM((rows, feat), F32), FAR)],
        [pltpu.VMEM((peers, chunk_rows, feat), BF), pltpu.SemaphoreType.DMA((3,))],
        aliases={4: 0},
        moved=2 * 10**6,
    )
    joined, acts_buf = tie(joined, acts_buf)
    acts = travel(acts_buf)
    layer_acts = put_home(acts_buf, *acts)
    returned, layer_acts = tie(exchange(joined), layer_acts)
    own_sum, *sums = run(
        chunk_kernel,
        "sum_chunks",
        scalars,
        [returned, (sums, FAR)],
        [near(chunk_shape)] * spans,
        [pltpu.VMEM((spans, *chunk_shape), BF), buf_sem],
        moved=10**6,
    )
    sums = [shift(v, "layer", s) for s, v in zip(all_shifts, sums)]
    grads_buf = run(
        end_kernel,
        "input_grads",
        scalars,
        [
            returned,
            (part, whole((rows, feat))),
            (pick_far, whole(pick_far.shape)),
            (grads_buf, FAR),
        ],
        [stack],
        [pltpu.VMEM((rows, feat), BF), buf_sem],
        {3: 0},
        flops=10**8,
        moved=10**6,
    )[0]
    pieces = tie(*sums, *[grads_buf[s] for s in all_shifts])
    sums, to_send = pieces[:3], pieces[3:]
    spread = run(
        layer_sum_kernel,
        "sum_over_layer",
        scalars,
        [own_sum, *sums],
        [far_block((peers, chunk_rows, feat))],
        moved=10**6,
    )[0]
    grads = [shift(v, "layer", s) for s, v in zip(all_shifts, to_send)]
    gathered, *grads = tie(exchange(spread), *grads)
    gathered = gathered.reshape(feat, feat)
    other = sibling(gathered)
    act_grads = put_home(grads_buf, *grads)
    out_square = (1, feat, feat)
    grad_self, grad_neigh = run(
        functools.partial(scale_kernel, scale),
        "scale_grads",
        scalars,
        [gathered, other],
        [(pltpu.HBM(out_square, F32), FAR)] * 2,
        [pltpu.VMEM((feat, feat), F32)] * 2 + [pltpu.SemaphoreType.DMA((2, 4))],
        moved=3 * 10**6,
    )
    return (layer_acts, act_grads, grad_self, grad_neigh)


def solution(mesh):
    in_specs = (
        P(None, "node", None),
        P("layer", None, None),
        P("layer", None, None),
        P(),
        P(None, "node"),
        P(None, "node"),
        P(None, "node", None, None),
        P(None, "node", None, None, None, None),
        P(None, "node", None, None),
        P(None, "node", None),
    )
    out_specs = (
        P("layer", None, "node", None),
        P("layer", None, "node", None),
        P("layer", None, None),
        P("layer", None, None),
    )
    return jax.shard_map(body, mesh=mesh, in_specs=in_specs, out_specs=out_specs, check_vma=False)
```

```python
import functools

import jax
import jax.numpy as jnp
from jax import lax
from jax.experimental import pallas as pl
from jax.experimental.pallas import tpu as pltpu
from jax.sharding import PartitionSpec as P

BF = jnp.bfloat16
F32 = jnp.float32
NN = (((1,), (0,)), ((), ()))
NT = (((1,), (1,)), ((), ()))
TN = (((0,), (0,)), ((), ()))
FAR = pl.BlockSpec(memory_space=pltpu.HBM)
LOCAL = pl.BlockSpec(memory_space=pltpu.VMEM)
VMEM_BYTES = 16 * 1024 * 1024


def dot(a, b, dims=NN):
    return lax.dot_general(a, b, dims, preferred_element_type=F32)


def shift(value, axis, steps):
    count = lax.axis_size(axis)
    return lax.ppermute(value, axis, [(i, (i + steps) % count) for i in range(count)])


def sibling(value):
    count = lax.axis_size("node")
    return lax.ppermute(value, "node", [(i, i ^ 1) for i in range(count)])


def exchange(value):
    return lax.all_to_all(value, "node", split_axis=0, concat_axis=0, tiled=True)


def of_span(shape):
    return pl.BlockSpec((None, *shape), lambda i, ids: (ids[0], *((0,) * len(shape))))


def whole(shape):
    return pl.BlockSpec(shape, lambda i, ids: (0,) * len(shape))


def near(shape, dtype=BF):
    return pltpu.VMEM(shape, dtype), LOCAL


def far_block(shape, dtype=BF):
    return pltpu.HBM(shape, dtype), whole(shape)


def run(kernel, name, scalars, ins, outs, scratch=(), aliases=None, flops=0, moved=0):
    ins = [v if isinstance(v, tuple) else (v, LOCAL) for v in ins]
    arrays = [
        pltpu.with_memory_space_constraint(a, pltpu.VMEM if s is LOCAL else pltpu.HBM)
        for a, s in ins
    ]
    return pl.pallas_call(
        kernel,
        name=name,
        grid_spec=pltpu.PrefetchScalarGridSpec(
            num_scalar_prefetch=1,
            grid=(1,),
            in_specs=[s for _, s in ins],
            out_specs=[s for _, s in outs],
            scratch_shapes=list(scratch),
        ),
        out_shape=[o for o, _ in outs],
        input_output_aliases={} if aliases is None else {k + 1: v for k, v in aliases.items()},
        compiler_params=pltpu.CompilerParams(vmem_limit_bytes=VMEM_BYTES),
        cost_estimate=pl.CostEstimate(flops=flops, bytes_accessed=moved, transcendentals=0),
    )(scalars, *arrays)


def tie(*values):
    return lax.optimization_barrier(values)


def weight_copies(layer, ids, w_refs, w_scr, sems, act):
    own_s, own_n, left, left_x, right, right_x, far, far_x = w_refs
    core = ids[1]
    pairs = [
        [(own_s, 0), (own_n, 1)],
        [(right, core), (right_x, 1 - core)],
        [(far, core), (far_x, 1 - core)],
        [(left, core), (left_x, 1 - core)],
    ]
    which = lax.rem(layer - ids[0] + 4, 4)
    for option, pair in enumerate(pairs):

        @pl.when(which == option)
        def _():
            for n, (ref, place) in enumerate(pair):
                act(pltpu.make_async_copy(ref, w_scr.at[place], sems.at[n]))


def start_weights(*args):
    weight_copies(*args, lambda copy: copy.start())


def wait_weights(*args):
    weight_copies(*args, lambda copy: copy.wait())


def side_by_side(vals_ref, r, degree):
    return jnp.concatenate([vals_ref[r, j] for j in range(degree)], axis=1)


def aggregate_rows(ids, vals_ref, ext):
    tiles, degree, size = vals_ref.shape[0], vals_ref.shape[1], vals_ref.shape[2]
    parts = []
    for r in range(tiles):
        picked = jnp.concatenate(
            [ext[pl.ds(pl.multiple_of(ids[2 + r * degree + j] * size, size), size), :] for j in range(degree)],
            axis=0,
        )
        parts.append(dot(side_by_side(vals_ref, r, degree), picked))
    return jnp.concatenate(parts, axis=0).astype(BF)


def spread_rows(ids, vals_t, d_agg, d_ext):
    tiles, size = vals_t.shape[0], vals_t.shape[2]
    degree = vals_t.shape[1] // size
    d_ext[...] = jnp.zeros_like(d_ext)
    for r in range(tiles):
        pieces = dot(vals_t[r], d_agg[r * size : (r + 1) * size])
        for j in range(degree):
            rows = pl.ds(pl.multiple_of(ids[2 + r * degree + j] * size, size), size)
            d_ext[rows, :] += pieces[j * size : (j + 1) * size]


def to_slot(value_ref, layer, ids, buf_ref, sem):
    return pltpu.make_async_copy(value_ref, buf_ref.at[lax.rem(layer - ids[0] + 4, 4)], sem)


def sigmoid(v):
    return 1.0 / (1.0 + jnp.exp(-v))


def pre_kernel(ids, h_ref, rows_ref, counts_ref, vals_ref, pick_ref, out_ref, h_out, vals_out, vals_t, pick_t, pick_far):
    slots, peers = rows_ref.shape
    total, node_rows = pick_ref.shape
    bits = slots.bit_length() - 1
    slot = lax.broadcasted_iota(jnp.int32, (total, peers), 0)
    owner = lax.broadcasted_iota(jnp.int32, (total, peers), 1)
    mine = lax.shift_right_logical(slot, bits) == owner
    wide = dot(mine.astype(F32).astype(BF), rows_ref[...].astype(F32).astype(BF), NT)
    slot_k = lax.broadcasted_iota(jnp.int32, (total, slots), 0) & (slots - 1)
    in_slot = slot_k == lax.broadcasted_iota(jnp.int32, (total, slots), 1)
    row = jnp.sum(jnp.where(in_slot, wide, 0.0), axis=1, keepdims=True)
    counts = jnp.broadcast_to(counts_ref[...].astype(F32), (total, peers))
    count = jnp.sum(jnp.where(mine, counts, 0.0), axis=1, keepdims=True)
    k = (lax.broadcasted_iota(jnp.int32, (total, 1), 0) & (slots - 1)).astype(F32)
    row = jnp.where(k < count, row, -1.0)
    place = lax.broadcasted_iota(jnp.int32, (total, node_rows), 1).astype(F32)
    pick = (place == row).astype(F32).astype(BF)
    pick_ref[...] = pick
    turned = jnp.transpose(pick)
    pick_t[...] = turned
    pick_far[...] = turned
    out_ref[...] = dot(pick, h_ref[...]).astype(BF)
    h_out[...] = h_ref[...]
    vals_out[...] = vals_ref[...]
    for r in range(vals_ref.shape[0]):
        vals_t[r] = jnp.transpose(side_by_side(vals_ref, r, vals_ref.shape[1]))


def forward_math(ids, h_ref, arr_ref, vals_ref, w_ref, ext, ready=None):
    rows = h_ref.shape[0]
    ext[0:rows, :] = h_ref[...]
    ext[rows : 2 * rows, :] = arr_ref[...]
    agg = aggregate_rows(ids, vals_ref, ext)
    if ready is not None:
        ready()
    pre = dot(h_ref[...], w_ref[0]) + dot(agg, w_ref[1])
    sig = sigmoid(pre)
    return agg, pre, sig, (pre * sig).astype(BF)


def forward_kernel(layer, ids, h_ref, arr_ref, vals_ref, pick_ref, *rest):
    w_refs, rest = rest[:8], rest[8:]
    first = layer == 0
    if first:
        agg_ref, pre_ref, hid_ref, out_ref, next_ref, w_ref = rest[:6]
    else:
        w_ref, *rest = rest[0:1] + rest[1 + (layer > 1) :]
        agg_ref, pre_ref, hid_ref, out_ref, next_ref, buf_ref = rest[:6]
    ext, buf_sem, sems = rest[-3:]
    if not first:
        copy = to_slot(h_ref, layer - 1, ids, buf_ref, buf_sem)
        copy.start()
    ready = None
    if first:
        here = (layer, ids, w_refs, w_ref, sems.at[0])
        start_weights(*here)
        ready = lambda: wait_weights(*here)
    ahead = (layer + 1, ids, w_refs, next_ref, sems.at[1])
    start_weights(*ahead)
    agg, pre, _, hid = forward_math(ids, h_ref, arr_ref, vals_ref, w_ref, ext, ready)
    hid_ref[...] = hid
    out_ref[...] = dot(pick_ref[...], hid).astype(BF)
    agg_ref[...] = agg
    pre_ref[...] = pre
    if not first:
        copy.wait()
    wait_weights(*ahead)


def backward_math(ids, d_pre, vals_ref, w_ref, d_ext):
    d_agg = dot(d_pre, w_ref[1], NT).astype(BF)
    spread_rows(ids, vals_ref, d_agg, d_ext)
    return dot(d_pre, w_ref[0], NT)


def weight_partials(ids, h_ref, agg, d_pre, keep_ref, send_ref):
    on_rows = dot(h_ref[...], d_pre, TN).astype(BF)
    on_agg = dot(agg, d_pre, TN).astype(BF)

    @pl.when(ids[1] == 0)
    def _():
        keep_ref[...] = on_rows
        send_ref[...] = on_agg

    @pl.when(ids[1] != 0)
    def _():
        keep_ref[...] = on_agg
        send_ref[...] = on_rows


def top_kernel(layer, ids, h_ref, arr_ref, vals_ref, vals_t, wout_ref, lab_ref, mask_ref, w_ref, *rest):
    remote_ref, part_ref, keep_ref, send_ref, buf_ref, hid_ref, ext, d_ext, buf_sem = rest[1:]
    copy = to_slot(h_ref, layer - 1, ids, buf_ref, buf_sem)
    copy.start()
    rows = h_ref.shape[0]
    agg, pre, sig, hid = forward_math(ids, h_ref, arr_ref, vals_ref, w_ref, ext)
    hid_ref[...] = hid
    last = to_slot(hid_ref, layer, ids, buf_ref, buf_sem)
    copy.wait()
    last.start()
    logits = dot(wout_ref[...], hid, NT)
    expo = jnp.exp(logits)
    probs = expo / jnp.sum(expo, axis=0, keepdims=True)
    label = lab_ref[pl.ds(ids[0], 1), :]
    onehot = (label == lax.broadcasted_iota(jnp.int32, logits.shape, 0)).astype(F32)
    live = mask_ref[pl.ds(ids[0], 1), :].astype(F32)
    g_logits = (live * (probs - onehot)).astype(BF)
    d_out = dot(g_logits, wout_ref[...], TN).astype(BF)
    d_pre = (d_out.astype(F32) * (sig * (1.0 + pre * (1.0 - sig)))).astype(BF)
    back = backward_math(ids, d_pre, vals_t, w_ref, d_ext)
    remote_ref[...] = d_ext[rows : 2 * rows, :].astype(BF).reshape(remote_ref.shape)
    part_ref[...] = back + d_ext[0:rows, :]
    weight_partials(ids, h_ref, agg, d_pre, keep_ref, send_ref)
    last.wait()


def chunk_sum(block):
    total = block[0:2].astype(F32)
    for n in range(2, block.shape[0], 2):
        total = total + block[n : n + 2].astype(F32)
    return total


def slope_math(ids, layer, ret_ref, part_in, pre_ref, pick_ref, dout_ref, buf_ref, buf_sem):
    rows, feat = part_in.shape
    returned = ret_ref[:, 0 : rows // ret_ref.shape[0], :].reshape(rows, feat)
    d_out = (part_in[...] + dot(pick_ref[...], returned)).astype(BF)
    dout_ref[...] = d_out
    copy = to_slot(dout_ref, layer + 1, ids, buf_ref, buf_sem)
    copy.start()
    pre = pre_ref[...]
    sig = sigmoid(pre)
    return (d_out.astype(F32) * (sig * (1.0 + pre * (1.0 - sig)))).astype(BF), copy


def backward_kernel(layer, carry, ids, ret_ref, part_in, pre_ref, h_ref, agg_ref, *rest):
    (vals_ref, pick_ref, w_ref), rest = rest[:3], rest[3:]
    if carry:
        keep_in, recv_in, rest = rest[0], rest[1], rest[3:]
    out_ref, part_ref, buf_ref, keep_ref, send_ref, dout_ref, d_ext, buf_sem = rest
    rows, feat = part_in.shape
    d_pre, copy = slope_math(
        ids, layer, ret_ref, part_in, pre_ref, pick_ref, dout_ref, buf_ref, buf_sem
    )
    back = backward_math(ids, d_pre, vals_ref, w_ref, d_ext)
    peers, slots = out_ref.shape[0], rows // out_ref.shape[0]
    out_ref[:, 0:slots, :] = d_ext[rows : 2 * rows, :].astype(BF).reshape(peers, slots, feat)
    if carry:
        put_carry(keep_in, recv_in, out_ref, slots)
    part_ref[...] = back + d_ext[0:rows, :]
    weight_partials(ids, h_ref, agg_ref[...], d_pre, keep_ref, send_ref)
    copy.wait()


def last_slope_kernel(
    ids, ret_ref, part_in, pre_ref, h_ref, agg_ref, pick_ref, buf_in,
    dpre_ref, buf_ref, keep_ref, send_ref, chunk_ref, dout_ref, buf_sem,
):
    d_pre, copy = slope_math(
        ids, 0, ret_ref, part_in, pre_ref, pick_ref, dout_ref, buf_ref, buf_sem
    )
    dpre_ref[...] = d_pre
    weight_partials(ids, h_ref, agg_ref[...], d_pre, keep_ref, send_ref)
    slots = part_in.shape[0] // ret_ref.shape[0]
    chunk_ref[...] = chunk_sum(ret_ref[:, slots:, :]).astype(BF)
    copy.wait()


def last_spread_kernel(
    ids, dpre_ref, vals_ref, w_ref, keep_a, recv_a, keep_b, recv_b, c_in,
    out_ref, part_ref, local_ref, c_ref, d_ext, carried, sems,
):
    rows, feat = dpre_ref.shape
    peers, slots = local_ref.shape[0], local_ref.shape[1]
    size = keep_a.shape[0] // peers
    copies = [
        pltpu.make_async_copy(c_in, c_ref, sems.at[0]),
        pltpu.make_async_copy(
            carried, out_ref.at[:, pl.ds(slots, 2 * size), :], sems.at[1]
        ),
    ]
    copies[0].start()
    put_carry(keep_a, recv_a, carried, 0)
    put_carry(keep_b, recv_b, carried, size)
    copies[1].start()
    back = backward_math(ids, dpre_ref[...], vals_ref, w_ref, d_ext)
    local_ref[...] = d_ext[rows : 2 * rows, :].astype(BF).reshape(local_ref.shape)
    part_ref[...] = back + d_ext[0:rows, :]
    for copy in copies:
        copy.wait()


def put_carry(keep_ref, recv_ref, out_ref, first):
    peers, feat = out_ref.shape[0], out_ref.shape[2]
    size = keep_ref.shape[0] // peers
    total = (keep_ref[...].astype(F32) + recv_ref[...].astype(F32)).astype(BF)
    out_ref[:, first : first + size, :] = total.reshape(peers, size, feat)


def join_kernel(ids, keep_ref, recv_ref, local_ref, part_ref, buf_in, out_ref, part_out, both, sems):
    size, slots = both.shape[1], local_ref.shape[1]
    first = out_ref.shape[1] - size
    copies = [
        pltpu.make_async_copy(part_ref, part_out, sems.at[0]),
        pltpu.make_async_copy(local_ref, out_ref.at[:, pl.ds(0, slots), :], sems.at[1]),
        pltpu.make_async_copy(both, out_ref.at[:, pl.ds(first, size), :], sems.at[2]),
    ]
    copies[0].start()
    copies[1].start()
    put_carry(keep_ref, recv_ref, both, 0)
    copies[2].start()
    for copy in copies:
        copy.wait()


def chunk_kernel(ids, ret_ref, c_in, o_0, o_1, o_2, o_3, sums, sem):
    copy = pltpu.make_async_copy(c_in, sums.at[3], sem)
    copy.start()
    size = sums.shape[2]
    slots = ret_ref.shape[1] - 3 * size
    for n, layer in enumerate((2, 1, 0)):
        first = slots + n * size
        sums[layer] = chunk_sum(ret_ref[:, first : first + size, :]).astype(BF)
    copy.wait()
    for s, out_ref in enumerate((o_0, o_1, o_2, o_3)):
        out_ref[...] = sums[lax.rem(ids[0] + s, 4)]


def end_kernel(ids, ret_ref, part_in, pick_ref, buf_in, buf_ref, o_1, o_2, o_3, dout_ref, sems):
    rows, feat = part_in.shape
    outs = (o_1, o_2, o_3)
    copies = [
        pltpu.make_async_copy(buf_in.at[s + 1], out_ref, sems.at[s])
        for s, out_ref in enumerate(outs)
    ]
    for copy in copies:
        copy.start()
    returned = ret_ref[:, 0 : rows // ret_ref.shape[0], :].reshape(rows, feat)
    dout_ref[...] = (part_in[...] + dot(pick_ref[...], returned)).astype(BF)
    for copy in copies:
        copy.wait()
    for s, out_ref in enumerate(outs):

        @pl.when(lax.rem(ids[0] + s + 1, 4) == 0)
        def _():
            out_ref[...] = dout_ref[...]

    @pl.when(ids[0] == 0)
    def _():
        home = pltpu.make_async_copy(dout_ref, buf_ref.at[0], sems.at[3])
        home.start()
        home.wait()


def layer_sum_kernel(ids, own_ref, a_ref, b_ref, c_ref, out_ref):
    total = own_ref[...].astype(F32) + a_ref[...].astype(F32)
    total = (total + b_ref[...].astype(F32) + c_ref[...].astype(F32)).astype(BF)
    for n in range(0, out_ref.shape[0], 2):
        out_ref[n : n + 2] = total


def scale_kernel(scale, ids, mine_ref, other_ref, self_ref, neigh_ref, mine, other, sems):
    core = ids[1]
    size = mine_ref.shape[0] // 4
    for step in range(4):
        rows = pl.ds(step * size, size)
        mine[rows, :] = mine_ref[rows, :].astype(F32) * scale
        other[rows, :] = other_ref[rows, :].astype(F32) * scale
        for value, place, sem in ((mine, core, 0), (other, 1 - core, 1)):
            for target, out_ref in enumerate((self_ref, neigh_ref)):

                @pl.when(place == target)
                def _():
                    pltpu.make_async_copy(
                        value.at[rows], out_ref.at[0, rows], sems.at[sem, step]
                    ).start()

    for step in range(4):
        rows = pl.ds(step * size, size)
        for value, sem in ((mine, 0), (other, 1)):
            pltpu.make_async_copy(value.at[rows], self_ref.at[0, rows], sems.at[sem, step]).wait()


def home_kernel(ids, *refs):
    pieces, out_ref = refs[:-1], refs[-1]
    for s, piece in enumerate(pieces):
        out_ref[0, lax.rem(ids[0] + 4 - s, 4)] = piece[...]


def body(
    features,
    w_self,
    w_neigh,
    w_out,
    labels,
    train_mask,
    tile_cols,
    tile_vals,
    send_rows,
    send_counts,
):
    home = lax.axis_index("layer")
    node = lax.axis_index("node")
    core = lax.rem(node, 2)
    spans, rows, feat = features.shape
    peers, slots = send_rows.shape[2], send_rows.shape[3]
    tiles, degree, size = tile_vals.shape[2], tile_vals.shape[3], tile_vals.shape[4]
    scale = 1.0 / (spans * rows * peers)
    own_cols = lax.dynamic_index_in_dim(tile_cols.reshape(spans, tiles * degree), home, 0, False)
    scalars = jnp.concatenate([jnp.stack([home, core]).astype(jnp.int32), own_cols])
    act, wide, square = near((rows, feat)), near((rows, feat), F32), near((feat, feat))
    ext_scratch = pltpu.VMEM((2 * rows, feat), BF)
    d_ext_scratch = pltpu.VMEM((2 * rows, feat), F32)
    all_shifts = range(1, spans)

    mine = jnp.where(core == 0, w_self[0], w_neigh[0])
    left, right, far = (shift(mine, "layer", s) for s in (1, -1, 2))
    pick, outgoing, features_0, vals, vals_t, pick_t, pick_far = run(
        pre_kernel,
        "gather_rows",
        scalars,
        [
            (features, of_span((rows, feat))),
            (send_rows.reshape(spans, peers, slots).swapaxes(1, 2), of_span((slots, peers))),
            (send_counts.reshape(spans, 1, peers), of_span((1, peers))),
            (
                tile_vals.reshape(spans, tiles, degree, size, size),
                of_span((tiles, degree, size, size)),
            ),
        ],
        [
            near((peers * slots, rows)),
            act,
            act,
            near((tiles, degree, size, size)),
            near((tiles, degree * size, size)),
            near((rows, peers * slots)),
            far_block((rows, peers * slots)),
        ],
        flops=10**8,
        moved=10**6,
    )
    arrived = exchange(outgoing.reshape(peers, slots, feat))
    arrived, left, right, far = tie(arrived, left, right, far)
    sources = [w_self[0], w_neigh[0], left, sibling(left), right, sibling(right)]
    sources += [far, sibling(far)]
    weight = near((2, feat, feat))

    hidden, aggs, pres, weights = [features_0], [], [], []
    top = spans - 1
    stack = (pltpu.HBM((spans, rows, feat), BF), FAR)
    buf_sem = pltpu.SemaphoreType.DMA
    acts_buf = None
    for layer in range(top):
        ins = [hidden[layer], arrived.reshape(rows, feat), vals, pick, *sources]
        if layer:
            ins.append(weights[layer])
        if layer > 1:
            ins.append((acts_buf, FAR))
        agg, pre, hid, outgoing, arranged, last = run(
            functools.partial(forward_kernel, layer),
            f"layer_forward_{layer}",
            scalars,
            ins,
            [act, wide, act, act, weight, stack if layer else weight],
            [ext_scratch, buf_sem, pltpu.SemaphoreType.DMA((2, 2))],
            {len(ins) - 1: 5} if layer > 1 else None,
            flops=6 * 10**8,
            moved=4 * 10**6,
        )
        if layer:
            acts_buf = last
        else:
            weights.append(last)
        weights.append(arranged)
        hidden.append(hid)
        aggs.append(agg)
        pres.append(pre)
        arrived = exchange(outgoing.reshape(peers, slots, feat))

    ins = [
        hidden[top],
        arrived.reshape(rows, feat),
        vals,
        vals_t,
        w_out.T,
        labels,
        train_mask,
        weights[top],
        (acts_buf, FAR),
    ]
    remote, part, keep, send, acts_buf = run(
        functools.partial(top_kernel, top),
        "top_layer",
        scalars,
        ins,
        [near((peers, slots, feat)), wide, square, square, stack],
        [
            pltpu.VMEM((rows, feat), BF),
            ext_scratch,
            d_ext_scratch,
            buf_sem,
        ],
        {len(ins) - 1: 4},
        flops=10**9,
        moved=5 * 10**6,
    )

    def travel(buf):
        return [shift(buf[s], "layer", s) for s in all_shifts]

    first_block = pl.BlockSpec((None, rows, feat), lambda i, ids: (0, 0, 0))

    def put_home(buf, *pieces):
        shape = (1, spans, rows, feat)
        return run(
            home_kernel,
            "put_home",
            scalars,
            [(buf, first_block), *pieces],
            [far_block(shape)],
            moved=2 * 10**6,
        )[0]

    chunk_rows = feat // peers
    pairs, grads_buf = [], None
    for layer in range(top - 1, 0, -1):
        returned, send = tie(exchange(remote), send)
        pairs.append((keep, sibling(send)))
        carry = layer < top - 1
        width = slots + chunk_rows * carry
        ins = [
            returned,
            part,
            pres[layer],
            hidden[layer],
            aggs[layer],
            vals_t,
            pick_t,
            weights[layer],
        ]
        aliases = None
        if carry:
            ins += [*pairs[-2], (grads_buf, FAR)]
            aliases = {len(ins) - 1: 2}
        remote, part, grads_buf, keep, send = run(
            functools.partial(backward_kernel, layer, carry),
            f"layer_backward_{layer}",
            scalars,
            ins,
            [near((peers, width, feat)), wide, stack, square, square],
            [pltpu.VMEM((rows, feat), BF), d_ext_scratch, buf_sem],
            aliases,
            flops=10**9,
            moved=5 * 10**6,
        )
        remote, recv = tie(remote, pairs[-1][1])
        pairs[-1] = (pairs[-1][0], recv)

    returned, send = tie(exchange(remote), send)
    recv_1, keep_1 = sibling(send), keep
    chunk_shape = (2, chunk_rows, feat)
    d_pre, grads_buf, keep, send, c_3 = run(
        last_slope_kernel,
        "last_slope",
        scalars,
        [returned, part, pres[0], hidden[0], aggs[0], pick_t, (grads_buf, FAR)],
        [act, stack, square, square, near(chunk_shape)],
        [pltpu.VMEM((rows, feat), BF), buf_sem],
        {6: 1},
        flops=4 * 10**8,
        moved=3 * 10**6,
    )
    d_pre, recv_1, send = tie(d_pre, recv_1, send)
    recv = sibling(send)
    width = slots + 3 * chunk_rows
    operand = (pltpu.HBM((peers, width, feat), BF), FAR)
    sums_out = (pltpu.HBM(chunk_shape, BF), FAR)
    remote, part, local, sums = run(
        last_spread_kernel,
        "last_spread",
        scalars,
        [d_pre, vals_t, weights[0], *pairs[-1], keep_1, recv_1, c_3],
        [operand, wide, near((peers, slots, feat)), sums_out],
        [
            d_ext_scratch,
            pltpu.VMEM((peers, 2 * chunk_rows, feat), BF),
            pltpu.SemaphoreType.DMA((2,)),
        ],
        flops=5 * 10**8,
        moved=4 * 10**6,
    )
    remote, recv = tie(remote, recv)
    joined, part = run(
        join_kernel,
        "join_rows",
        scalars,
        [keep, recv, local, part, (remote, FAR)],
        [operand, (pltpu.HBM((rows, feat), F32), FAR)],
        [pltpu.VMEM((peers, chunk_rows, feat), BF), pltpu.SemaphoreType.DMA((3,))],
        aliases={4: 0},
        moved=2 * 10**6,
    )
    joined, acts_buf = tie(joined, acts_buf)
    acts = travel(acts_buf)
    layer_acts = put_home(acts_buf, *acts)
    returned, layer_acts = tie(exchange(joined), layer_acts)
    own_sum, *sums = run(
        chunk_kernel,
        "sum_chunks",
        scalars,
        [returned, (sums, FAR)],
        [near(chunk_shape)] * spans,
        [pltpu.VMEM((spans, *chunk_shape), BF), buf_sem],
        moved=10**6,
    )
    sums = [shift(v, "layer", s) for s, v in zip(all_shifts, sums)]
    grads_buf, *to_send = run(
        end_kernel,
        "input_grads",
        scalars,
        [
            returned,
            (part, whole((rows, feat))),
            (pick_far, whole(pick_far.shape)),
            (grads_buf, FAR),
        ],
        [stack, act, act, act],
        [pltpu.VMEM((rows, feat), BF), pltpu.SemaphoreType.DMA((4,))],
        {3: 0},
        flops=10**8,
        moved=10**6,
    )
    pieces = tie(*sums, *to_send)
    sums, to_send = pieces[:3], pieces[3:]
    spread = run(
        layer_sum_kernel,
        "sum_over_layer",
        scalars,
        [own_sum, *sums],
        [far_block((peers, chunk_rows, feat))],
        moved=10**6,
    )[0]
    grads = [shift(v, "layer", s) for s, v in zip(all_shifts, to_send)]
    gathered, *grads = tie(exchange(spread), *grads)
    gathered = gathered.reshape(feat, feat)
    other = sibling(gathered)
    act_grads = put_home(grads_buf, *grads)
    out_square = (1, feat, feat)
    grad_self, grad_neigh = run(
        functools.partial(scale_kernel, scale),
        "scale_grads",
        scalars,
        [gathered, other],
        [(pltpu.HBM(out_square, F32), FAR)] * 2,
        [pltpu.VMEM((feat, feat), F32)] * 2 + [pltpu.SemaphoreType.DMA((2, 4))],
        moved=3 * 10**6,
    )
    return (layer_acts, act_grads, grad_self, grad_neigh)


def solution(mesh):
    in_specs = (
        P(None, "node", None),
        P("layer", None, None),
        P("layer", None, None),
        P(),
        P(None, "node"),
        P(None, "node"),
        P(None, "node", None, None),
        P(None, "node", None, None, None, None),
        P(None, "node", None, None),
        P(None, "node", None),
    )
    out_specs = (
        P("layer", None, "node", None),
        P("layer", None, "node", None),
        P("layer", None, None),
        P("layer", None, None),
    )
    return jax.shard_map(body, mesh=mesh, in_specs=in_specs, out_specs=out_specs, check_vma=False)
```

```python
import functools

import jax
import jax.numpy as jnp
from jax import lax
from jax.experimental import pallas as pl
from jax.experimental.pallas import tpu as pltpu
from jax.sharding import PartitionSpec as P

BF = jnp.bfloat16
F32 = jnp.float32
NN = (((1,), (0,)), ((), ()))
NT = (((1,), (1,)), ((), ()))
TN = (((0,), (0,)), ((), ()))
FAR = pl.BlockSpec(memory_space=pltpu.HBM)
LOCAL = pl.BlockSpec(memory_space=pltpu.VMEM)
VMEM_BYTES = 16 * 1024 * 1024


def dot(a, b, dims=NN):
    return lax.dot_general(a, b, dims, preferred_element_type=F32)


def shift(value, axis, steps):
    count = lax.axis_size(axis)
    return lax.ppermute(value, axis, [(i, (i + steps) % count) for i in range(count)])


def sibling(value):
    count = lax.axis_size("node")
    return lax.ppermute(value, "node", [(i, i ^ 1) for i in range(count)])


def exchange(value):
    return lax.all_to_all(value, "node", split_axis=0, concat_axis=0, tiled=True)


def of_span(shape):
    return pl.BlockSpec((None, *shape), lambda i, ids: (ids[0], *((0,) * len(shape))))


def whole(shape):
    return pl.BlockSpec(shape, lambda i, ids: (0,) * len(shape))


def near(shape, dtype=BF):
    return pltpu.VMEM(shape, dtype), LOCAL


def far_block(shape, dtype=BF):
    return pltpu.HBM(shape, dtype), whole(shape)


def run(kernel, name, scalars, ins, outs, scratch=(), aliases=None, flops=0, moved=0):
    ins = [v if isinstance(v, tuple) else (v, LOCAL) for v in ins]
    arrays = [
        pltpu.with_memory_space_constraint(a, pltpu.VMEM if s is LOCAL else pltpu.HBM)
        for a, s in ins
    ]
    return pl.pallas_call(
        kernel,
        name=name,
        grid_spec=pltpu.PrefetchScalarGridSpec(
            num_scalar_prefetch=1,
            grid=(1,),
            in_specs=[s for _, s in ins],
            out_specs=[s for _, s in outs],
            scratch_shapes=list(scratch),
        ),
        out_shape=[o for o, _ in outs],
        input_output_aliases={} if aliases is None else {k + 1: v for k, v in aliases.items()},
        compiler_params=pltpu.CompilerParams(vmem_limit_bytes=VMEM_BYTES),
        cost_estimate=pl.CostEstimate(flops=flops, bytes_accessed=moved, transcendentals=0),
    )(scalars, *arrays)


def tie(*values):
    return lax.optimization_barrier(values)


def weight_copies(layer, ids, w_refs, w_scr, sems, act):
    own_s, own_n, left, left_x, right, right_x, far, far_x = w_refs
    core = ids[1]
    pairs = [
        [(own_s, 0), (own_n, 1)],
        [(right, core), (right_x, 1 - core)],
        [(far, core), (far_x, 1 - core)],
        [(left, core), (left_x, 1 - core)],
    ]
    which = lax.rem(layer - ids[0] + 4, 4)
    for option, pair in enumerate(pairs):

        @pl.when(which == option)
        def _():
            for n, (ref, place) in enumerate(pair):
                act(pltpu.make_async_copy(ref, w_scr.at[place], sems.at[n]))


def start_weights(*args):
    weight_copies(*args, lambda copy: copy.start())


def wait_weights(*args):
    weight_copies(*args, lambda copy: copy.wait())


def side_by_side(vals_ref, r, degree):
    return jnp.concatenate([vals_ref[r, j] for j in range(degree)], axis=1)


def aggregate_rows(ids, vals_ref, ext):
    tiles, degree, size = vals_ref.shape[0], vals_ref.shape[1], vals_ref.shape[2]
    parts = []
    for r in range(tiles):
        picked = jnp.concatenate(
            [ext[pl.ds(pl.multiple_of(ids[2 + r * degree + j] * size, size), size), :] for j in range(degree)],
            axis=0,
        )
        parts.append(dot(side_by_side(vals_ref, r, degree), picked))
    return jnp.concatenate(parts, axis=0).astype(BF)


def spread_rows(ids, vals_t, d_agg, d_ext):
    tiles, size = vals_t.shape[0], vals_t.shape[2]
    degree = vals_t.shape[1] // size
    d_ext[...] = jnp.zeros_like(d_ext)
    for r in range(tiles):
        pieces = dot(vals_t[r], d_agg[r * size : (r + 1) * size])
        for j in range(degree):
            rows = pl.ds(pl.multiple_of(ids[2 + r * degree + j] * size, size), size)
            d_ext[rows, :] += pieces[j * size : (j + 1) * size]


def to_slot(value_ref, layer, ids, buf_ref, sem):
    return pltpu.make_async_copy(value_ref, buf_ref.at[lax.rem(layer - ids[0] + 4, 4)], sem)


def sigmoid(v):
    return 1.0 / (1.0 + jnp.exp(-v))


def pre_kernel(ids, h_ref, rows_ref, counts_ref, vals_ref, pick_ref, out_ref, h_out, vals_out, vals_t, pick_t, pick_far):
    slots, peers = rows_ref.shape
    total, node_rows = pick_ref.shape
    bits = slots.bit_length() - 1
    slot = lax.broadcasted_iota(jnp.int32, (total, peers), 0)
    owner = lax.broadcasted_iota(jnp.int32, (total, peers), 1)
    mine = lax.shift_right_logical(slot, bits) == owner
    wide = dot(mine.astype(F32).astype(BF), rows_ref[...].astype(F32).astype(BF), NT)
    slot_k = lax.broadcasted_iota(jnp.int32, (total, slots), 0) & (slots - 1)
    in_slot = slot_k == lax.broadcasted_iota(jnp.int32, (total, slots), 1)
    row = jnp.sum(jnp.where(in_slot, wide, 0.0), axis=1, keepdims=True)
    counts = jnp.broadcast_to(counts_ref[...].astype(F32), (total, peers))
    count = jnp.sum(jnp.where(mine, counts, 0.0), axis=1, keepdims=True)
    k = (lax.broadcasted_iota(jnp.int32, (total, 1), 0) & (slots - 1)).astype(F32)
    row = jnp.where(k < count, row, -1.0)
    place = lax.broadcasted_iota(jnp.int32, (total, node_rows), 1).astype(F32)
    pick = (place == row).astype(F32).astype(BF)
    pick_ref[...] = pick
    turned = jnp.transpose(pick)
    pick_t[...] = turned
    pick_far[...] = turned
    out_ref[...] = dot(pick, h_ref[...]).astype(BF)
    h_out[...] = h_ref[...]
    vals_out[...] = vals_ref[...]
    for r in range(vals_ref.shape[0]):
        vals_t[r] = jnp.transpose(side_by_side(vals_ref, r, vals_ref.shape[1]))


def forward_math(ids, h_ref, arr_ref, vals_ref, w_ref, ext, ready=None):
    rows = h_ref.shape[0]
    ext[0:rows, :] = h_ref[...]
    ext[rows : 2 * rows, :] = arr_ref[...]
    agg = aggregate_rows(ids, vals_ref, ext)
    if ready is not None:
        ready()
    pre = dot(h_ref[...], w_ref[0]) + dot(agg, w_ref[1])
    sig = sigmoid(pre)
    return agg, pre, sig, (pre * sig).astype(BF)


def forward_kernel(layer, ids, h_ref, arr_ref, vals_ref, pick_ref, *rest):
    w_refs, rest = rest[:8], rest[8:]
    first = layer == 0
    if first:
        agg_ref, pre_ref, hid_ref, out_ref, next_ref, w_ref = rest[:6]
    else:
        w_ref, *rest = rest[0:1] + rest[1 + (layer > 1) :]
        agg_ref, pre_ref, hid_ref, out_ref, next_ref, buf_ref = rest[:6]
    ext, buf_sem, sems = rest[-3:]
    if not first:
        copy = to_slot(h_ref, layer - 1, ids, buf_ref, buf_sem)
        copy.start()
    ready = None
    if first:
        here = (layer, ids, w_refs, w_ref, sems.at[0])
        start_weights(*here)
        ready = lambda: wait_weights(*here)
    ahead = (layer + 1, ids, w_refs, next_ref, sems.at[1])
    start_weights(*ahead)
    agg, pre, _, hid = forward_math(ids, h_ref, arr_ref, vals_ref, w_ref, ext, ready)
    hid_ref[...] = hid
    out_ref[...] = dot(pick_ref[...], hid).astype(BF)
    agg_ref[...] = agg
    pre_ref[...] = pre
    if not first:
        copy.wait()
    wait_weights(*ahead)


def backward_math(ids, d_pre, vals_ref, w_ref, d_ext):
    d_agg = dot(d_pre, w_ref[1], NT).astype(BF)
    spread_rows(ids, vals_ref, d_agg, d_ext)
    return dot(d_pre, w_ref[0], NT)


def weight_partials(ids, h_ref, agg, d_pre, keep_ref, send_ref):
    on_rows = dot(h_ref[...], d_pre, TN).astype(BF)
    on_agg = dot(agg, d_pre, TN).astype(BF)

    @pl.when(ids[1] == 0)
    def _():
        keep_ref[...] = on_rows
        send_ref[...] = on_agg

    @pl.when(ids[1] != 0)
    def _():
        keep_ref[...] = on_agg
        send_ref[...] = on_rows


def top_kernel(layer, ids, h_ref, arr_ref, vals_ref, vals_t, wout_ref, lab_ref, mask_ref, w_ref, *rest):
    remote_ref, part_ref, keep_ref, send_ref, buf_ref, hid_ref, ext, d_ext, buf_sem = rest[1:]
    copy = to_slot(h_ref, layer - 1, ids, buf_ref, buf_sem)
    copy.start()
    rows = h_ref.shape[0]
    agg, pre, sig, hid = forward_math(ids, h_ref, arr_ref, vals_ref, w_ref, ext)
    hid_ref[...] = hid
    last = to_slot(hid_ref, layer, ids, buf_ref, buf_sem)
    copy.wait()
    last.start()
    logits = dot(wout_ref[...], hid, NT)
    expo = jnp.exp(logits)
    probs = expo / jnp.sum(expo, axis=0, keepdims=True)
    label = lab_ref[pl.ds(ids[0], 1), :]
    onehot = (label == lax.broadcasted_iota(jnp.int32, logits.shape, 0)).astype(F32)
    live = mask_ref[pl.ds(ids[0], 1), :].astype(F32)
    g_logits = (live * (probs - onehot)).astype(BF)
    d_out = dot(g_logits, wout_ref[...], TN).astype(BF)
    d_pre = (d_out.astype(F32) * (sig * (1.0 + pre * (1.0 - sig)))).astype(BF)
    back = backward_math(ids, d_pre, vals_t, w_ref, d_ext)
    remote_ref[...] = d_ext[rows : 2 * rows, :].astype(BF).reshape(remote_ref.shape)
    part_ref[...] = back + d_ext[0:rows, :]
    weight_partials(ids, h_ref, agg, d_pre, keep_ref, send_ref)
    last.wait()


def chunk_sum(block):
    total = block[0:2].astype(F32)
    for n in range(2, block.shape[0], 2):
        total = total + block[n : n + 2].astype(F32)
    return total


def slope_math(ids, layer, ret_ref, part_in, pre_ref, pick_ref, dout_ref, buf_ref, buf_sem):
    rows, feat = part_in.shape
    returned = ret_ref[:, 0 : rows // ret_ref.shape[0], :].reshape(rows, feat)
    d_out = (part_in[...] + dot(pick_ref[...], returned)).astype(BF)
    dout_ref[...] = d_out
    copy = to_slot(dout_ref, layer + 1, ids, buf_ref, buf_sem)
    copy.start()
    pre = pre_ref[...]
    sig = sigmoid(pre)
    return (d_out.astype(F32) * (sig * (1.0 + pre * (1.0 - sig)))).astype(BF), copy


def backward_kernel(layer, carry, ids, ret_ref, part_in, pre_ref, h_ref, agg_ref, *rest):
    (vals_ref, pick_ref, w_ref), rest = rest[:3], rest[3:]
    if carry:
        keep_in, recv_in, rest = rest[0], rest[1], rest[3:]
    out_ref, part_ref, buf_ref, keep_ref, send_ref, dout_ref, d_ext, buf_sem = rest
    rows, feat = part_in.shape
    d_pre, copy = slope_math(
        ids, layer, ret_ref, part_in, pre_ref, pick_ref, dout_ref, buf_ref, buf_sem
    )
    back = backward_math(ids, d_pre, vals_ref, w_ref, d_ext)
    peers, slots = out_ref.shape[0], rows // out_ref.shape[0]
    out_ref[:, 0:slots, :] = d_ext[rows : 2 * rows, :].astype(BF).reshape(peers, slots, feat)
    if carry:
        put_carry(keep_in, recv_in, out_ref, slots)
    part_ref[...] = back + d_ext[0:rows, :]
    weight_partials(ids, h_ref, agg_ref[...], d_pre, keep_ref, send_ref)
    copy.wait()


def last_slope_kernel(
    ids, ret_ref, part_in, pre_ref, h_ref, agg_ref, pick_ref, buf_in,
    dpre_ref, buf_ref, keep_ref, send_ref, chunk_ref, dout_ref, buf_sem,
):
    d_pre, copy = slope_math(
        ids, 0, ret_ref, part_in, pre_ref, pick_ref, dout_ref, buf_ref, buf_sem
    )
    dpre_ref[...] = d_pre
    weight_partials(ids, h_ref, agg_ref[...], d_pre, keep_ref, send_ref)
    slots = part_in.shape[0] // ret_ref.shape[0]
    chunk_ref[...] = chunk_sum(ret_ref[:, slots:, :]).astype(BF)
    copy.wait()


def last_spread_kernel(
    ids, dpre_ref, vals_ref, w_ref, keep_a, recv_a, keep_b, recv_b, c_in,
    out_ref, part_ref, local_ref, c_ref, d_ext, carried, sems,
):
    rows, feat = dpre_ref.shape
    peers, slots = local_ref.shape[0], local_ref.shape[1]
    size = keep_a.shape[0] // peers
    copies = [
        pltpu.make_async_copy(c_in, c_ref, sems.at[0]),
        pltpu.make_async_copy(
            carried, out_ref.at[:, pl.ds(slots, 2 * size), :], sems.at[1]
        ),
    ]
    copies[0].start()
    put_carry(keep_a, recv_a, carried, 0)
    put_carry(keep_b, recv_b, carried, size)
    copies[1].start()
    back = backward_math(ids, dpre_ref[...], vals_ref, w_ref, d_ext)
    local_ref[...] = d_ext[rows : 2 * rows, :].astype(BF).reshape(local_ref.shape)
    part_ref[...] = back + d_ext[0:rows, :]
    for copy in copies:
        copy.wait()


def put_carry(keep_ref, recv_ref, out_ref, first):
    peers, feat = out_ref.shape[0], out_ref.shape[2]
    size = keep_ref.shape[0] // peers
    total = (keep_ref[...].astype(F32) + recv_ref[...].astype(F32)).astype(BF)
    out_ref[:, first : first + size, :] = total.reshape(peers, size, feat)


def join_kernel(ids, keep_ref, recv_ref, local_ref, part_ref, buf_in, out_ref, part_out, both, sems):
    size, slots = both.shape[1], local_ref.shape[1]
    first = out_ref.shape[1] - size
    copies = [
        pltpu.make_async_copy(part_ref, part_out, sems.at[0]),
        pltpu.make_async_copy(local_ref, out_ref.at[:, pl.ds(0, slots), :], sems.at[1]),
        pltpu.make_async_copy(both, out_ref.at[:, pl.ds(first, size), :], sems.at[2]),
    ]
    copies[0].start()
    copies[1].start()
    put_carry(keep_ref, recv_ref, both, 0)
    copies[2].start()
    for copy in copies:
        copy.wait()


def chunk_kernel(ids, ret_ref, c_in, o_0, o_1, o_2, o_3, sums, sem):
    copy = pltpu.make_async_copy(c_in, sums.at[3], sem)
    copy.start()
    size = sums.shape[2]
    slots = ret_ref.shape[1] - 3 * size
    for n, layer in enumerate((2, 1, 0)):
        first = slots + n * size
        sums[layer] = chunk_sum(ret_ref[:, first : first + size, :]).astype(BF)
    copy.wait()
    for s, out_ref in enumerate((o_0, o_1, o_2, o_3)):
        out_ref[...] = sums[lax.rem(ids[0] + s, 4)]


def end_kernel(ids, ret_ref, part_in, pick_ref, buf_in, buf_ref, o_1, o_2, o_3, dout_ref, sems):
    rows, feat = part_in.shape
    outs = (o_1, o_2, o_3)
    copies = [
        pltpu.make_async_copy(buf_in.at[s + 1], out_ref, sems.at[s])
        for s, out_ref in enumerate(outs)
    ]
    for copy in copies:
        copy.start()
    returned = ret_ref[:, 0 : rows // ret_ref.shape[0], :].reshape(rows, feat)
    dout_ref[...] = (part_in[...] + dot(pick_ref[...], returned)).astype(BF)
    home = pltpu.make_async_copy(dout_ref, buf_ref.at[0], sems.at[3])

    @pl.when(ids[0] == 0)
    def _():
        home.start()

    for copy in copies:
        copy.wait()
    for s, out_ref in enumerate(outs):

        @pl.when(lax.rem(ids[0] + s + 1, 4) == 0)
        def _():
            out_ref[...] = dout_ref[...]

    @pl.when(ids[0] == 0)
    def _():
        home.wait()


def layer_sum_kernel(ids, own_ref, a_ref, b_ref, c_ref, out_ref):
    total = own_ref[...].astype(F32) + a_ref[...].astype(F32)
    total = (total + b_ref[...].astype(F32) + c_ref[...].astype(F32)).astype(BF)
    for n in range(0, out_ref.shape[0], 2):
        out_ref[n : n + 2] = total


def scale_kernel(scale, ids, mine_ref, other_ref, self_ref, neigh_ref, mine, other, sems):
    core = ids[1]
    size = mine_ref.shape[0] // 4
    for step in range(4):
        rows = pl.ds(step * size, size)
        mine[rows, :] = mine_ref[rows, :].astype(F32) * scale
        other[rows, :] = other_ref[rows, :].astype(F32) * scale
        for value, place, sem in ((mine, core, 0), (other, 1 - core, 1)):
            for target, out_ref in enumerate((self_ref, neigh_ref)):

                @pl.when(place == target)
                def _():
                    pltpu.make_async_copy(
                        value.at[rows], out_ref.at[0, rows], sems.at[sem, step]
                    ).start()

    for step in range(4):
        rows = pl.ds(step * size, size)
        for value, sem in ((mine, 0), (other, 1)):
            pltpu.make_async_copy(value.at[rows], self_ref.at[0, rows], sems.at[sem, step]).wait()


def home_kernel(ids, own_ref, a_ref, b_ref, c_ref, out_ref, own, sems):
    load = pltpu.make_async_copy(own_ref.at[0], own, sems.at[4])
    load.start()
    copies = [
        pltpu.make_async_copy(piece, out_ref.at[0, lax.rem(ids[0] + 4 - s, 4)], sems.at[s])
        for s, piece in enumerate((own, a_ref, b_ref, c_ref))
    ]
    for copy in copies[1:]:
        copy.start()
    load.wait()
    copies[0].start()
    for copy in copies:
        copy.wait()


def body(
    features,
    w_self,
    w_neigh,
    w_out,
    labels,
    train_mask,
    tile_cols,
    tile_vals,
    send_rows,
    send_counts,
):
    home = lax.axis_index("layer")
    node = lax.axis_index("node")
    core = lax.rem(node, 2)
    spans, rows, feat = features.shape
    peers, slots = send_rows.shape[2], send_rows.shape[3]
    tiles, degree, size = tile_vals.shape[2], tile_vals.shape[3], tile_vals.shape[4]
    scale = 1.0 / (spans * rows * peers)
    own_cols = lax.dynamic_index_in_dim(tile_cols.reshape(spans, tiles * degree), home, 0, False)
    scalars = jnp.concatenate([jnp.stack([home, core]).astype(jnp.int32), own_cols])
    act, wide, square = near((rows, feat)), near((rows, feat), F32), near((feat, feat))
    ext_scratch = pltpu.VMEM((2 * rows, feat), BF)
    d_ext_scratch = pltpu.VMEM((2 * rows, feat), F32)
    all_shifts = range(1, spans)

    mine = jnp.where(core == 0, w_self[0], w_neigh[0])
    left, right, far = (shift(mine, "layer", s) for s in (1, -1, 2))
    pick, outgoing, features_0, vals, vals_t, pick_t, pick_far = run(
        pre_kernel,
        "gather_rows",
        scalars,
        [
            (features, of_span((rows, feat))),
            (send_rows.reshape(spans, peers, slots).swapaxes(1, 2), of_span((slots, peers))),
            (send_counts.reshape(spans, 1, peers), of_span((1, peers))),
            (
                tile_vals.reshape(spans, tiles, degree, size, size),
                of_span((tiles, degree, size, size)),
            ),
        ],
        [
            near((peers * slots, rows)),
            act,
            act,
            near((tiles, degree, size, size)),
            near((tiles, degree * size, size)),
            near((rows, peers * slots)),
            far_block((rows, peers * slots)),
        ],
        flops=10**8,
        moved=10**6,
    )
    arrived = exchange(outgoing.reshape(peers, slots, feat))
    arrived, left, right, far = tie(arrived, left, right, far)
    sources = [w_self[0], w_neigh[0], left, sibling(left), right, sibling(right)]
    sources += [far, sibling(far)]
    weight = near((2, feat, feat))

    hidden, aggs, pres, weights = [features_0], [], [], []
    top = spans - 1
    stack = (pltpu.HBM((spans, rows, feat), BF), FAR)
    buf_sem = pltpu.SemaphoreType.DMA
    acts_buf = None
    for layer in range(top):
        ins = [hidden[layer], arrived.reshape(rows, feat), vals, pick, *sources]
        if layer:
            ins.append(weights[layer])
        if layer > 1:
            ins.append((acts_buf, FAR))
        agg, pre, hid, outgoing, arranged, last = run(
            functools.partial(forward_kernel, layer),
            f"layer_forward_{layer}",
            scalars,
            ins,
            [act, wide, act, act, weight, stack if layer else weight],
            [ext_scratch, buf_sem, pltpu.SemaphoreType.DMA((2, 2))],
            {len(ins) - 1: 5} if layer > 1 else None,
            flops=6 * 10**8,
            moved=4 * 10**6,
        )
        if layer:
            acts_buf = last
        else:
            weights.append(last)
        weights.append(arranged)
        hidden.append(hid)
        aggs.append(agg)
        pres.append(pre)
        arrived = exchange(outgoing.reshape(peers, slots, feat))

    ins = [
        hidden[top],
        arrived.reshape(rows, feat),
        vals,
        vals_t,
        w_out.T,
        labels,
        train_mask,
        weights[top],
        (acts_buf, FAR),
    ]
    remote, part, keep, send, acts_buf = run(
        functools.partial(top_kernel, top),
        "top_layer",
        scalars,
        ins,
        [near((peers, slots, feat)), wide, square, square, stack],
        [
            pltpu.VMEM((rows, feat), BF),
            ext_scratch,
            d_ext_scratch,
            buf_sem,
        ],
        {len(ins) - 1: 4},
        flops=10**9,
        moved=5 * 10**6,
    )

    def travel(buf):
        return [shift(buf[s], "layer", s) for s in all_shifts]

    first_block = pl.BlockSpec((None, rows, feat), lambda i, ids: (0, 0, 0))

    def put_home(buf, *pieces):
        shape = (1, spans, rows, feat)
        return run(
            home_kernel,
            "put_home",
            scalars,
            [(buf, FAR), *pieces],
            [(pltpu.HBM(shape, BF), FAR)],
            [pltpu.VMEM((rows, feat), BF), pltpu.SemaphoreType.DMA((5,))],
            moved=2 * 10**6,
        )[0]

    chunk_rows = feat // peers
    pairs, grads_buf = [], None
    for layer in range(top - 1, 0, -1):
        returned, send = tie(exchange(remote), send)
        pairs.append((keep, sibling(send)))
        carry = layer < top - 1
        width = slots + chunk_rows * carry
        ins = [
            returned,
            part,
            pres[layer],
            hidden[layer],
            aggs[layer],
            vals_t,
            pick_t,
            weights[layer],
        ]
        aliases = None
        if carry:
            ins += [*pairs[-2], (grads_buf, FAR)]
            aliases = {len(ins) - 1: 2}
        remote, part, grads_buf, keep, send = run(
            functools.partial(backward_kernel, layer, carry),
            f"layer_backward_{layer}",
            scalars,
            ins,
            [near((peers, width, feat)), wide, stack, square, square],
            [pltpu.VMEM((rows, feat), BF), d_ext_scratch, buf_sem],
            aliases,
            flops=10**9,
            moved=5 * 10**6,
        )
        remote, recv = tie(remote, pairs[-1][1])
        pairs[-1] = (pairs[-1][0], recv)

    returned, send = tie(exchange(remote), send)
    recv_1, keep_1 = sibling(send), keep
    chunk_shape = (2, chunk_rows, feat)
    d_pre, grads_buf, keep, send, c_3 = run(
        last_slope_kernel,
        "last_slope",
        scalars,
        [returned, part, pres[0], hidden[0], aggs[0], pick_t, (grads_buf, FAR)],
        [act, stack, square, square, near(chunk_shape)],
        [pltpu.VMEM((rows, feat), BF), buf_sem],
        {6: 1},
        flops=4 * 10**8,
        moved=3 * 10**6,
    )
    d_pre, recv_1, send = tie(d_pre, recv_1, send)
    recv = sibling(send)
    width = slots + 3 * chunk_rows
    operand = (pltpu.HBM((peers, width, feat), BF), FAR)
    sums_out = (pltpu.HBM(chunk_shape, BF), FAR)
    remote, part, local, sums = run(
        last_spread_kernel,
        "last_spread",
        scalars,
        [d_pre, vals_t, weights[0], *pairs[-1], keep_1, recv_1, c_3],
        [operand, wide, near((peers, slots, feat)), sums_out],
        [
            d_ext_scratch,
            pltpu.VMEM((peers, 2 * chunk_rows, feat), BF),
            pltpu.SemaphoreType.DMA((2,)),
        ],
        flops=5 * 10**8,
        moved=4 * 10**6,
    )
    remote, recv = tie(remote, recv)
    joined, part = run(
        join_kernel,
        "join_rows",
        scalars,
        [keep, recv, local, part, (remote, FAR)],
        [operand, (pltpu.HBM((rows, feat), F32), FAR)],
        [pltpu.VMEM((peers, chunk_rows, feat), BF), pltpu.SemaphoreType.DMA((3,))],
        aliases={4: 0},
        moved=2 * 10**6,
    )
    joined, acts_buf = tie(joined, acts_buf)
    acts = travel(acts_buf)
    layer_acts = put_home(acts_buf, *acts)
    returned, layer_acts = tie(exchange(joined), layer_acts)
    own_sum, *sums = run(
        chunk_kernel,
        "sum_chunks",
        scalars,
        [returned, (sums, FAR)],
        [near(chunk_shape)] * spans,
        [pltpu.VMEM((spans, *chunk_shape), BF), buf_sem],
        moved=10**6,
    )
    sums = [shift(v, "layer", s) for s, v in zip(all_shifts, sums)]
    grads_buf, *to_send = run(
        end_kernel,
        "input_grads",
        scalars,
        [
            returned,
            (part, whole((rows, feat))),
            (pick_far, whole(pick_far.shape)),
            (grads_buf, FAR),
        ],
        [stack, act, act, act],
        [pltpu.VMEM((rows, feat), BF), pltpu.SemaphoreType.DMA((4,))],
        {3: 0},
        flops=10**8,
        moved=10**6,
    )
    pieces = tie(*sums, *to_send)
    sums, to_send = pieces[:3], pieces[3:]
    spread = run(
        layer_sum_kernel,
        "sum_over_layer",
        scalars,
        [own_sum, *sums],
        [far_block((peers, chunk_rows, feat))],
        moved=10**6,
    )[0]
    grads = [shift(v, "layer", s) for s, v in zip(all_shifts, to_send)]
    gathered, *grads = tie(exchange(spread), *grads)
    gathered = gathered.reshape(feat, feat)
    other = sibling(gathered)
    act_grads = put_home(grads_buf, *grads)
    out_square = (1, feat, feat)
    grad_self, grad_neigh = run(
        functools.partial(scale_kernel, scale),
        "scale_grads",
        scalars,
        [gathered, other],
        [(pltpu.HBM(out_square, F32), FAR)] * 2,
        [pltpu.VMEM((feat, feat), F32)] * 2 + [pltpu.SemaphoreType.DMA((2, 4))],
        moved=3 * 10**6,
    )
    return (layer_acts, act_grads, grad_self, grad_neigh)


def solution(mesh):
    in_specs = (
        P(None, "node", None),
        P("layer", None, None),
        P("layer", None, None),
        P(),
        P(None, "node"),
        P(None, "node"),
        P(None, "node", None, None),
        P(None, "node", None, None, None, None),
        P(None, "node", None, None),
        P(None, "node", None),
    )
    out_specs = (
        P("layer", None, "node", None),
        P("layer", None, "node", None),
        P("layer", None, None),
        P("layer", None, None),
    )
    return jax.shard_map(body, mesh=mesh, in_specs=in_specs, out_specs=out_specs, check_vma=False)
```
